128 devices in a mesh: member: 4 (over y_lo, core), region: 32 (over z, y_hi, x).
Axes of the slice: x: 4, y: 4 (y_hi: 2, y_lo: 2; y = y_hi * 2 + y_lo), z: 4, core: 2. Of those that a mesh axis runs over, the one named last changes fastest.
Arguments:
- latent: bfloat16 [8, 4096, 1024], P('member', 'region'), may hold values from -6 to 6
- w_node: bfloat16 [1024, 1024], replicated, may hold values from -0.1875 to 0.1875
- bias: float32 [1024], replicated, may hold values from -3 to 3
- w_out: bfloat16 [100, 1024], replicated, may hold values from -0.1875 to 0.1875
- edge_src: int32 [65536, 3], P('region'), may hold values from 0 to 383
- edge_weight: float32 [65536, 3], P('region'), may hold values from 0.2 to 0.6
- target: float32 [100, 65536], P(None, 'region'), may hold values from -6 to 6
- area: float32 [65536], P('region'), may hold values from 0.3 to 30
Outputs:
- grad_node: float32 [1024, 1024], P('region')
- grad_out: float32 [100, 1024], replicated
- grad_bias: float32 [1024], replicated
- loss: float32 [32], P('region')
The draws below stay inside these ranges and needn't reach their ends.
Inputs may be any that keep to these rules, and one draw needn't show every extreme that they name: `edge_src`: an index into the latent nodes of the previous region, then the grid point's own region, then the next region, 128 each; regions form a loop.
All inputs are finite; a program needn't handle non-finite values.
Results may differ from the reference program's by a relative error of at most 0.007.
Values may be sent and summed in bfloat16 or wider, within the bound.
No kernel may reach another device: no remote copies, remote signals or barrier semaphores. Data moves between devices by JAX's collectives and lax.ppermute only.
A program may use at most 128 MiB of HBM per device.

```python
import jax
import jax.numpy as jnp
from jax import lax

H = 1024
V = 100
K = 3
LAT_DEV = 128
GRID_DEV = 2048
MEMBERS = 8
NLAT = 4096
NGRID = 65536
N_REGION = 32


def draw_area(key, part):
    position = jnp.arange(NGRID).astype(jnp.float32) / NGRID
    spread = jax.random.uniform(key, (NGRID,), jnp.float32, -1.15, 1.15)
    rise = 1.0 + 2.0 * position
    return rise * jnp.exp(spread)


def place_ends(array, stream_key, least, high):
    place = [jax.random.randint(jax.random.fold_in(stream_key, axis), (), 0, length) for axis, length in enumerate(array.shape)]
    longest = array.shape.index(max(array.shape))
    beside = place[:longest] + [(place[longest] + 1) % array.shape[longest]] + place[longest + 1:]
    return array.at[tuple(place)].set(least).at[tuple(beside)].set(high)


def steps_of(stream_key, shape, shards, smallest, high):
    def one(dim, parts):
        steps = jax.random.uniform(jax.random.fold_in(jax.random.fold_in(stream_key, 6), dim), (parts,), jnp.float32, smallest / len(shards), high / len(shards))
        return jnp.repeat(jnp.exp(steps), shape[dim] // parts).reshape((-1,) + (1,) * (len(shape) - dim - 1))

    gain = one(*shards[0])
    for cut in shards[1:]:
        gain = gain * one(*cut)
    return gain


def gaussian(key, shape, scale, reach, split=(), held_as=jnp.bfloat16):
    drawn = jax.random.normal(key, shape, jnp.float32) * scale
    if len(split) > 0:
        drawn = steps_of(key, shape, split, -0.22, 0.18) * drawn
    return jnp.clip(drawn, min=-reach, max=reach).astype(held_as)


def setup_inputs(seed: int = 0) -> dict:
    splits = jax.random.split(jax.random.key(seed), 9)
    latent = gaussian(splits[0], (MEMBERS, NLAT, H), 1.0, 6.0, ((0, 4), (1, 32)))
    w_node = gaussian(splits[1], (H, H), H ** -0.5, 0.1875)
    bias = gaussian(splits[2], (H,), 0.5, 3.0, (), jnp.float32)
    w_out = gaussian(splits[3], (V, H), H ** -0.5, 0.1875)
    edge_src = place_ends(jax.random.randint(splits[4], (NGRID, K), 0, 3 * LAT_DEV), jax.random.fold_in(splits[4], 1), 0, (3 * LAT_DEV) - 1).astype(jnp.int32)
    edge_weight = jnp.clip(0.2 + 0.400000021 * jax.random.uniform(splits[5], (NGRID, K), jnp.float32) ** steps_of(splits[5], (NGRID, K), ((0, 32),), -0.2, 0.2), 0.2, 0.6)
    target = gaussian(splits[6], (V, NGRID), 1.0, 6.0, ((1, 32),), jnp.float32)
    area = draw_area(jax.random.fold_in(splits[8], 71), 0)
    return {"latent": latent, "w_node": w_node, "bias": bias, "w_out": w_out, "edge_src": edge_src, "edge_weight": edge_weight, "target": target, "area": area}


smooth_sq = 0.01
smooth_width = 0.1

def gelu_slope(values):
    inner = 0.7978845608028654 * (values + 0.044715 * values * values * values)
    tanh_part = jnp.tanh(inner)
    return 0.5 * (1.0 + tanh_part) + 0.5 * values * (1.0 - tanh_part * tanh_part) * 0.7978845608028654 * (1.0 + 3.0 * 0.044715 * values * values)

def reference(latent, w_node, bias, w_out, edge_src, edge_weight, target, area):
    grid_region = (jnp.arange(NGRID, dtype=jnp.int32) // GRID_DEV)[:, None]
    node_index = ((grid_region - 1 + edge_src // LAT_DEV) % N_REGION * LAT_DEV + edge_src % LAT_DEV).astype(jnp.int32)
    segment_ids = (grid_region * (3 * LAT_DEV) + edge_src).astype(jnp.int32)
    count = MEMBERS

    def forward(member_latent):
        proj = jnp.dot(member_latent, w_node, preferred_element_type=jnp.float32).astype(jnp.bfloat16)
        pre = jnp.zeros((NGRID, H), jnp.float32) + bias[None, :]
        for slot in range(K):
            pre = pre + edge_weight[:, slot][:, None] * proj[node_index[:, slot]].astype(jnp.float32)
        return pre

    def predict(member_latent):
        hidden = jax.nn.gelu(forward(member_latent), approximate=True).astype(jnp.bfloat16)
        return lax.dot_general(w_out, hidden, (((1,), (1,)), ((), ())), preferred_element_type=jnp.float32)
    preds = lax.map(predict, latent)
    errors = preds - target[None]
    own = jnp.sqrt(errors * errors + smooth_sq)
    dist_sum = jnp.zeros_like(errors)
    slope_sum = jnp.zeros_like(errors)
    for other in range(count):
        diff = errors - errors[other][None]
        dist = jnp.sqrt(diff * diff + smooth_sq)
        dist_sum = dist_sum + dist
        slope_sum = slope_sum + diff / dist
    crps = lax.optimization_barrier(jnp.mean(own, 0)) - (lax.optimization_barrier(jnp.sum(dist_sum, 0)) - count * smooth_width) / (2.0 * count * (count - 1))
    weighted = (area[None, :] * crps).reshape(V, N_REGION, GRID_DEV)
    loss = lax.optimization_barrier(jnp.sum(weighted, axis=(0, 2))) / V / GRID_DEV
    bracket = errors / own / count - slope_sum / (count * (count - 1))
    dpred = (bracket * (area / V)[None, None, :]).astype(jnp.bfloat16)

    def step(carry, pair):
        grad_node, grad_out, grad_bias = carry
        member_latent, member_dpred = pair
        pre = forward(member_latent)
        hidden = jax.nn.gelu(pre, approximate=True).astype(jnp.bfloat16)
        grad_out = grad_out + jnp.dot(member_dpred, hidden, preferred_element_type=jnp.float32)
        dhidden = lax.dot_general(member_dpred, w_out, (((0,), (0,)), ((), ())), preferred_element_type=jnp.float32)
        dpre = (dhidden * gelu_slope(pre)).astype(jnp.bfloat16)
        grad_bias = grad_bias + lax.optimization_barrier(jnp.sum(dpre.astype(jnp.float32), 0))
        contrib = jnp.zeros((N_REGION * 3 * LAT_DEV, H), jnp.float32)
        for slot in range(K):
            contrib = contrib + jax.ops.segment_sum(dpre.astype(jnp.float32) * edge_weight[:, slot][:, None], segment_ids[:, slot], num_segments=N_REGION * 3 * LAT_DEV)
        rounded = contrib.astype(jnp.bfloat16)
        blocks = member_latent.reshape(N_REGION, LAT_DEV, H)
        extended = jnp.stack([jnp.roll(blocks, 1, axis=0), blocks, jnp.roll(blocks, -1, axis=0)], axis=1).reshape(N_REGION * 3 * LAT_DEV, H)
        grad_node = grad_node + lax.dot_general(extended, rounded, (((0,), (0,)), ((), ())), preferred_element_type=jnp.float32)
        return ((grad_node, grad_out, grad_bias), None)
    init = (jnp.zeros((H, H), jnp.float32), jnp.zeros((V, H), jnp.float32), jnp.zeros((H,), jnp.float32))
    (grad_node, grad_out, grad_bias), unused = lax.scan(step, init, (latent, dpred))
    return (grad_node, grad_out, grad_bias, loss)
```

```python
import jax
import jax.numpy as jnp
from jax import lax
from jax.experimental import pallas as pl
from jax.experimental.pallas import tpu as pltpu
from jax.sharding import Mesh
from jax.sharding import PartitionSpec as P

REGION = ("z", "yhi", "x")
MEMBER = ("ylo", "core")
CHIPS = ("ylo", "z", "yhi", "x")
EVERY = ("ylo", "core", "z", "yhi", "x")

SMOOTH_SQ = 0.01
C0 = 0.7978845608028654
C1 = 0.044715
WIDE = 256
PAD = 128
bf16 = jnp.bfloat16
f32 = jnp.float32
f16 = jnp.float16


def dot(a, b, ca=1, cb=0):
    return lax.dot_general(a, b, (((ca,), (cb,)), ((), ())), preferred_element_type=f32)


def params(semantics, mib=48):
    return pltpu.CompilerParams(dimension_semantics=semantics, vmem_limit_bytes=mib << 20)


def prep_kernel(src, weight, at_hi, at_lo, a_hi, a_lo):
    nodes, wide = at_hi.shape
    place = lax.broadcasted_iota(jnp.int32, (nodes, wide), 0)
    total = jnp.zeros((nodes, wide), f32)
    for k in range(src.shape[0]):
        total = total + jnp.where(src[k : k + 1, :] == place, weight[k : k + 1, :], 0.0)
    high = total.astype(bf16)
    low = total - high.astype(f32)
    at_hi[...] = high
    at_lo[...] = low.astype(bf16)
    a_hi[...] = total.T.astype(bf16)
    a_lo[...] = low.T.astype(bf16)


def prep(src, weight, nodes):
    fan, points = src.shape
    row = pl.BlockSpec((fan, WIDE), lambda i: (0, i))
    wide = pl.BlockSpec((nodes, WIDE), lambda i: (0, i))
    tall = pl.BlockSpec((WIDE, nodes), lambda i: (i, 0))
    return pl.pallas_call(
        prep_kernel,
        grid=(points // WIDE,),
        in_specs=[row, row],
        out_specs=[wide, wide, tall, tall],
        out_shape=[jax.ShapeDtypeStruct((nodes, points), bf16)] * 2
        + [jax.ShapeDtypeStruct((points, nodes), bf16)] * 2,
        compiler_params=params(("arbitrary",)),
        name="prep",
    )(src, weight)


def forward_kernel(low, own, high, w_node, at_hi, at_lo, bias, w_out, target, hid, slope, err):
    step = pl.program_id(0)
    parts = [dot(block[...], w_node[...]).T.astype(bf16) for block in (low, own, high)]
    proj = jnp.concatenate(parts, axis=1)
    shift = bias[...]
    for g in range(at_hi.shape[1] // WIDE):
        at = slice(g * WIDE, (g + 1) * WIDE)
        x = dot(proj, at_hi[:, at]) + dot(proj, at_lo[:, at]) + shift
        sq = x * x
        u = 0.5 + 0.5 * jnp.tanh(x * (C0 + (C0 * C1) * sq))
        h = x * u
        hb = h.astype(bf16)
        hid[:, at] = hb
        slope[:, at] = (u + h * (1.0 - u) * (2.0 * C0 + (6.0 * C0 * C1) * sq)).astype(bf16)
        part = dot(w_out[...], hb)

        @pl.when(step == 0)
        def _():
            err[:, at] = part - target[:, at]

        @pl.when(step > 0)
        def _():
            err[:, at] += part


def forward(low, own, high, w_node, at_hi, at_lo, bias, w_out, target):
    width = w_node.shape[1]
    nodes, points = at_hi.shape
    variables = target.shape[0]

    def whole(a):
        return pl.BlockSpec(a.shape, lambda i: (0,) * a.ndim)

    rows = pl.BlockSpec((WIDE, points), lambda i: (i, 0))
    field = pl.BlockSpec((variables, points), lambda i: (0, 0))
    return pl.pallas_call(
        forward_kernel,
        grid=(width // WIDE,),
        in_specs=[
            whole(low),
            whole(own),
            whole(high),
            pl.BlockSpec((w_node.shape[0], WIDE), lambda i: (0, i)),
            whole(at_hi),
            whole(at_lo),
            pl.BlockSpec((WIDE, 1), lambda i: (i, 0)),
            pl.BlockSpec((variables, WIDE), lambda i: (0, i)),
            whole(target),
        ],
        out_specs=[rows, rows, field],
        out_shape=[
            jax.ShapeDtypeStruct((width, points), bf16),
            jax.ShapeDtypeStruct((width, points), bf16),
            jax.ShapeDtypeStruct((variables, points), f32),
        ],
        compiler_params=params(("arbitrary",)),
        name="forward",
    )(low, own, high, w_node, at_hi, at_lo, bias, w_out, target)


def crps_kernel(count, scale, own_0, own_1, *rest):
    others, (area, d_0, d_1, loss) = rest[:-4], rest[-4:]
    variables, wide = own_0.shape

    @pl.when(pl.program_id(0) == 0)
    def _():
        loss[...] = jnp.zeros_like(loss)

    def apart(d):
        q = d * d + SMOOTH_SQ
        r = lax.rsqrt(q)
        return q * r, d * r

    for c in range(wide // PAD):
        at = slice(c * PAD, (c + 1) * PAD)
        a, b = own_0[:, at], own_1[:, at]
        own_a, slope_a = apart(a)
        own_b, slope_b = apart(b)
        dist, t = apart(a - b)
        dist = 2.0 * dist
        sum_a, sum_b = t, -t
        for other in others:
            o = other[:, at]
            s, t = apart(a - o)
            dist = dist + s
            sum_a = sum_a + t
            s, t = apart(b - o)
            dist = dist + s
            sum_b = sum_b + t
        where = area[:, at]
        pairs = count * (count - 1)
        crps = (own_a + own_b) * (1.0 / count) - dist * (0.5 / pairs)
        loss[...] += jnp.sum(crps, axis=0, keepdims=True) * where * (1.0 / scale)
        fold = where * (1.0 / variables)
        for ref, s, t in ((d_0, slope_a, sum_a), (d_1, slope_b, sum_b)):
            ref[:variables, at] = ((s * (1.0 / count) - t * (1.0 / pairs)) * fold).astype(bf16)
            ref[variables:, at] = jnp.zeros((PAD - variables, PAD), bf16)


def crps(own, others, area, count):
    variables, points = own[0].shape
    wide = 512
    field = pl.BlockSpec((variables, wide), lambda i: (0, i))
    padded = pl.BlockSpec((PAD, wide), lambda i: (0, i))
    return pl.pallas_call(
        lambda *refs: crps_kernel(count, variables * points, *refs),
        grid=(points // wide,),
        in_specs=[field] * (2 + len(others)) + [pl.BlockSpec((1, wide), lambda i: (0, i))],
        out_specs=[padded, padded, pl.BlockSpec((1, PAD), lambda i: (0, 0))],
        out_shape=[jax.ShapeDtypeStruct((PAD, points), bf16)] * 2
        + [jax.ShapeDtypeStruct((1, PAD), f32)],
        compiler_params=params(("arbitrary",)),
        name="crps",
    )(*own, *others, area)


def backward_kernel(variables, d_0, d_1, w_out_t, s_0, s_1, h_0, h_1, a_hi, a_lo, c_0, c_1, heads, dpre):
    column = lax.broadcasted_iota(jnp.int32, heads.shape, 1)
    total = jnp.zeros(heads.shape, f32)
    for d, slope, hid, out in ((d_0, s_0, h_0, c_0), (d_1, s_1, h_1, c_1)):
        summed = jnp.zeros((WIDE, PAD), f32)
        for g in range(d.shape[1] // WIDE):
            at = slice(g * WIDE, (g + 1) * WIDE)
            part = (dot(w_out_t[...], d[:, at]) * slope[:, at].astype(f32)).astype(bf16)
            dpre[:, at] = part
            wide = part.astype(f32)
            summed = summed + wide[:, :PAD] + wide[:, PAD:]
        out[...] = (dot(dpre[...], a_hi[...]) + dot(dpre[...], a_lo[...])).astype(bf16)
        total = total + dot(hid[...], d[...], 1, 1)
        total = total + jnp.where(column == variables, jnp.sum(summed, axis=1, keepdims=True), 0.0)
    heads[...] = total


def backward(variables, dpred, w_out_t, slope, hid, a_hi, a_lo):
    width, points = hid[0].shape
    nodes = a_hi.shape[1]

    def whole(a):
        return pl.BlockSpec(a.shape, lambda i: (0,) * a.ndim)

    rows = pl.BlockSpec((WIDE, points), lambda i: (i, 0))
    contrib = pl.BlockSpec((WIDE, nodes), lambda i: (i, 0))
    narrow = pl.BlockSpec((WIDE, PAD), lambda i: (i, 0))
    return pl.pallas_call(
        lambda *refs: backward_kernel(variables, *refs),
        grid=(width // WIDE,),
        in_specs=[whole(dpred[0]), whole(dpred[1]), narrow, rows, rows, rows, rows, whole(a_hi), whole(a_lo)],
        out_specs=[contrib, contrib, narrow],
        out_shape=[jax.ShapeDtypeStruct((width, nodes), bf16)] * 2
        + [jax.ShapeDtypeStruct((width, PAD), f32)],
        scratch_shapes=[pltpu.VMEM((WIDE, points), bf16)],
        compiler_params=params(("arbitrary",)),
        name="backward",
    )(*dpred, w_out_t, *slope, *hid, a_hi, a_lo)


def outer_kernel(lat_own, lat_other, c_own, c_other, out):
    total = None
    for lat, c in ((lat_own, c_own), (lat_other, c_other)):
        for m in range(lat.shape[0]):
            part = dot(lat[m], c[m], 1, 1)
            total = part if total is None else total + part
    out[...] = total.astype(bf16)


def outer(lat_own, lat_other, c_own, c_other):
    members, inputs, nodes = lat_own.shape
    halves, quarter = c_own.shape[1], c_own.shape[2]
    lat = pl.BlockSpec((members, WIDE, nodes), lambda y, i: (0, i, 0))
    col = pl.BlockSpec((members, None, quarter, nodes), lambda y, i: (0, y, 0, 0))
    return pl.pallas_call(
        outer_kernel,
        grid=(halves, inputs // WIDE),
        in_specs=[lat, lat, col, col],
        out_specs=pl.BlockSpec((None, WIDE, quarter), lambda y, i: (y, i, 0)),
        out_shape=jax.ShapeDtypeStruct((halves, inputs, quarter), bf16),
        compiler_params=params(("arbitrary", "arbitrary")),
        name="outer",
    )(lat_own, lat_other, c_own, c_other)


def local(latent, w_node, bias, w_out, edge_src, edge_weight, target, area):
    members, nodes, width = latent.shape
    points = edge_src.shape[0]
    variables = target.shape[0]
    regions = lax.axis_size(REGION)
    count = members * lax.axis_size(MEMBER)
    ahead = [(i, (i + 1) % regions) for i in range(regions)]
    behind = [(t, s) for s, t in ahead]
    swap = [(0, 1), (1, 0)]

    low = [lax.ppermute(latent[m], REGION, ahead) for m in range(members)]
    high = [lax.ppermute(latent[m], REGION, behind) for m in range(members)]
    at_hi, at_lo, a_hi, a_lo = prep(edge_src.T, edge_weight.T, 3 * nodes)
    w_out_t = jnp.pad(w_out, ((0, PAD - variables), (0, 0))).T
    bias_col = bias[:, None]

    hid, slope, err, near, far, beside = [], [], [], [], [], []
    for m in range(members):
        h, s, e = forward(
            low[m], latent[m], high[m], w_node, at_hi, at_lo, bias_col, w_out, target
        )
        hid.append(h)
        slope.append(s)
        err.append(e)
        sent = (e * 0.125).astype(f16)
        over = lax.ppermute(sent, "ylo", swap)
        near.append(lax.ppermute(sent, "core", swap))
        far.append(over)
        beside.append(lax.ppermute(over, "core", swap))

    lat_t = jnp.stack(
        [jnp.concatenate([low[m], latent[m], high[m]], axis=0).T for m in range(members)]
    )
    lat_t_other = lax.ppermute(lat_t, "core", swap)

    d_0, d_1, loss = crps(err, [o.astype(f32) * 8.0 for o in near + far + beside], area[None, :], count)
    c_0, c_1, heads = backward(variables, (d_0, d_1), w_out_t, slope, hid, a_hi, a_lo)

    where = lax.axis_index(REGION)
    row = lax.broadcasted_iota(jnp.int32, heads.shape, 0)
    column = lax.broadcasted_iota(jnp.int32, heads.shape, 1)
    heads = jnp.where((row == where) & (column == variables + 1), jnp.sum(loss), heads)
    every = lax.axis_size(EVERY)
    pieces = lax.all_to_all(
        heads.reshape(every, width // every, PAD), EVERY, split_axis=0, concat_axis=0, tiled=True
    )
    mine = pieces.sum(axis=0)
    table = lax.all_to_all(
        jnp.broadcast_to(mine, pieces.shape), EVERY, split_axis=0, concat_axis=0, tiled=True
    ).reshape(width, PAD)
    grad_out = table[:, :variables].T
    grad_bias = table[:, variables]
    loss_here = lax.dynamic_slice(table, (where, variables + 1), (1, 1)).reshape(1)

    core = lax.axis_index("core")
    quarters = jnp.stack([c_0, c_1]).reshape(members, 2, 2, width // 4, 3 * nodes)
    kept = lax.dynamic_index_in_dim(quarters, core, 2, keepdims=False)
    given = lax.dynamic_index_in_dim(quarters, 1 - core, 2, keepdims=False)
    taken = lax.ppermute(given, "core", swap)
    part = outer(lat_t, lat_t_other, kept, taken)
    chips = lax.axis_size(CHIPS)
    shares = lax.all_to_all(
        part.reshape(chips, width // regions, width // 4), CHIPS, split_axis=0, concat_axis=0, tiled=True
    )
    own = shares.astype(f32).sum(axis=0)
    grad_node = lax.all_gather(own, MEMBER, axis=1, tiled=True)
    return grad_node, grad_out, grad_bias, loss_here


def solution(mesh):
    finer = Mesh(mesh.devices.reshape(2, 2, 4, 2, 4), EVERY)
    in_specs = (
        P(MEMBER, REGION, None),
        P(),
        P(),
        P(),
        P(REGION, None),
        P(REGION, None),
        P(None, REGION),
        P(REGION),
    )
    out_specs = (P(REGION, None), P(), P(), P(REGION))
    return jax.shard_map(local, mesh=finer, in_specs=in_specs, out_specs=out_specs, check_vma=False)
```

```python
import jax
import jax.numpy as jnp
from jax import lax
from jax.experimental import pallas as pl
from jax.experimental.pallas import tpu as pltpu
from jax.sharding import Mesh
from jax.sharding import PartitionSpec as P

REGION = ("z", "yhi", "x")
MEMBER = ("ylo", "core")
CHIPS = ("ylo", "z", "yhi", "x")
EVERY = ("ylo", "core", "z", "yhi", "x")

SMOOTH_SQ = 0.01
C0 = 0.7978845608028654
C1 = 0.044715
WIDE = 256
PAD = 128
bf16 = jnp.bfloat16
f32 = jnp.float32
f16 = jnp.float16
EDGE = 16


def dot(a, b, ca=1, cb=0):
    return lax.dot_general(a, b, (((ca,), (cb,)), ((), ())), preferred_element_type=f32)


def params(semantics, mib):
    return pltpu.CompilerParams(dimension_semantics=semantics, vmem_limit_bytes=mib << 20)


def whole(a):
    return pl.BlockSpec(a.shape, lambda *i: (0,) * a.ndim)


def prep_kernel(src, weight, at):
    nodes, wide = at.shape[0] - EDGE, at.shape[1]
    place = lax.broadcasted_iota(jnp.int32, (nodes, wide), 0)
    total = jnp.zeros((nodes, wide), f32)
    for k in range(src.shape[0]):
        total = total + jnp.where(src[k : k + 1, :] == place, weight[k : k + 1, :], 0.0)
    at[:nodes, :] = total.astype(bf16)
    first = lax.broadcasted_iota(jnp.int32, (EDGE, wide), 0) == 0
    at[nodes:, :] = jnp.where(first, 1.0, 0.0).astype(bf16)


def prep(src, weight, nodes):
    fan, points = src.shape
    row = pl.BlockSpec((fan, WIDE), lambda i: (0, i))
    return pl.pallas_call(
        prep_kernel,
        grid=(points // WIDE,),
        in_specs=[row, row],
        out_specs=pl.BlockSpec((nodes + EDGE, WIDE), lambda i: (0, i)),
        out_shape=jax.ShapeDtypeStruct((nodes + EDGE, points), bf16),
        compiler_params=params(("arbitrary",), 8),
        name="prep",
    )(src, weight)


def turn_kernel(*refs):
    blocks, out = refs[:-1], refs[-1]
    for b, block in enumerate(blocks):
        nodes = block.shape[0]
        out[:, b * nodes : (b + 1) * nodes] = block[...].T


def turn(blocks):
    nodes, width = blocks[0].shape
    return pl.pallas_call(
        turn_kernel,
        grid=(width // WIDE,),
        in_specs=[pl.BlockSpec((nodes, WIDE), lambda i: (0, i))] * len(blocks),
        out_specs=pl.BlockSpec((WIDE, nodes * len(blocks)), lambda i: (i, 0)),
        out_shape=jax.ShapeDtypeStruct((width, nodes * len(blocks)), bf16),
        compiler_params=params(("arbitrary",), 8),
        name="turn",
    )(*blocks)


def forward_kernel(low, own, high, w_node, at, bias, w_out, target, hid, slope, err, proj):
    nodes = low.shape[0]

    @pl.when(pl.program_id(0) == 0)
    def _():
        for b, block in enumerate((low, own, high)):
            proj[:, b * nodes : (b + 1) * nodes] = dot(block[...], w_node[...]).T.astype(bf16)

    for g in range(target.shape[1] // WIDE):
        cols = slice(g * WIDE, (g + 1) * WIDE)
        total = -target[:, cols]
        for r in range(proj.shape[0] // WIDE):
            rows = slice(r * WIDE, (r + 1) * WIDE)
            x = dot(proj[rows, :], at[: 3 * nodes, cols]) + bias[rows, :]
            sq = x * x
            u = 0.5 + 0.5 * jnp.tanh(x * (C0 + (C0 * C1) * sq))
            h = x * u
            hb = h.astype(bf16)
            hid[rows, cols] = hb
            slope[rows, cols] = (u + h * (1.0 - u) * (2.0 * C0 + (6.0 * C0 * C1) * sq)).astype(bf16)
            total = total + dot(w_out[:, rows], hb)
        err[:, cols] = total


def forward(low, own, high, w_node, at, bias, w_out, target):
    width = w_node.shape[1]
    points = at.shape[1]
    variables = target.shape[0]
    nodes = low.shape[0]
    wide = 512

    def cut(rows):
        return pl.BlockSpec((rows, wide), lambda i: (0, i))

    return pl.pallas_call(
        forward_kernel,
        grid=(points // wide,),
        in_specs=[whole(low), whole(own), whole(high), whole(w_node), cut(at.shape[0]), whole(bias), whole(w_out), cut(variables)],
        out_specs=[cut(width), cut(width), cut(variables)],
        out_shape=[
            jax.ShapeDtypeStruct((width, points), bf16),
            jax.ShapeDtypeStruct((width, points), bf16),
            jax.ShapeDtypeStruct((variables, points), f32),
        ],
        scratch_shapes=[pltpu.VMEM((width, 3 * nodes), bf16)],
        compiler_params=params(("arbitrary",), 28),
        name="forward",
    )(low, own, high, w_node, at, bias, w_out, target)


def apart(d):
    q = d * d + SMOOTH_SQ
    r = lax.rsqrt(q)
    return q * r, d * r


def near_kernel(count, scale, own_0, own_1, *rest):
    others, (area, p_0, p_1, loss) = rest[:-4], rest[-4:]
    pairs = count * (count - 1)

    @pl.when(pl.program_id(0) == 0)
    def _():
        loss[...] = jnp.zeros_like(loss)

    for c in range(own_0.shape[1] // PAD):
        at = slice(c * PAD, (c + 1) * PAD)
        a, b = own_0[:, at], own_1[:, at]
        own_a, slope_a = apart(a)
        own_b, slope_b = apart(b)
        dist, t = apart(a - b)
        dist = 2.0 * dist
        sum_a, sum_b = t, -t
        for other in others:
            o = other[:, at]
            s, t = apart(a - o)
            dist = dist + s
            sum_a = sum_a + t
            s, t = apart(b - o)
            dist = dist + s
            sum_b = sum_b + t
        value = (own_a + own_b) * (1.0 / count) - dist * (0.5 / pairs)
        loss[...] += jnp.sum(value, axis=0, keepdims=True) * area[:, at] * (1.0 / scale)
        p_0[:, at] = slope_a * (1.0 / count) - sum_a * (1.0 / pairs)
        p_1[:, at] = slope_b * (1.0 / count) - sum_b * (1.0 / pairs)


def far_kernel(count, scale, own_0, own_1, *rest):
    others, (p_0, p_1, area, before, d_0, d_1, loss) = rest[:-7], rest[-7:]
    variables = own_0.shape[0]
    pairs = count * (count - 1)

    @pl.when(pl.program_id(0) == 0)
    def _():
        loss[...] = before[...]

    for c in range(own_0.shape[1] // PAD):
        at = slice(c * PAD, (c + 1) * PAD)
        a, b = own_0[:, at], own_1[:, at]
        dist, sum_a, sum_b = 0.0, 0.0, 0.0
        for other in others:
            o = other[:, at]
            s, t = apart(a - o)
            dist = dist + s
            sum_a = sum_a + t
            s, t = apart(b - o)
            dist = dist + s
            sum_b = sum_b + t
        where = area[:, at]
        loss[...] -= jnp.sum(dist, axis=0, keepdims=True) * where * (0.5 / pairs / scale)
        fold = where * (1.0 / variables)
        for ref, p, t in ((d_0, p_0, sum_a), (d_1, p_1, sum_b)):
            ref[:variables, at] = ((p[:, at] - t * (1.0 / pairs)) * fold).astype(bf16)
            ref[variables:, at] = jnp.zeros((PAD - variables, PAD), bf16)


def crps_near(own, others, area, count):
    variables, points = own[0].shape
    wide = 512
    field = pl.BlockSpec((variables, wide), lambda i: (0, i))
    row = pl.BlockSpec((1, wide), lambda i: (0, i))
    return pl.pallas_call(
        lambda *refs: near_kernel(count, variables * points, *refs),
        grid=(points // wide,),
        in_specs=[field] * (2 + len(others)) + [row],
        out_specs=[field, field, pl.BlockSpec((1, PAD), lambda i: (0, 0))],
        out_shape=[jax.ShapeDtypeStruct((variables, points), f32)] * 2 + [jax.ShapeDtypeStruct((1, PAD), f32)],
        compiler_params=params(("arbitrary",), 16),
        name="crps_near",
    )(*own, *others, area)


def crps_far(own, others, partial, area, before, count):
    variables, points = own[0].shape
    wide = 512
    field = pl.BlockSpec((variables, wide), lambda i: (0, i))
    padded = pl.BlockSpec((PAD, wide), lambda i: (0, i))
    row = pl.BlockSpec((1, wide), lambda i: (0, i))
    one = pl.BlockSpec((1, PAD), lambda i: (0, 0))
    return pl.pallas_call(
        lambda *refs: far_kernel(count, variables * points, *refs),
        grid=(points // wide,),
        in_specs=[field] * (4 + len(others)) + [row, one],
        out_specs=[padded, padded, one],
        out_shape=[jax.ShapeDtypeStruct((PAD, points), bf16)] * 2 + [jax.ShapeDtypeStruct((1, PAD), f32)],
        compiler_params=params(("arbitrary",), 16),
        name="crps_far",
    )(*own, *others, *partial, area, before)


def backward_kernel(variables, who, d_0, d_1, w_out_t, s_0, s_1, h_0, h_1, at, loss, contrib, heads, dpre):
    quarter = 2 * pl.program_id(0) + who[0]
    nodes = at.shape[0] - EDGE
    shape = (PAD, WIDE)
    row = lax.broadcasted_iota(jnp.int32, shape, 0)
    spot = lax.broadcasted_iota(jnp.int32, shape, 1) + quarter * WIDE
    total = jnp.where((row == variables + 1) & (spot == who[1]), jnp.sum(loss[...]), 0.0)
    for m, (d, slope, hid) in enumerate(((d_0, s_0, h_0), (d_1, s_1, h_1))):
        for g in range(d.shape[1] // WIDE):
            cut = slice(g * WIDE, (g + 1) * WIDE)
            dpre[m, :, cut] = (dot(w_out_t[...], d[:, cut]) * slope[:, cut].astype(f32)).astype(bf16)
        total = total + dot(d[...], hid[...], 1, 1)
        part = dot(at[...], dpre[m], 1, 1)
        contrib[m * nodes : (m + 1) * nodes, :] = part[:nodes].astype(bf16)
        total = total + jnp.where(row == variables, part[nodes : nodes + 1], 0.0)
    for i in range(PAD // 8):
        for j in range(WIDE // 128):
            heads[i, j] = total[i * 8 : (i + 1) * 8, j * 128 : (j + 1) * 128]


def backward(who, variables, dpred, w_out_t, slope, hid, at, loss):
    width, points = hid[0].shape
    nodes = at.shape[0] - EDGE
    count = width // WIDE // 2

    def fixed(a):
        return pl.BlockSpec(a.shape, lambda y, w: (0,) * a.ndim)

    rows = pl.BlockSpec((WIDE, points), lambda y, w: (2 * y + w[0], 0))
    narrow = pl.BlockSpec((WIDE, PAD), lambda y, w: (2 * y + w[0], 0))
    return pl.pallas_call(
        lambda *refs: backward_kernel(variables, *refs),
        grid_spec=pltpu.PrefetchScalarGridSpec(
            num_scalar_prefetch=1,
            grid=(count,),
            in_specs=[fixed(dpred[0]), fixed(dpred[1]), narrow, rows, rows, rows, rows, fixed(at), fixed(loss)],
            out_specs=[
                pl.BlockSpec((None, 2 * nodes, WIDE), lambda y, w: (y, 0, 0)),
                pl.BlockSpec((None, PAD // 8, WIDE // 128, 8, 128), lambda y, w: (y, 0, 0, 0, 0)),
            ],
            scratch_shapes=[pltpu.VMEM((2, WIDE, points), bf16)],
        ),
        out_shape=[
            jax.ShapeDtypeStruct((count, 2 * nodes, WIDE), bf16),
            jax.ShapeDtypeStruct((count, PAD // 8, WIDE // 128, 8, 128), f32),
        ],
        compiler_params=params(("arbitrary",), 28),
        name="backward",
    )(who, *dpred, w_out_t, *slope, *hid, at, loss)


def outer_kernel(lat_own, lat_other, c_own, c_other, out):
    for y in range(c_own.shape[0]):
        out[y] = (dot(lat_own[...], c_own[y]) + dot(lat_other[...], c_other[y])).astype(bf16)


def outer(lat_own, lat_other, c_own, c_other):
    inputs, nodes = lat_own.shape
    halves, _, quarter = c_own.shape
    lat = pl.BlockSpec((WIDE, nodes), lambda i: (i, 0))
    return pl.pallas_call(
        outer_kernel,
        grid=(inputs // WIDE,),
        in_specs=[lat, lat, whole(c_own), whole(c_own)],
        out_specs=pl.BlockSpec((halves, WIDE, quarter), lambda i: (0, i, 0)),
        out_shape=jax.ShapeDtypeStruct((halves, inputs, quarter), bf16),
        compiler_params=params(("arbitrary",), 16),
        name="outer",
    )(lat_own, lat_other, c_own, c_other)


def finish_kernel(width, order, pieces, out):
    quarters = width // WIDE
    for k in range(quarters):
        for i in range(PAD // 8):
            for j in range(WIDE // 128):
                left = k * WIDE + j * 128
                out[i * 8 : (i + 1) * 8, left : left + 128] = pieces[k, i, j]


def finish(pieces, width):
    return pl.pallas_call(
        lambda *refs: finish_kernel(width, None, *refs),
        out_shape=jax.ShapeDtypeStruct((PAD, width), f32),
        compiler_params=pltpu.CompilerParams(vmem_limit_bytes=8 << 20),
        name="finish",
    )(pieces)


def local(latent, w_node, bias, w_out, edge_src, edge_weight, target, area):
    members, nodes, width = latent.shape
    points = edge_src.shape[0]
    variables = target.shape[0]
    regions = lax.axis_size(REGION)
    count = members * lax.axis_size(MEMBER)
    ahead = [(i, (i + 1) % regions) for i in range(regions)]
    behind = [(t, s) for s, t in ahead]
    swap = [(0, 1), (1, 0)]
    core = lax.axis_index("core")
    where = lax.axis_index(REGION)

    mine = [latent[m] for m in range(members)]
    low, high = [], []
    low.append(lax.ppermute(mine[0], REGION, ahead))
    high.append(lax.ppermute(mine[0], REGION, behind))
    at = prep(edge_src.T, edge_weight.T, 3 * nodes)
    at, second = lax.optimization_barrier((at, mine[1]))
    low.append(lax.ppermute(second, REGION, ahead))
    high.append(lax.ppermute(second, REGION, behind))
    w_out_t = jnp.pad(w_out, ((0, PAD - variables), (0, 0))).T
    bias_col = bias[:, None]

    hid, slope, err, near, far, beside = [], [], [], [], [], []
    for m in range(members):
        h, s, e = forward(low[m], mine[m], high[m], w_node, at, bias_col, w_out, target)
        hid.append(h)
        slope.append(s)
        err.append(e)
        over = lax.ppermute((e * 0.125).astype(f16), "ylo", swap)
        near.append(lax.ppermute(e, "core", swap))
        far.append(over.astype(f32) * 8.0)
        beside.append(lax.ppermute(over, "core", swap).astype(f32) * 8.0)

    first, err[1] = lax.optimization_barrier((mine[0], err[1]))
    lat_t = turn((low[0], first, high[0], low[1], mine[1], high[1]))
    lat_t_other = lax.ppermute(lat_t, "core", swap)

    area_row = area[None, :]
    p_0, p_1, loss = crps_near(err, near + [far[0], beside[0]], area_row, count)
    d_0, d_1, loss = crps_far(err, [far[1], beside[1]], (p_0, p_1), area_row, loss, count)

    def back(side):
        who = jnp.stack([side, where]).astype(jnp.int32)
        return backward(who, variables, (d_0, d_1), w_out_t, slope, hid, at, loss)

    given, heads_given = back(1 - core)
    taken = lax.ppermute(given, "core", swap)
    kept, heads_kept = back(core)

    every = lax.axis_size(EVERY)
    even = core == 0
    heads = jnp.stack(
        [jnp.where(even, heads_kept, heads_given), jnp.where(even, heads_given, heads_kept)], axis=1
    )
    pieces = lax.all_to_all(heads.reshape(every, 8, 128), EVERY, split_axis=0, concat_axis=0, tiled=True)
    part = outer(lat_t, lat_t_other, kept, taken)
    pieces, part = lax.optimization_barrier((pieces, part))
    chips = lax.axis_size(CHIPS)
    shares = lax.all_to_all(
        part.reshape(chips, width // regions, width // 4), CHIPS, split_axis=0, concat_axis=0, tiled=True
    )
    table = lax.all_to_all(
        jnp.broadcast_to(pieces.sum(axis=0), pieces.shape), EVERY, split_axis=0, concat_axis=0, tiled=True
    )
    own = shares.astype(f32).sum(axis=0)
    grad_node = lax.all_gather(own, MEMBER, axis=1, tiled=True)
    full = finish(table.reshape(width // WIDE, PAD // 8, WIDE // 128, 8, 128), width)
    grad_out = full[:variables]
    grad_bias = full[variables]
    loss_here = lax.dynamic_slice(full, (variables + 1, where), (1, 1)).reshape(1)
    return grad_node, grad_out, grad_bias, loss_here


def solution(mesh):
    finer = Mesh(mesh.devices.reshape(2, 2, 4, 2, 4), EVERY)
    in_specs = (
        P(MEMBER, REGION, None),
        P(),
        P(),
        P(),
        P(REGION, None),
        P(REGION, None),
        P(None, REGION),
        P(REGION),
    )
    out_specs = (P(REGION, None), P(), P(), P(REGION))
    return jax.shard_map(local, mesh=finer, in_specs=in_specs, out_specs=out_specs, check_vma=False)
```

```python
import jax
import jax.numpy as jnp
from jax import lax
from jax.experimental import pallas as pl
from jax.experimental.pallas import tpu as pltpu
from jax.sharding import Mesh
from jax.sharding import PartitionSpec as P


REGION = ("z", "yhi", "x")
MEMBER = ("ylo", "core")
CHIPS = ("ylo", "z", "yhi", "x")
EVERY = ("ylo", "core", "z", "yhi", "x")

SMOOTH_SQ = 0.01
C0 = 0.7978845608028654
C1 = 0.044715
WIDE = 256
PAD = 128
bf16 = jnp.bfloat16
f32 = jnp.float32
f16 = jnp.float16
EDGE = 16
DEEP = 128
SPLIT = 3


def dot(a, b, ca=1, cb=0):
    return lax.dot_general(a, b, (((ca,), (cb,)), ((), ())), preferred_element_type=f32)


def params(semantics, mib):
    return pltpu.CompilerParams(dimension_semantics=semantics, vmem_limit_bytes=mib << 20)


def whole(a):
    return pl.BlockSpec(a.shape, lambda *i: (0,) * a.ndim)


def prep_kernel(src, weight, at):
    nodes, wide = at.shape[0] - DEEP, at.shape[1]
    place = lax.broadcasted_iota(jnp.int32, (nodes, wide), 0)
    total = jnp.zeros((nodes, wide), f32)
    for k in range(src.shape[0]):
        total = total + jnp.where(src[k : k + 1, :] == place, weight[k : k + 1, :], 0.0)
    at[:nodes, :] = total.astype(bf16)
    first = lax.broadcasted_iota(jnp.int32, (DEEP, wide), 0) < SPLIT
    at[nodes:, :] = jnp.where(first, 1.0, 0.0).astype(bf16)


def prep(src, weight, nodes):
    fan, points = src.shape
    row = pl.BlockSpec((fan, WIDE), lambda i: (0, i))
    return pl.pallas_call(
        prep_kernel,
        grid=(points // WIDE,),
        in_specs=[row, row],
        out_specs=pl.BlockSpec((nodes + DEEP, WIDE), lambda i: (0, i)),
        out_shape=jax.ShapeDtypeStruct((nodes + DEEP, points), bf16),
        compiler_params=params(("arbitrary",), 8),
        name="prep",
    )(src, weight)


def turn_kernel(*refs):
    blocks, out = refs[:-1], refs[-1]
    for b, block in enumerate(blocks):
        nodes = block.shape[0]
        out[:, b * nodes : (b + 1) * nodes] = block[...].T


def turn(blocks):
    nodes, width = blocks[0].shape
    return pl.pallas_call(
        turn_kernel,
        grid=(width // WIDE,),
        in_specs=[pl.BlockSpec((nodes, WIDE), lambda i: (0, i))] * len(blocks),
        out_specs=pl.BlockSpec((WIDE, nodes * len(blocks)), lambda i: (i, 0)),
        out_shape=jax.ShapeDtypeStruct((width, nodes * len(blocks)), bf16),
        compiler_params=params(("arbitrary",), 8),
        name="turn",
    )(*blocks)


def forward_kernel(low, own, high, w_node, at, bias, w_out, target, hid, pre, err, proj):
    nodes = 3 * low.shape[0]

    @pl.when(pl.program_id(0) == 0)
    def _():
        stacked = jnp.concatenate([low[...], own[...], high[...]], axis=0)
        proj[:, :nodes] = dot(stacked, w_node[...]).astype(bf16).T
        proj[:, nodes:] = bias[...]

    for g in range(target.shape[1] // WIDE):
        cols = slice(g * WIDE, (g + 1) * WIDE)
        total = -target[:, cols]
        for r in range(proj.shape[0] // WIDE):
            rows = slice(r * WIDE, (r + 1) * WIDE)
            x = dot(proj[rows, :], at[:, cols])
            pre[rows, cols] = x.astype(bf16)
            u = 0.5 + 0.5 * jnp.tanh(x * (C0 + (C0 * C1) * (x * x)))
            hb = (x * u).astype(bf16)
            hid[rows, cols] = hb
            total = total + dot(w_out[:, rows], hb)
        err[:, cols] = total


def forward(low, own, high, w_node, at, bias, w_out, target):
    width = w_node.shape[1]
    points = at.shape[1]
    variables = target.shape[0]
    wide = 512

    def cut(rows):
        return pl.BlockSpec((rows, wide), lambda i: (0, i))

    return pl.pallas_call(
        forward_kernel,
        grid=(points // wide,),
        in_specs=[whole(low), whole(own), whole(high), whole(w_node), cut(at.shape[0]), whole(bias), whole(w_out), cut(variables)],
        out_specs=[cut(width), cut(width), cut(variables)],
        out_shape=[
            jax.ShapeDtypeStruct((width, points), bf16),
            jax.ShapeDtypeStruct((width, points), bf16),
            jax.ShapeDtypeStruct((variables, points), f32),
        ],
        scratch_shapes=[pltpu.VMEM((width, at.shape[0]), bf16)],
        compiler_params=params(("arbitrary",), 24),
        name="forward",
    )(low, own, high, w_node, at, bias, w_out, target)


def slope_kernel(pre_0, pre_1, out_0, out_1):
    for pre, out in ((pre_0, out_0), (pre_1, out_1)):
        for g in range(pre.shape[1] // WIDE):
            cols = slice(g * WIDE, (g + 1) * WIDE)
            x = pre[:, cols].astype(f32)
            sq = x * x
            u = 0.5 + 0.5 * jnp.tanh(x * (C0 + (C0 * C1) * sq))
            out[:, cols] = (u + (x * u) * (1.0 - u) * (2.0 * C0 + (6.0 * C0 * C1) * sq)).astype(bf16)


def slopes(pre):
    width, points = pre[0].shape
    rows = pl.BlockSpec((128, points), lambda i: (i, 0))
    return pl.pallas_call(
        slope_kernel,
        grid=(width // 128,),
        in_specs=[rows, rows],
        out_specs=[rows, rows],
        out_shape=[jax.ShapeDtypeStruct((width, points), bf16)] * 2,
        compiler_params=params(("arbitrary",), 8),
        name="slope",
    )(*pre)


def apart(d):
    q = d * d + SMOOTH_SQ
    r = lax.rsqrt(q)
    return q * r, d * r


def near_kernel(count, scale, own_0, own_1, *rest):
    others, (area, p_0, p_1, loss) = rest[:-4], rest[-4:]
    pairs = count * (count - 1)

    @pl.when(pl.program_id(0) == 0)
    def _():
        loss[...] = jnp.zeros_like(loss)

    for c in range(own_0.shape[1] // PAD):
        at = slice(c * PAD, (c + 1) * PAD)
        a, b = own_0[:, at], own_1[:, at]
        own_a, slope_a = apart(a)
        own_b, slope_b = apart(b)
        dist, t = apart(a - b)
        dist = 2.0 * dist
        sum_a, sum_b = t, -t
        for other in others:
            o = other[:, at]
            s, t = apart(a - o)
            dist = dist + s
            sum_a = sum_a + t
            s, t = apart(b - o)
            dist = dist + s
            sum_b = sum_b + t
        value = (own_a + own_b) * (1.0 / count) - dist * (0.5 / pairs)
        loss[...] += jnp.sum(value, axis=0, keepdims=True) * area[:, at] * (1.0 / scale)
        p_0[:, at] = slope_a * (1.0 / count) - sum_a * (1.0 / pairs)
        p_1[:, at] = slope_b * (1.0 / count) - sum_b * (1.0 / pairs)


def far_kernel(count, scale, own_0, own_1, *rest):
    others, (p_0, p_1, area, before, d_0, d_1, loss) = rest[:-7], rest[-7:]
    variables = own_0.shape[0]
    pairs = count * (count - 1)

    @pl.when(pl.program_id(0) == 0)
    def _():
        loss[...] = before[...]

    for c in range(own_0.shape[1] // PAD):
        at = slice(c * PAD, (c + 1) * PAD)
        a, b = own_0[:, at], own_1[:, at]
        dist, sum_a, sum_b = 0.0, 0.0, 0.0
        for other in others:
            o = other[:, at]
            s, t = apart(a - o)
            dist = dist + s
            sum_a = sum_a + t
            s, t = apart(b - o)
            dist = dist + s
            sum_b = sum_b + t
        where = area[:, at]
        loss[...] -= jnp.sum(dist, axis=0, keepdims=True) * where * (0.5 / pairs / scale)
        fold = where * (1.0 / variables)
        for ref, p, t in ((d_0, p_0, sum_a), (d_1, p_1, sum_b)):
            ref[:variables, at] = ((p[:, at] - t * (1.0 / pairs)) * fold).astype(bf16)
            ref[variables:, at] = jnp.zeros((PAD - variables, PAD), bf16)


def crps_near(own, others, area, count):
    variables, points = own[0].shape
    wide = 512
    field = pl.BlockSpec((variables, wide), lambda i: (0, i))
    row = pl.BlockSpec((1, wide), lambda i: (0, i))
    return pl.pallas_call(
        lambda *refs: near_kernel(count, variables * points, *refs),
        grid=(points // wide,),
        in_specs=[field] * (2 + len(others)) + [row],
        out_specs=[field, field, pl.BlockSpec((1, PAD), lambda i: (0, 0))],
        out_shape=[jax.ShapeDtypeStruct((variables, points), f32)] * 2 + [jax.ShapeDtypeStruct((1, PAD), f32)],
        compiler_params=params(("arbitrary",), 16),
        name="crps_near",
    )(*own, *others, area)


def crps_far(own, others, partial, area, before, count):
    variables, points = own[0].shape
    wide = 512
    field = pl.BlockSpec((variables, wide), lambda i: (0, i))
    padded = pl.BlockSpec((PAD, wide), lambda i: (0, i))
    row = pl.BlockSpec((1, wide), lambda i: (0, i))
    one = pl.BlockSpec((1, PAD), lambda i: (0, 0))
    return pl.pallas_call(
        lambda *refs: far_kernel(count, variables * points, *refs),
        grid=(points // wide,),
        in_specs=[field] * (4 + len(others)) + [row, one],
        out_specs=[padded, padded, one],
        out_shape=[jax.ShapeDtypeStruct((PAD, points), bf16)] * 2 + [jax.ShapeDtypeStruct((1, PAD), f32)],
        compiler_params=params(("arbitrary",), 16),
        name="crps_far",
    )(*own, *others, *partial, area, before)


def backward_kernel(variables, who, d_0, d_1, w_out_t, s_0, s_1, h_0, h_1, at, loss, contrib, heads, dpre):
    quarter = 2 * pl.program_id(0) + who[0]
    nodes = at.shape[0] - DEEP
    shape = (PAD, WIDE)
    row = lax.broadcasted_iota(jnp.int32, shape, 0)
    spot = lax.broadcasted_iota(jnp.int32, shape, 1) + quarter * WIDE
    total = jnp.where((row == variables + 1) & (spot == who[1]), jnp.sum(loss[...]), 0.0)
    for m, (d, slope, hid) in enumerate(((d_0, s_0, h_0), (d_1, s_1, h_1))):
        for g in range(d.shape[1] // WIDE):
            cut = slice(g * WIDE, (g + 1) * WIDE)
            dpre[m, :, cut] = (dot(w_out_t[...], d[:, cut]) * slope[:, cut].astype(f32)).astype(bf16)
        total = total + dot(d[...], hid[...], 1, 1)
        part = dot(at[: nodes + EDGE], dpre[m], 1, 1)
        contrib[m * nodes : (m + 1) * nodes, :] = part[:nodes].astype(bf16)
        total = total + jnp.where(row == variables, part[nodes : nodes + 1], 0.0)
    for i in range(PAD // 8):
        for j in range(WIDE // 128):
            heads[i, j] = total[i * 8 : (i + 1) * 8, j * 128 : (j + 1) * 128]


def backward(who, variables, dpred, w_out_t, slope, hid, at, loss):
    width, points = hid[0].shape
    nodes = at.shape[0] - DEEP
    count = width // WIDE // 2

    def fixed(a):
        return pl.BlockSpec(a.shape, lambda y, w: (0,) * a.ndim)

    rows = pl.BlockSpec((WIDE, points), lambda y, w: (2 * y + w[0], 0))
    narrow = pl.BlockSpec((WIDE, PAD), lambda y, w: (2 * y + w[0], 0))
    return pl.pallas_call(
        lambda *refs: backward_kernel(variables, *refs),
        grid_spec=pltpu.PrefetchScalarGridSpec(
            num_scalar_prefetch=1,
            grid=(count,),
            in_specs=[fixed(dpred[0]), fixed(dpred[1]), narrow, rows, rows, rows, rows, fixed(at), fixed(loss)],
            out_specs=[
                pl.BlockSpec((None, 2 * nodes, WIDE), lambda y, w: (y, 0, 0)),
                pl.BlockSpec((None, PAD // 8, WIDE // 128, 8, 128), lambda y, w: (y, 0, 0, 0, 0)),
            ],
            scratch_shapes=[pltpu.VMEM((2, WIDE, points), bf16)],
        ),
        out_shape=[
            jax.ShapeDtypeStruct((count, 2 * nodes, WIDE), bf16),
            jax.ShapeDtypeStruct((count, PAD // 8, WIDE // 128, 8, 128), f32),
        ],
        compiler_params=params(("arbitrary",), 28),
        name="backward",
    )(who, *dpred, w_out_t, *slope, *hid, at, loss)


def outer_kernel(lat_own, lat_other, c_own, c_other, out):
    for y in range(c_own.shape[0]):
        out[y] = (dot(lat_own[...], c_own[y]) + dot(lat_other[...], c_other[y])).astype(bf16)


def outer(lat_own, lat_other, c_own, c_other):
    inputs, nodes = lat_own.shape
    halves, _, quarter = c_own.shape
    lat = pl.BlockSpec((WIDE, nodes), lambda i: (i, 0))
    return pl.pallas_call(
        outer_kernel,
        grid=(inputs // WIDE,),
        in_specs=[lat, lat, whole(c_own), whole(c_own)],
        out_specs=pl.BlockSpec((halves, WIDE, quarter), lambda i: (0, i, 0)),
        out_shape=jax.ShapeDtypeStruct((halves, inputs, quarter), bf16),
        compiler_params=params(("arbitrary",), 16),
        name="outer",
    )(lat_own, lat_other, c_own, c_other)


def finish_kernel(pieces, out):
    per_row = WIDE // 128
    down = PAD // 8
    for at in range(pieces.shape[0]):
        core, z, x, yhi, ylo = at // 64, at // 16 % 4, at // 4 % 4, at // 2 % 2, at % 2
        piece = (((ylo * 2 + core) * 4 + z) * 2 + yhi) * 4 + x
        quarter, i, j = piece // (down * per_row), piece // per_row % down, piece % per_row
        left = quarter * WIDE + j * 128
        out[i * 8 : (i + 1) * 8, left : left + 128] = pieces[at]


def finish(pieces, width):
    return pl.pallas_call(
        finish_kernel,
        out_shape=jax.ShapeDtypeStruct((PAD, width), f32),
        compiler_params=pltpu.CompilerParams(vmem_limit_bytes=8 << 20),
        name="finish",
    )(pieces)


def local(latent, w_node, bias, w_out, edge_src, edge_weight, target, area):
    members, nodes, width = latent.shape
    variables = target.shape[0]
    regions = lax.axis_size(REGION)
    count = members * lax.axis_size(MEMBER)
    ahead = [(i, (i + 1) % regions) for i in range(regions)]
    behind = [(t, s) for s, t in ahead]
    swap = [(0, 1), (1, 0)]
    core = lax.axis_index("core")
    where = lax.axis_index(REGION)

    mine = [latent[m] for m in range(members)]

    def halo(block):
        before = lax.ppermute(block, REGION, ahead)
        return before, lax.ppermute(block, REGION, behind)

    low, high = [None] * members, [None] * members
    low[0], high[0] = halo(mine[0])
    at = prep(edge_src.T, edge_weight.T, 3 * nodes)
    parts, rest = [], bias
    for _ in range(SPLIT):
        parts.append(rest.astype(bf16))
        rest = rest - parts[-1].astype(f32)
    bias_cols = jnp.pad(jnp.stack(parts, axis=1), ((0, 0), (0, DEEP - SPLIT)))
    low[0], high[0], second = lax.optimization_barrier((low[0], high[0], mine[1]))
    low[1], high[1] = halo(second)
    w_out_t = jnp.pad(w_out, ((0, PAD - variables), (0, 0))).T

    hid, pre, err, near, far, beside = [], [], [], [], [], []
    for m in range(members):
        h, s, e = forward(low[m], mine[m], high[m], w_node, at, bias_cols, w_out, target)
        hid.append(h)
        pre.append(s)
        err.append(e)
        over = lax.ppermute((e * 0.125).astype(f16), "ylo", swap)
        near.append(lax.ppermute(e, "core", swap))
        far.append(over.astype(f32) * 8.0)
        beside.append(lax.ppermute(over, "core", swap).astype(f32) * 8.0)

    first, err[1] = lax.optimization_barrier((mine[0], err[1]))
    lat_t = turn((low[0], first, high[0], low[1], mine[1], high[1]))
    lat_t_other = lax.ppermute(lat_t, "core", swap)
    slope = slopes(pre)

    area_row = area[None, :]
    p_0, p_1, loss = crps_near(err, near + [far[0], beside[0]], area_row, count)
    d_0, d_1, loss = crps_far(err, [far[1], beside[1]], (p_0, p_1), area_row, loss, count)

    def back(side):
        who = jnp.stack([side, where]).astype(jnp.int32)
        return backward(who, variables, (d_0, d_1), w_out_t, slope, hid, at, loss)

    given, heads_given = back(1 - core)
    taken = lax.ppermute(given, "core", swap)
    kept, heads_kept = back(core)

    every = lax.axis_size(EVERY)
    even = core == 0
    heads = jnp.stack(
        [jnp.where(even, heads_kept, heads_given), jnp.where(even, heads_given, heads_kept)], axis=1
    )
    pieces = lax.all_to_all(heads.reshape(every, 8, 128), EVERY, split_axis=0, concat_axis=0, tiled=True)
    part = outer(lat_t, lat_t_other, kept, taken)
    chips = lax.axis_size(CHIPS)
    shares = lax.all_to_all(
        part.reshape(chips, width // regions, width // 4), CHIPS, split_axis=0, concat_axis=0, tiled=True
    )
    spread = pieces.sum(axis=0)[None]
    ring = [(0, 3), (3, 0), (1, 2), (2, 1)]
    pair = [(0, 1), (1, 0), (2, 3), (3, 2)]
    x, z = lax.axis_index("x"), lax.axis_index("z")
    steps = (
        ("ylo", swap, lax.axis_index("ylo")),
        (("ylo", "yhi"), ring, lax.axis_index("yhi")),
        ("x", pair, x % 2),
        ("x", ring, x // 2),
        ("z", pair, z % 2),
        ("z", ring, z // 2),
        ("core", swap, core),
    )
    for axis, moves, place in steps:
        other = lax.ppermute(spread, axis, moves)
        spread = jnp.where(
            place == 0, jnp.concatenate([spread, other]), jnp.concatenate([other, spread])
        )
    own = shares.astype(f32).sum(axis=0)
    grad_node = lax.all_gather(own, MEMBER, axis=1, tiled=True)
    full = finish(spread, width)
    grad_out = full[:variables]
    grad_bias = full[variables]
    loss_here = lax.dynamic_slice(full, (variables + 1, where), (1, 1)).reshape(1)
    return grad_node, grad_out, grad_bias, loss_here


def solution(mesh):
    finer = Mesh(mesh.devices.reshape(2, 2, 4, 2, 4), EVERY)
    in_specs = (
        P(MEMBER, REGION, None),
        P(),
        P(),
        P(),
        P(REGION, None),
        P(REGION, None),
        P(None, REGION),
        P(REGION),
    )
    out_specs = (P(REGION, None), P(), P(), P(REGION))

    return jax.shard_map(local, mesh=finer, in_specs=in_specs, out_specs=out_specs, check_vma=False)
```

```python
import jax
import jax.numpy as jnp
from jax import lax
from jax.experimental import pallas as pl
from jax.experimental.pallas import tpu as pltpu
from jax.sharding import Mesh
from jax.sharding import PartitionSpec as P


REGION = ("z", "yhi", "x")
MEMBER = ("ylo", "core")
CHIPS = ("ylo", "z", "yhi", "x")
EVERY = ("ylo", "core", "z", "yhi", "x")

SMOOTH_SQ = 0.01
C0 = 0.7978845608028654
C1 = 0.044715
WIDE = 256
PAD = 128
bf16 = jnp.bfloat16
f32 = jnp.float32
f16 = jnp.float16
EDGE = 16
DEEP = 128
SPLIT = 3


def dot(a, b, ca=1, cb=0):
    return lax.dot_general(a, b, (((ca,), (cb,)), ((), ())), preferred_element_type=f32)


def params(semantics, mib):
    return pltpu.CompilerParams(dimension_semantics=semantics, vmem_limit_bytes=mib << 20)


def parked(a):
    return pltpu.with_memory_space_constraint(a, pltpu.HBM)


def whole(a):
    return pl.BlockSpec(a.shape, lambda *i: (0,) * a.ndim)


def prep_kernel(src, weight, at):
    nodes, wide = at.shape[0] - DEEP, at.shape[1]
    place = lax.broadcasted_iota(jnp.int32, (nodes, wide), 0)
    total = jnp.zeros((nodes, wide), f32)
    for k in range(src.shape[0]):
        total = total + jnp.where(src[k : k + 1, :] == place, weight[k : k + 1, :], 0.0)
    at[:nodes, :] = total.astype(bf16)
    first = lax.broadcasted_iota(jnp.int32, (DEEP, wide), 0) < SPLIT
    at[nodes:, :] = jnp.where(first, 1.0, 0.0).astype(bf16)


def prep(src, weight, nodes):
    fan, points = src.shape
    row = pl.BlockSpec((fan, WIDE), lambda i: (0, i))
    return pl.pallas_call(
        prep_kernel,
        grid=(points // WIDE,),
        in_specs=[row, row],
        out_specs=pl.BlockSpec((nodes + DEEP, WIDE), lambda i: (0, i)),
        out_shape=jax.ShapeDtypeStruct((nodes + DEEP, points), bf16),
        compiler_params=params(("arbitrary",), 8),
        name="prep",
    )(src, weight)


def turn_kernel(*refs):
    blocks, out = refs[:-1], refs[-1]
    for b, block in enumerate(blocks):
        nodes = block.shape[0]
        out[:, b * nodes : (b + 1) * nodes] = block[...].T


def turn(blocks):
    nodes, width = blocks[0].shape
    return pl.pallas_call(
        turn_kernel,
        grid=(width // WIDE,),
        in_specs=[pl.BlockSpec((nodes, WIDE), lambda i: (0, i))] * len(blocks),
        out_specs=pl.BlockSpec((WIDE, nodes * len(blocks)), lambda i: (i, 0)),
        out_shape=jax.ShapeDtypeStruct((width, nodes * len(blocks)), bf16),
        compiler_params=params(("arbitrary",), 8),
        name="turn",
    )(*blocks)


def forward_kernel(low, own, high, w_node, at, bias, w_out, target, hid, pre, err, proj):
    nodes = 3 * low.shape[0]

    @pl.when(pl.program_id(0) == 0)
    def _():
        stacked = jnp.concatenate([low[...], own[...], high[...]], axis=0)
        proj[:, :nodes] = dot(stacked, w_node[...]).astype(bf16).T
        row = lax.broadcasted_iota(jnp.int32, (DEEP, proj.shape[0]), 0)
        block, rest = jnp.zeros(row.shape, f32), bias[...]
        for k in range(SPLIT):
            part = rest.astype(bf16).astype(f32)
            block = jnp.where(row == k, part, block)
            rest = rest - part
        proj[:, nodes:] = block.T.astype(bf16)

    for g in range(target.shape[1] // WIDE):
        cols = slice(g * WIDE, (g + 1) * WIDE)
        total = -target[:, cols]
        for r in range(proj.shape[0] // WIDE):
            rows = slice(r * WIDE, (r + 1) * WIDE)
            x = dot(proj[rows, :], at[:, cols])
            pre[rows, cols] = x.astype(bf16)
            u = 0.5 + 0.5 * jnp.tanh(x * (C0 + (C0 * C1) * (x * x)))
            hb = (x * u).astype(bf16)
            hid[rows, cols] = hb
            total = total + dot(w_out[:, rows], hb)
        err[:, cols] = total


def forward(low, own, high, w_node, at, bias, w_out, target):
    width = w_node.shape[1]
    points = at.shape[1]
    variables = target.shape[0]
    wide = 512

    def cut(rows):
        return pl.BlockSpec((rows, wide), lambda i: (0, i))

    return pl.pallas_call(
        forward_kernel,
        grid=(points // wide,),
        in_specs=[whole(low), whole(own), whole(high), whole(w_node), cut(at.shape[0]), whole(bias), whole(w_out), cut(variables)],
        out_specs=[cut(width), cut(width), cut(variables)],
        out_shape=[
            pltpu.HBM((width, points), bf16),
            pltpu.HBM((width, points), bf16),
            jax.ShapeDtypeStruct((variables, points), f32),
        ],
        scratch_shapes=[pltpu.VMEM((width, at.shape[0]), bf16)],
        compiler_params=params(("arbitrary",), 24),
        name="forward",
    )(low, own, high, parked(w_node), at, bias, w_out, parked(target))


def slope_kernel(pre_0, pre_1, out_0, out_1):
    for pre, out in ((pre_0, out_0), (pre_1, out_1)):
        for g in range(pre.shape[1] // WIDE):
            cols = slice(g * WIDE, (g + 1) * WIDE)
            x = pre[:, cols].astype(f32)
            sq = x * x
            u = 0.5 + 0.5 * jnp.tanh(x * (C0 + (C0 * C1) * sq))
            out[:, cols] = (u + (x * u) * (1.0 - u) * (2.0 * C0 + (6.0 * C0 * C1) * sq)).astype(bf16)


def slopes(pre):
    width, points = pre[0].shape
    rows = pl.BlockSpec((128, points), lambda i: (i, 0))
    return pl.pallas_call(
        slope_kernel,
        grid=(width // 128,),
        in_specs=[rows, rows],
        out_specs=[rows, rows],
        out_shape=[pltpu.HBM((width, points), bf16)] * 2,
        compiler_params=params(("arbitrary",), 8),
        name="slope",
    )(*map(parked, pre))


def apart(d):
    q = d * d + SMOOTH_SQ
    r = lax.rsqrt(q)
    return q * r, d * r


def near_kernel(count, scale, own_0, own_1, *rest):
    others, (area, p_0, p_1, loss) = rest[:-4], rest[-4:]
    pairs = count * (count - 1)

    @pl.when(pl.program_id(0) == 0)
    def _():
        loss[...] = jnp.zeros_like(loss)

    for c in range(own_0.shape[1] // PAD):
        at = slice(c * PAD, (c + 1) * PAD)
        a, b = own_0[:, at], own_1[:, at]
        own_a, slope_a = apart(a)
        own_b, slope_b = apart(b)
        dist, t = apart(a - b)
        dist = 2.0 * dist
        sum_a, sum_b = t, -t
        for other in others:
            o = other[:, at]
            s, t = apart(a - o)
            dist = dist + s
            sum_a = sum_a + t
            s, t = apart(b - o)
            dist = dist + s
            sum_b = sum_b + t
        value = (own_a + own_b) * (1.0 / count) - dist * (0.5 / pairs)
        loss[...] += jnp.sum(value, axis=0, keepdims=True) * area[:, at] * (1.0 / scale)
        p_0[:, at] = slope_a * (1.0 / count) - sum_a * (1.0 / pairs)
        p_1[:, at] = slope_b * (1.0 / count) - sum_b * (1.0 / pairs)


def far_kernel(count, scale, own_0, own_1, *rest):
    others, (p_0, p_1, area, before, d_0, d_1, loss) = rest[:-7], rest[-7:]
    variables = own_0.shape[0]
    pairs = count * (count - 1)

    @pl.when(pl.program_id(0) == 0)
    def _():
        loss[...] = before[...]

    for c in range(own_0.shape[1] // PAD):
        at = slice(c * PAD, (c + 1) * PAD)
        a, b = own_0[:, at], own_1[:, at]
        dist, sum_a, sum_b = 0.0, 0.0, 0.0
        for other in others:
            o = other[:, at]
            s, t = apart(a - o)
            dist = dist + s
            sum_a = sum_a + t
            s, t = apart(b - o)
            dist = dist + s
            sum_b = sum_b + t
        where = area[:, at]
        loss[...] -= jnp.sum(dist, axis=0, keepdims=True) * where * (0.5 / pairs / scale)
        fold = where * (1.0 / variables)
        for ref, p, t in ((d_0, p_0, sum_a), (d_1, p_1, sum_b)):
            ref[:variables, at] = ((p[:, at] - t * (1.0 / pairs)) * fold).astype(bf16)
            ref[variables:, at] = jnp.zeros((PAD - variables, PAD), bf16)


def crps_near(own, others, area, count):
    variables, points = own[0].shape
    wide = 512
    field = pl.BlockSpec((variables, wide), lambda i: (0, i))
    row = pl.BlockSpec((1, wide), lambda i: (0, i))
    return pl.pallas_call(
        lambda *refs: near_kernel(count, variables * points, *refs),
        grid=(points // wide,),
        in_specs=[field] * (2 + len(others)) + [row],
        out_specs=[field, field, pl.BlockSpec((1, PAD), lambda i: (0, 0))],
        out_shape=[jax.ShapeDtypeStruct((variables, points), f32)] * 2 + [jax.ShapeDtypeStruct((1, PAD), f32)],
        compiler_params=params(("arbitrary",), 16),
        name="crps_near",
    )(*own, *others, area)


def crps_far(own, others, partial, area, before, count):
    variables, points = own[0].shape
    wide = 512
    field = pl.BlockSpec((variables, wide), lambda i: (0, i))
    padded = pl.BlockSpec((PAD, wide), lambda i: (0, i))
    row = pl.BlockSpec((1, wide), lambda i: (0, i))
    one = pl.BlockSpec((1, PAD), lambda i: (0, 0))
    return pl.pallas_call(
        lambda *refs: far_kernel(count, variables * points, *refs),
        grid=(points // wide,),
        in_specs=[field] * (4 + len(others)) + [row, one],
        out_specs=[padded, padded, one],
        out_shape=[jax.ShapeDtypeStruct((PAD, points), bf16)] * 2 + [jax.ShapeDtypeStruct((1, PAD), f32)],
        compiler_params=params(("arbitrary",), 16),
        name="crps_far",
    )(*own, *others, *partial, area, before)


def heads_kernel(variables, where, d_0, d_1, h_0, h_1, loss, heads):
    shape = (PAD, WIDE)
    row = lax.broadcasted_iota(jnp.int32, shape, 0)
    spot = lax.broadcasted_iota(jnp.int32, shape, 1) + pl.program_id(0) * WIDE
    total = jnp.where((row == variables + 1) & (spot == where[0]), jnp.sum(loss[...]), 0.0)
    total = total + dot(d_0[...], h_0[...], 1, 1) + dot(d_1[...], h_1[...], 1, 1)
    for i in range(PAD // 8):
        for j in range(WIDE // 128):
            heads[i, j] = total[i * 8 : (i + 1) * 8, j * 128 : (j + 1) * 128]


def head_parts(where, variables, dpred, hid, loss):
    width, points = hid[0].shape
    quarters = width // WIDE

    def fixed(a):
        return pl.BlockSpec(a.shape, lambda q, w: (0,) * a.ndim)

    rows = pl.BlockSpec((WIDE, points), lambda q, w: (q, 0))
    return pl.pallas_call(
        lambda *refs: heads_kernel(variables, *refs),
        grid_spec=pltpu.PrefetchScalarGridSpec(
            num_scalar_prefetch=1,
            grid=(quarters,),
            in_specs=[fixed(dpred[0]), fixed(dpred[1]), rows, rows, fixed(loss)],
            out_specs=pl.BlockSpec((None, PAD // 8, WIDE // 128, 8, 128), lambda q, w: (q, 0, 0, 0, 0)),
        ),
        out_shape=pltpu.HBM((quarters, PAD // 8, WIDE // 128, 8, 128), f32),
        compiler_params=params(("arbitrary",), 16),
        name="heads",
    )(where, *dpred, *map(parked, hid), loss)


def backward_kernel(who, d_0, d_1, w_out, s_0, s_1, at, contrib, summed, dpre):
    nodes = at.shape[0] - DEEP
    variables = w_out.shape[0]
    turned = w_out[...].T
    total = None
    for m, (d, slope) in enumerate(((d_0, s_0), (d_1, s_1))):
        for g in range(d.shape[1] // WIDE):
            cut = slice(g * WIDE, (g + 1) * WIDE)
            dpre[m, :, cut] = (dot(turned, d[:variables, cut]) * slope[:, cut].astype(f32)).astype(bf16)
        part = dot(at[: nodes + EDGE], dpre[m], 1, 1)
        contrib[m * nodes : (m + 1) * nodes, :] = part[:nodes].astype(bf16)
        edge = part[nodes : nodes + 8]
        total = edge if total is None else total + edge
    summed[...] = total


def backward(who, dpred, w_out, slope, at):
    width, points = slope[0].shape
    nodes = at.shape[0] - DEEP
    count = width // WIDE // 2

    def fixed(a):
        return pl.BlockSpec(a.shape, lambda y, w: (0,) * a.ndim)

    rows = pl.BlockSpec((WIDE, points), lambda y, w: (2 * y + w[0], 0))
    narrow = pl.BlockSpec((w_out.shape[0], WIDE), lambda y, w: (0, 2 * y + w[0]))
    return pl.pallas_call(
        backward_kernel,
        grid_spec=pltpu.PrefetchScalarGridSpec(
            num_scalar_prefetch=1,
            grid=(count,),
            in_specs=[fixed(dpred[0]), fixed(dpred[1]), narrow, rows, rows, fixed(at)],
            out_specs=[
                pl.BlockSpec((None, 2 * nodes, WIDE), lambda y, w: (y, 0, 0)),
                pl.BlockSpec((None, 8, WIDE), lambda y, w: (y, 0, 0)),
            ],
            scratch_shapes=[pltpu.VMEM((2, WIDE, points), bf16)],
        ),
        out_shape=[
            pltpu.HBM((count, 2 * nodes, WIDE), bf16),
            jax.ShapeDtypeStruct((count, 8, WIDE), f32),
        ],
        compiler_params=params(("arbitrary",), 20),
        name="backward",
    )(who, *dpred, w_out, *map(parked, slope), at)


def outer_kernel(lat_own, lat_other, c_own, c_other, out):
    for y in range(c_own.shape[0]):
        out[y] = (dot(lat_own[...], c_own[y]) + dot(lat_other[...], c_other[y])).astype(bf16)


def outer(lat_own, lat_other, c_own, c_other):
    inputs, nodes = lat_own.shape
    halves, _, quarter = c_own.shape
    lat = pl.BlockSpec((WIDE, nodes), lambda i: (i, 0))
    return pl.pallas_call(
        outer_kernel,
        grid=(inputs // WIDE,),
        in_specs=[lat, lat, whole(c_own), whole(c_own)],
        out_specs=pl.BlockSpec((halves, WIDE, quarter), lambda i: (0, i, 0)),
        out_shape=jax.ShapeDtypeStruct((halves, inputs, quarter), bf16),
        compiler_params=params(("arbitrary",), 16),
        name="outer",
    )(parked(lat_own), parked(lat_other), parked(c_own), parked(c_other))


def finish_kernel(where, pieces, grad_out, grad_bias, loss):
    variables, width = grad_out.shape
    per_row = WIDE // 128
    down = PAD // 8
    groups, held = pieces.shape[0], pieces.shape[1] - 1
    total = pieces[0, held]
    for group in range(1, groups):
        total = total + pieces[group, held]
    for k in range(width // 128):
        grad_bias[:, k * 128 : (k + 1) * 128] = total[k : k + 1]
    for group in range(groups):
        core, z = group // 4, group % 4
        for at in range(held):
            x, yhi, ylo = at // 4, at // 2 % 2, at % 2
            piece = (((ylo * 2 + core) * 4 + z) * 2 + yhi) * 4 + x
            quarter, i, j = piece // (down * per_row), piece // per_row % down, piece % per_row
            left = quarter * WIDE + j * 128
            top = i * 8
            rows = max(0, min(8, variables - top))
            if rows:
                grad_out[top : top + rows, left : left + 128] = pieces[group, at, :rows]
            line = variables + 1 - top
            if left == 0 and 0 <= line < 8:
                values = pieces[group, at, line : line + 1]
                spot = lax.broadcasted_iota(jnp.int32, values.shape, 1)
                loss[...] = jnp.sum(jnp.where(spot == where[0], values, 0.0), axis=1, keepdims=True)


def finish(where, pieces, variables, width):
    return pl.pallas_call(
        finish_kernel,
        in_specs=[pl.BlockSpec(memory_space=pltpu.SMEM), pl.BlockSpec(memory_space=pltpu.VMEM)],
        out_shape=[
            jax.ShapeDtypeStruct((variables, width), f32),
            jax.ShapeDtypeStruct((1, width), f32),
            jax.ShapeDtypeStruct((1, 1), f32),
        ],
        compiler_params=pltpu.CompilerParams(vmem_limit_bytes=8 << 20),
        name="finish",
    )(where, pieces)


def local(latent, w_node, bias, w_out, edge_src, edge_weight, target, area):
    members, nodes, width = latent.shape
    variables = target.shape[0]
    regions = lax.axis_size(REGION)
    count = members * lax.axis_size(MEMBER)
    ahead = [(i, (i + 1) % regions) for i in range(regions)]
    behind = [(t, s) for s, t in ahead]
    swap = [(0, 1), (1, 0)]
    core = lax.axis_index("core")
    where = lax.axis_index(REGION)

    mine = [latent[m] for m in range(members)]

    low, high = [], []
    for m in range(members):
        low.append(lax.ppermute(mine[m], REGION, ahead))
        high.append(lax.ppermute(mine[m], REGION, behind))
    at = prep(edge_src.T, edge_weight.T, 3 * nodes)
    bias_row = bias[None, :]

    hid, pre, err, near, far, beside = [], [], [], [], [], []
    for m in range(members):
        h, s, e = forward(low[m], mine[m], high[m], w_node, at, bias_row, w_out, target)
        hid.append(h)
        pre.append(s)
        err.append(e)
        over = lax.ppermute((e * 0.125).astype(f16), "ylo", swap)
        near.append(lax.ppermute(e, "core", swap))
        far.append(over.astype(f32) * 8.0)
        beside.append(lax.ppermute(over, "core", swap).astype(f32) * 8.0)

    first, err[1] = lax.optimization_barrier((mine[0], err[1]))
    lat_t = turn((low[0], first, high[0], low[1], mine[1], high[1]))
    lat_t_other = lax.ppermute(lat_t, "core", swap)
    slope = slopes(pre)

    area_row = area[None, :]
    p_0, p_1, loss = crps_near(err, near + [far[0], beside[0]], area_row, count)
    d_0, d_1, loss = crps_far(err, [far[1], beside[1]], (p_0, p_1), area_row, loss, count)

    spot = where[None].astype(jnp.int32)
    every = lax.axis_size(EVERY)
    heads = head_parts(spot, variables, (d_0, d_1), hid, loss)
    pieces = lax.all_to_all(heads.reshape(every, 8, 128), EVERY, split_axis=0, concat_axis=0, tiled=True)

    def back(side):
        return backward(side[None].astype(jnp.int32), (d_0, d_1), w_out, slope, at)

    given, bias_given = back(1 - core)
    taken = lax.ppermute(given, "core", swap)
    kept, bias_kept = back(core)
    part = outer(lat_t, lat_t_other, kept, taken)
    chips = lax.axis_size(CHIPS)
    shares = lax.all_to_all(
        part.reshape(chips, width // regions, width // 4), CHIPS, split_axis=0, concat_axis=0, tiled=True
    )
    even = core == 0
    summed = jnp.stack(
        [jnp.where(even, bias_kept, bias_given)[:, 0], jnp.where(even, bias_given, bias_kept)[:, 0]], axis=1
    ).reshape(1, 8, 128)
    spread = pieces.sum(axis=0)[None]
    ring = [(0, 3), (3, 0), (1, 2), (2, 1)]
    pair = [(0, 1), (1, 0), (2, 3), (3, 2)]
    x = lax.axis_index("x")
    steps = (
        ("ylo", swap, lax.axis_index("ylo")),
        (("ylo", "yhi"), ring, lax.axis_index("yhi")),
        ("x", pair, x % 2),
        ("x", ring, x // 2),
    )
    for axis, moves, place in steps:
        other = lax.ppermute(jnp.concatenate([spread, summed]), axis, moves)
        summed = summed + other[-1:]
        other = other[:-1]
        spread = jnp.where(
            place == 0, jnp.concatenate([spread, other]), jnp.concatenate([other, spread])
        )
    spread = jnp.concatenate([spread, summed])
    rest = ("core", "z")
    table = lax.all_to_all(
        jnp.broadcast_to(spread, (lax.axis_size(rest), *spread.shape)), rest, split_axis=0, concat_axis=0, tiled=True
    )
    own = shares.astype(f32).sum(axis=0)
    grad_node = lax.all_gather(own, MEMBER, axis=1, tiled=True)
    grad_out, grad_bias, loss_here = finish(spot, table, variables, width)
    grad_bias = grad_bias.reshape(width)
    loss_here = loss_here.reshape(1)
    return grad_node, grad_out, grad_bias, loss_here


def solution(mesh):
    finer = Mesh(mesh.devices.reshape(2, 2, 4, 2, 4), EVERY)
    in_specs = (
        P(MEMBER, REGION, None),
        P(),
        P(),
        P(),
        P(REGION, None),
        P(REGION, None),
        P(None, REGION),
        P(REGION),
    )
    out_specs = (P(REGION, None), P(), P(), P(REGION))

    return jax.shard_map(local, mesh=finer, in_specs=in_specs, out_specs=out_specs, check_vma=False)
```

```python
import jax
import jax.numpy as jnp
from jax import lax
from jax.experimental import pallas as pl
from jax.experimental.pallas import tpu as pltpu
from jax.sharding import Mesh
from jax.sharding import PartitionSpec as P


REGION = ("z", "yhi", "x")
MEMBER = ("ylo", "core")
CHIPS = ("ylo", "z", "yhi", "x")
EVERY = ("ylo", "core", "z", "yhi", "x")

SMOOTH_SQ = 0.01
C0 = 0.7978845608028654
C1 = 0.044715
WIDE = 256
PAD = 128
bf16 = jnp.bfloat16
f32 = jnp.float32
f16 = jnp.float16
EDGE = 16
DEEP = 128
SPLIT = 3


def dot(a, b, ca=1, cb=0):
    return lax.dot_general(a, b, (((ca,), (cb,)), ((), ())), preferred_element_type=f32)


def params(semantics, mib):
    return pltpu.CompilerParams(dimension_semantics=semantics, vmem_limit_bytes=mib << 20)


def parked(a):
    return pltpu.with_memory_space_constraint(a, pltpu.VMEM)


def whole(a):
    return pl.BlockSpec(a.shape, lambda *i: (0,) * a.ndim)


def prep_kernel(src, weight, at):
    nodes, wide = at.shape[0] - DEEP, at.shape[1]
    place = lax.broadcasted_iota(jnp.int32, (nodes, wide), 0)
    total = jnp.zeros((nodes, wide), f32)
    for k in range(src.shape[0]):
        total = total + jnp.where(src[k : k + 1, :] == place, weight[k : k + 1, :], 0.0)
    at[:nodes, :] = total.astype(bf16)
    first = lax.broadcasted_iota(jnp.int32, (DEEP, wide), 0) < SPLIT
    at[nodes:, :] = jnp.where(first, 1.0, 0.0).astype(bf16)


def prep(src, weight, nodes):
    fan, points = src.shape
    row = pl.BlockSpec((fan, WIDE), lambda i: (0, i))
    return pl.pallas_call(
        prep_kernel,
        grid=(points // WIDE,),
        in_specs=[row, row],
        out_specs=pl.BlockSpec((nodes + DEEP, WIDE), lambda i: (0, i)),
        out_shape=pltpu.VMEM((nodes + DEEP, points), bf16),
        compiler_params=params(("arbitrary",), 8),
        name="prep",
    )(src, weight)


def turn_kernel(*refs):
    blocks, out = refs[:-1], refs[-1]
    for b, block in enumerate(blocks):
        nodes = block.shape[0]
        out[:, b * nodes : (b + 1) * nodes] = block[...].T


def turn(blocks):
    nodes, width = blocks[0].shape
    return pl.pallas_call(
        turn_kernel,
        grid=(width // WIDE,),
        in_specs=[pl.BlockSpec((nodes, WIDE), lambda i: (0, i))] * len(blocks),
        out_specs=pl.BlockSpec((WIDE, nodes * len(blocks)), lambda i: (i, 0)),
        out_shape=pltpu.VMEM((width, nodes * len(blocks)), bf16),
        compiler_params=params(("arbitrary",), 8),
        name="turn",
    )(*blocks)


def forward_kernel(low, own, high, w_node, at, bias, w_out, target, hid, pre, err, proj):
    nodes = 3 * low.shape[0]

    @pl.when(pl.program_id(0) == 0)
    def _():
        stacked = jnp.concatenate([low[...], own[...], high[...]], axis=0)
        proj[:, :nodes] = dot(stacked, w_node[...]).astype(bf16).T
        row = lax.broadcasted_iota(jnp.int32, (DEEP, proj.shape[0]), 0)
        block, rest = jnp.zeros(row.shape, f32), bias[...]
        for k in range(SPLIT):
            part = rest.astype(bf16).astype(f32)
            block = jnp.where(row == k, part, block)
            rest = rest - part
        proj[:, nodes:] = block.T.astype(bf16)

    for g in range(target.shape[1] // WIDE):
        cols = slice(g * WIDE, (g + 1) * WIDE)
        total = -target[:, cols]
        for r in range(proj.shape[0] // WIDE):
            rows = slice(r * WIDE, (r + 1) * WIDE)
            x = dot(proj[rows, :], at[:, cols])
            pre[rows, cols] = x.astype(bf16)
            u = 0.5 + 0.5 * jnp.tanh(x * (C0 + (C0 * C1) * (x * x)))
            hb = (x * u).astype(bf16)
            hid[rows, cols] = hb
            total = total + dot(w_out[:, rows], hb)
        err[:, cols] = total


def forward(low, own, high, w_node, at, bias, w_out, target):
    width = w_node.shape[1]
    points = at.shape[1]
    variables = target.shape[0]
    wide = 512

    def cut(rows):
        return pl.BlockSpec((rows, wide), lambda i: (0, i))

    return pl.pallas_call(
        forward_kernel,
        grid=(points // wide,),
        in_specs=[whole(low), whole(own), whole(high), whole(w_node), cut(at.shape[0]), whole(bias), whole(w_out), cut(variables)],
        out_specs=[cut(width), cut(width), cut(variables)],
        out_shape=[
            pltpu.VMEM((width, points), bf16),
            pltpu.VMEM((width, points), bf16),
            pltpu.VMEM((variables, points), f32),
        ],
        scratch_shapes=[pltpu.VMEM((width, at.shape[0]), bf16)],
        compiler_params=params(("arbitrary",), 24),
        name="forward",
    )(low, own, high, parked(w_node), parked(at), bias, parked(w_out), parked(target))


def slope_kernel(pre_0, pre_1, out_0, out_1):
    for pre, out in ((pre_0, out_0), (pre_1, out_1)):
        for g in range(pre.shape[1] // WIDE):
            cols = slice(g * WIDE, (g + 1) * WIDE)
            x = pre[:, cols].astype(f32)
            sq = x * x
            u = 0.5 + 0.5 * jnp.tanh(x * (C0 + (C0 * C1) * sq))
            out[:, cols] = (u + (x * u) * (1.0 - u) * (2.0 * C0 + (6.0 * C0 * C1) * sq)).astype(bf16)


def slopes(pre):
    width, points = pre[0].shape
    rows = pl.BlockSpec((128, points), lambda i: (i, 0))
    return pl.pallas_call(
        slope_kernel,
        grid=(width // 128,),
        in_specs=[rows, rows],
        out_specs=[rows, rows],
        out_shape=[pltpu.VMEM((width, points), bf16)] * 2,
        compiler_params=params(("arbitrary",), 8),
        name="slope",
    )(*map(parked, pre))


def apart(d):
    q = d * d + SMOOTH_SQ
    r = lax.rsqrt(q)
    return q * r, d * r


def near_kernel(count, scale, own_0, own_1, *rest):
    others, (area, p_0, p_1, loss) = rest[:-4], rest[-4:]
    pairs = count * (count - 1)

    @pl.when(pl.program_id(0) == 0)
    def _():
        loss[...] = jnp.zeros_like(loss)

    for c in range(own_0.shape[1] // PAD):
        at = slice(c * PAD, (c + 1) * PAD)
        a, b = own_0[:, at], own_1[:, at]
        own_a, slope_a = apart(a)
        own_b, slope_b = apart(b)
        dist, t = apart(a - b)
        dist = 2.0 * dist
        sum_a, sum_b = t, -t
        for other in others:
            o = other[:, at]
            s, t = apart(a - o)
            dist = dist + s
            sum_a = sum_a + t
            s, t = apart(b - o)
            dist = dist + s
            sum_b = sum_b + t
        value = (own_a + own_b) * (1.0 / count) - dist * (0.5 / pairs)
        loss[...] += jnp.sum(value, axis=0, keepdims=True) * area[:, at] * (1.0 / scale)
        p_0[:, at] = slope_a * (1.0 / count) - sum_a * (1.0 / pairs)
        p_1[:, at] = slope_b * (1.0 / count) - sum_b * (1.0 / pairs)


def far_kernel(count, scale, own_0, own_1, *rest):
    others, (p_0, p_1, area, before, d_0, d_1, loss) = rest[:-7], rest[-7:]
    variables = own_0.shape[0]
    pairs = count * (count - 1)

    @pl.when(pl.program_id(0) == 0)
    def _():
        loss[...] = before[...]

    for c in range(own_0.shape[1] // PAD):
        at = slice(c * PAD, (c + 1) * PAD)
        a, b = own_0[:, at], own_1[:, at]
        dist, sum_a, sum_b = 0.0, 0.0, 0.0
        for other in others:
            o = other[:, at]
            s, t = apart(a - o)
            dist = dist + s
            sum_a = sum_a + t
            s, t = apart(b - o)
            dist = dist + s
            sum_b = sum_b + t
        where = area[:, at]
        loss[...] -= jnp.sum(dist, axis=0, keepdims=True) * where * (0.5 / pairs / scale)
        fold = where * (1.0 / variables)
        for ref, p, t in ((d_0, p_0, sum_a), (d_1, p_1, sum_b)):
            ref[:variables, at] = ((p[:, at] - t * (1.0 / pairs)) * fold).astype(bf16)
            ref[variables:, at] = jnp.zeros((PAD - variables, PAD), bf16)


def crps_near(own, others, area, count):
    variables, points = own[0].shape
    wide = 512
    field = pl.BlockSpec((variables, wide), lambda i: (0, i))
    row = pl.BlockSpec((1, wide), lambda i: (0, i))
    return pl.pallas_call(
        lambda *refs: near_kernel(count, variables * points, *refs),
        grid=(points // wide,),
        in_specs=[field] * (2 + len(others)) + [row],
        out_specs=[field, field, pl.BlockSpec((1, PAD), lambda i: (0, 0))],
        out_shape=[pltpu.VMEM((variables, points), f32)] * 2 + [jax.ShapeDtypeStruct((1, PAD), f32)],
        compiler_params=params(("arbitrary",), 16),
        name="crps_near",
    )(*map(parked, own), *others, area)


def crps_far(own, others, partial, area, before, count):
    variables, points = own[0].shape
    wide = 512
    field = pl.BlockSpec((variables, wide), lambda i: (0, i))
    padded = pl.BlockSpec((PAD, wide), lambda i: (0, i))
    row = pl.BlockSpec((1, wide), lambda i: (0, i))
    one = pl.BlockSpec((1, PAD), lambda i: (0, 0))
    return pl.pallas_call(
        lambda *refs: far_kernel(count, variables * points, *refs),
        grid=(points // wide,),
        in_specs=[field] * (4 + len(others)) + [row, one],
        out_specs=[padded, padded, one],
        out_shape=[pltpu.VMEM((PAD, points), bf16)] * 2 + [jax.ShapeDtypeStruct((1, PAD), f32)],
        compiler_params=params(("arbitrary",), 16),
        name="crps_far",
    )(*map(parked, own), *others, *map(parked, partial), area, before)


def backward_kernel(who, d_0, d_1, w_out, s_0, s_1, h_0, h_1, at, loss, contrib, heads, dpre):
    nodes = at.shape[0] - DEEP
    variables = w_out.shape[0]
    shape = (PAD, WIDE)
    row = lax.broadcasted_iota(jnp.int32, shape, 0)
    spot = lax.broadcasted_iota(jnp.int32, shape, 1) + (2 * pl.program_id(0) + who[0]) * WIDE
    total = jnp.where((row == variables + 1) & (spot == who[1]), jnp.sum(loss[...]), 0.0)
    turned = w_out[...].T
    for m, (d, slope, hid) in enumerate(((d_0, s_0, h_0), (d_1, s_1, h_1))):
        for g in range(d.shape[1] // WIDE):
            cut = slice(g * WIDE, (g + 1) * WIDE)
            dpre[m, :, cut] = (dot(turned, d[:variables, cut]) * slope[:, cut].astype(f32)).astype(bf16)
        total = total + dot(d[...], hid[...], 1, 1)
        part = dot(at[: nodes + EDGE], dpre[m], 1, 1)
        contrib[m * nodes : (m + 1) * nodes, :] = part[:nodes].astype(bf16)
        total = total + jnp.where(row == variables, part[nodes : nodes + 1], 0.0)
    for i in range(PAD // 8):
        for j in range(WIDE // 128):
            heads[i, j] = total[i * 8 : (i + 1) * 8, j * 128 : (j + 1) * 128]


def backward(who, dpred, w_out, slope, hid, at, loss):
    width, points = slope[0].shape
    nodes = at.shape[0] - DEEP
    count = width // WIDE // 2

    def fixed(a):
        return pl.BlockSpec(a.shape, lambda y, w: (0,) * a.ndim)

    rows = pl.BlockSpec((WIDE, points), lambda y, w: (2 * y + w[0], 0))
    narrow = pl.BlockSpec((w_out.shape[0], WIDE), lambda y, w: (0, 2 * y + w[0]))
    return pl.pallas_call(
        backward_kernel,
        grid_spec=pltpu.PrefetchScalarGridSpec(
            num_scalar_prefetch=1,
            grid=(count,),
            in_specs=[fixed(dpred[0]), fixed(dpred[1]), narrow, rows, rows, rows, rows, fixed(at), fixed(loss)],
            out_specs=[
                pl.BlockSpec((None, 2 * nodes, WIDE), lambda y, w: (y, 0, 0)),
                pl.BlockSpec((None, PAD // 8, WIDE // 128, 8, 128), lambda y, w: (y, 0, 0, 0, 0)),
            ],
            scratch_shapes=[pltpu.VMEM((2, WIDE, points), bf16)],
        ),
        out_shape=[
            pltpu.VMEM((count, 2 * nodes, WIDE), bf16),
            pltpu.VMEM((count, PAD // 8, WIDE // 128, 8, 128), f32),
        ],
        compiler_params=params(("arbitrary",), 28),
        name="backward",
    )(who, *map(parked, dpred), parked(w_out), *map(parked, slope), *map(parked, hid), parked(at), loss)


def outer_kernel(lat_own, lat_other, c_own, c_other, h_own, h_other, out):
    regions, rows, _ = out.shape[1:]
    share = rows - 8
    for y in range(c_own.shape[0]):
        part = (dot(lat_own[...], c_own[y]) + dot(lat_other[...], c_other[y])).astype(bf16)
        for r in range(regions):
            out[y, r, :share] = part[r * share : (r + 1) * share]
            piece = (h_own[y, r] + h_other[y, r]).astype(bf16)
            out[y, r, share:] = jnp.concatenate([piece, jnp.zeros_like(piece)], axis=1)


def outer(lat_own, lat_other, c_own, c_other, h_own, h_other, regions):
    inputs, nodes = lat_own.shape
    halves, _, quarter = c_own.shape
    share = inputs // regions
    here = WIDE // share
    lat = pl.BlockSpec((WIDE, nodes), lambda i: (i, 0))
    piece = pl.BlockSpec((halves, here, 8, 128), lambda i: (0, i, 0, 0))
    return pl.pallas_call(
        outer_kernel,
        grid=(inputs // WIDE,),
        in_specs=[lat, lat, whole(c_own), whole(c_own), piece, piece],
        out_specs=pl.BlockSpec((halves, here, share + 8, quarter), lambda i: (0, i, 0, 0)),
        out_shape=pltpu.VMEM((halves, regions, share + 8, quarter), bf16),
        compiler_params=params(("arbitrary",), 16),
        name="outer",
    )(parked(lat_own), lat_other, parked(c_own), c_other, parked(h_own), h_other)


def finish_kernel(where, pieces, grad_out, grad_bias, loss):
    variables, _ = grad_out.shape
    per_row = WIDE // 128
    for at in range(pieces.shape[0]):
        ylo, core, place = at // 64, at // 32 % 2, at % 32
        i, j = place // per_row, place % per_row
        left, top = (2 * ylo + core) * WIDE + j * 128, i * 8
        rows = max(0, min(8, variables - top))
        if rows:
            grad_out[top : top + rows, left : left + 128] = pieces[at, :rows]
        line = variables - top
        if 0 <= line < 7:
            grad_bias[:, left : left + 128] = pieces[at, line : line + 1]
            if left == 0:
                values = pieces[at, line + 1 : line + 2]
                spot = lax.broadcasted_iota(jnp.int32, values.shape, 1)
                loss[...] = jnp.sum(jnp.where(spot == where[0], values, 0.0), axis=1, keepdims=True)


def finish(where, pieces, variables, width):
    return pl.pallas_call(
        finish_kernel,
        in_specs=[pl.BlockSpec(memory_space=pltpu.SMEM), pl.BlockSpec(memory_space=pltpu.VMEM)],
        out_shape=[
            jax.ShapeDtypeStruct((variables, width), f32),
            jax.ShapeDtypeStruct((1, width), f32),
            jax.ShapeDtypeStruct((1, 1), f32),
        ],
        compiler_params=pltpu.CompilerParams(vmem_limit_bytes=8 << 20),
        name="finish",
    )(where, pieces)


def local(latent, w_node, bias, w_out, edge_src, edge_weight, target, area):
    members, nodes, width = latent.shape
    variables = target.shape[0]
    regions = lax.axis_size(REGION)
    count = members * lax.axis_size(MEMBER)
    ahead = [(i, (i + 1) % regions) for i in range(regions)]
    behind = [(t, s) for s, t in ahead]
    swap = [(0, 1), (1, 0)]
    core = lax.axis_index("core")
    where = lax.axis_index(REGION)

    mine = [latent[m] for m in range(members)]

    low, high = [], []
    for m in range(members):
        low.append(lax.ppermute(mine[m], REGION, ahead))
        high.append(lax.ppermute(mine[m], REGION, behind))
    at = prep(edge_src.T, edge_weight.T, 3 * nodes)
    bias_row = bias[None, :]

    hid, pre, err, near, far, beside = [], [], [], [], [], []
    for m in range(members):
        h, s, e = forward(low[m], mine[m], high[m], w_node, at, bias_row, w_out, target)
        hid.append(h)
        pre.append(s)
        err.append(e)
        over = lax.ppermute((e * 0.125).astype(f16), "ylo", swap)
        near.append(lax.ppermute(e, "core", swap))
        far.append(over.astype(f32) * 8.0)
        beside.append(lax.ppermute(over, "core", swap).astype(f32) * 8.0)

    first, err[1] = lax.optimization_barrier((mine[0], err[1]))
    lat_t = turn((low[0], first, high[0], low[1], mine[1], high[1]))
    lat_t_other = lax.ppermute(lat_t, "core", swap)
    slope = slopes(pre)

    area_row = area[None, :]
    p_0, p_1, loss = crps_near(err, near + [far[0], beside[0]], area_row, count)
    d_0, d_1, loss = crps_far(err, [far[1], beside[1]], (p_0, p_1), area_row, loss, count)

    spot = where[None].astype(jnp.int32)
    every = lax.axis_size(EVERY)

    def back(side):
        who = jnp.stack([side, where]).astype(jnp.int32)
        return backward(who, (d_0, d_1), w_out, slope, hid, at, loss)

    given, heads_given = back(1 - core)
    taken = lax.ppermute(given, "core", swap)
    heads_taken = lax.ppermute(heads_given, "core", swap)
    kept, heads_kept = back(core)
    tiles = (2, regions, 8, 128)
    part = outer(lat_t, lat_t_other, kept, taken, heads_kept.reshape(tiles), heads_taken.reshape(tiles), regions)
    chips = lax.axis_size(CHIPS)
    share = width // regions
    shares = lax.all_to_all(part.reshape(chips, share + 8, width // 4), CHIPS, split_axis=0, concat_axis=0, tiled=True)
    summed = shares.astype(f32).sum(axis=0)
    table = lax.all_to_all(
        jnp.broadcast_to(summed[share:, :128], (every, 8, 128)), EVERY, split_axis=0, concat_axis=0, tiled=True
    )
    grad_node = lax.all_gather(summed[:share], MEMBER, axis=1, tiled=True)
    grad_out, grad_bias, loss_here = finish(spot, table, variables, width)
    grad_bias = grad_bias.reshape(width)
    loss_here = loss_here.reshape(1)
    return grad_node, grad_out, grad_bias, loss_here


def solution(mesh):
    finer = Mesh(mesh.devices.reshape(2, 2, 4, 2, 4), EVERY)
    in_specs = (
        P(MEMBER, REGION, None),
        P(),
        P(),
        P(),
        P(REGION, None),
        P(REGION, None),
        P(None, REGION),
        P(REGION),
    )
    out_specs = (P(REGION, None), P(), P(), P(REGION))

    return jax.shard_map(local, mesh=finer, in_specs=in_specs, out_specs=out_specs, check_vma=False)
```

```python
import jax
import jax.numpy as jnp
from jax import lax
from jax.experimental import pallas as pl
from jax.experimental.pallas import tpu as pltpu
from jax.sharding import Mesh
from jax.sharding import PartitionSpec as P


REGION = ("z", "yhi", "x")
MEMBER = ("ylo", "core")
CHIPS = ("ylo", "z", "yhi", "x")
EVERY = ("ylo", "core", "z", "yhi", "x")

SMOOTH_SQ = 0.01
C0 = 0.7978845608028654
C1 = 0.044715
WIDE = 256
PAD = 128
bf16 = jnp.bfloat16
f32 = jnp.float32
f16 = jnp.float16
EDGE = 16
DEEP = 128
SPLIT = 3


def dot(a, b, ca=1, cb=0):
    return lax.dot_general(a, b, (((ca,), (cb,)), ((), ())), preferred_element_type=f32)


def params(semantics, mib):
    return pltpu.CompilerParams(dimension_semantics=semantics, vmem_limit_bytes=mib << 20)


def parked(a):
    return pltpu.with_memory_space_constraint(a, pltpu.VMEM)


def whole(a):
    return pl.BlockSpec(a.shape, lambda *i: (0,) * a.ndim)


def prep_kernel(src, weight, at):
    nodes, wide = at.shape[0] - DEEP, at.shape[1]
    place = lax.broadcasted_iota(jnp.int32, (nodes, wide), 0)
    total = jnp.zeros((nodes, wide), f32)
    for k in range(src.shape[0]):
        total = total + jnp.where(src[k : k + 1, :] == place, weight[k : k + 1, :], 0.0)
    at[:nodes, :] = total.astype(bf16)
    first = lax.broadcasted_iota(jnp.int32, (DEEP, wide), 0) < SPLIT
    at[nodes:, :] = jnp.where(first, 1.0, 0.0).astype(bf16)


def prep(src, weight, nodes):
    fan, points = src.shape
    row = pl.BlockSpec((fan, WIDE), lambda i: (0, i))
    return pl.pallas_call(
        prep_kernel,
        grid=(points // WIDE,),
        in_specs=[row, row],
        out_specs=pl.BlockSpec((nodes + DEEP, WIDE), lambda i: (0, i)),
        out_shape=pltpu.VMEM((nodes + DEEP, points), bf16),
        compiler_params=params(("arbitrary",), 8),
        name="prep",
    )(src, weight)


def turn_kernel(*refs):
    blocks, out = refs[:-1], refs[-1]
    for b, block in enumerate(blocks):
        nodes = block.shape[0]
        out[:, b * nodes : (b + 1) * nodes] = block[...].T


def turn(blocks):
    nodes, width = blocks[0].shape
    return pl.pallas_call(
        turn_kernel,
        grid=(width // WIDE,),
        in_specs=[pl.BlockSpec((nodes, WIDE), lambda i: (0, i))] * len(blocks),
        out_specs=pl.BlockSpec((WIDE, nodes * len(blocks)), lambda i: (i, 0)),
        out_shape=pltpu.VMEM((width, nodes * len(blocks)), bf16),
        compiler_params=params(("arbitrary",), 8),
        name="turn",
    )(*blocks)


def forward_kernel(low, own, high, w_node, at, bias, w_out, target, hid, pre, err, proj):
    nodes = 3 * low.shape[0]

    stacked = jnp.concatenate([low[...], own[...], high[...]], axis=0)
    proj[:, :nodes] = dot(stacked, w_node[...]).astype(bf16).T
    row = lax.broadcasted_iota(jnp.int32, (DEEP, proj.shape[0]), 0)
    block, rest = jnp.zeros(row.shape, f32), bias[...]
    for k in range(SPLIT):
        part = rest.astype(bf16).astype(f32)
        block = jnp.where(row == k, part, block)
        rest = rest - part
    proj[:, nodes:] = block.T.astype(bf16)

    for g in range(target.shape[1] // 256):
        cols = slice(g * 256, (g + 1) * 256)
        for r in range(proj.shape[0] // 256):
            rows = slice(r * 256, (r + 1) * 256)
            x = dot(proj[rows, :], at[:, cols])
            pre[rows, cols] = x.astype(bf16)
            u = 0.5 + 0.5 * jnp.tanh(x * (C0 + (C0 * C1) * (x * x)))
            hid[rows, cols] = (x * u).astype(bf16)
    err[...] = dot(w_out[...], hid[...]) - target[...]


def forward(low, own, high, w_node, at, bias, w_out, target):
    width = w_node.shape[1]
    points = at.shape[1]
    variables = target.shape[0]
    vm = pl.BlockSpec(memory_space=pltpu.VMEM)
    return pl.pallas_call(
        forward_kernel,
        in_specs=[vm] * 8,
        out_specs=[vm] * 3,
        out_shape=[
            pltpu.VMEM((width, points), bf16),
            pltpu.VMEM((width, points), bf16),
            pltpu.VMEM((variables, points), f32),
        ],
        scratch_shapes=[pltpu.VMEM((width, at.shape[0]), bf16)],
        compiler_params=pltpu.CompilerParams(vmem_limit_bytes=24 << 20),
        name="forward",
    )(parked(low), parked(own), parked(high), parked(w_node), parked(at), parked(bias), parked(w_out), parked(target))


def slope_kernel(pre, out):
    for g in range(pre.shape[1] // WIDE):
        cols = slice(g * WIDE, (g + 1) * WIDE)
        x = pre[:, cols].astype(f32)
        sq = x * x
        u = 0.5 + 0.5 * jnp.tanh(x * (C0 + (C0 * C1) * sq))
        out[:, cols] = (u + (x * u) * (1.0 - u) * (2.0 * C0 + (6.0 * C0 * C1) * sq)).astype(bf16)


def slopes(pre):
    width, points = pre.shape
    rows = pl.BlockSpec((128, points), lambda i: (i, 0))
    return pl.pallas_call(
        slope_kernel,
        grid=(width // 128,),
        in_specs=[rows],
        out_specs=rows,
        out_shape=pltpu.VMEM((width, points), bf16),
        compiler_params=params(("arbitrary",), 8),
        name="slope",
    )(parked(pre))


def apart(d):
    q = d * d + SMOOTH_SQ
    r = lax.rsqrt(q)
    return q * r, d * r


def near_kernel(count, scale, own_0, own_1, *rest):
    others, (area, p_0, p_1, loss) = rest[:-4], rest[-4:]
    pairs = count * (count - 1)

    @pl.when(pl.program_id(0) == 0)
    def _():
        loss[...] = jnp.zeros_like(loss)

    for c in range(own_0.shape[1] // PAD):
        at = slice(c * PAD, (c + 1) * PAD)
        a, b = own_0[:, at], own_1[:, at]
        own_a, slope_a = apart(a)
        own_b, slope_b = apart(b)
        dist, t = apart(a - b)
        dist = 2.0 * dist
        sum_a, sum_b = t, -t
        for other in others:
            o = other[:, at]
            s, t = apart(a - o)
            dist = dist + s
            sum_a = sum_a + t
            s, t = apart(b - o)
            dist = dist + s
            sum_b = sum_b + t
        value = (own_a + own_b) * (1.0 / count) - dist * (0.5 / pairs)
        loss[...] += jnp.sum(value, axis=0, keepdims=True) * area[:, at] * (1.0 / scale)
        p_0[:, at] = slope_a * (1.0 / count) - sum_a * (1.0 / pairs)
        p_1[:, at] = slope_b * (1.0 / count) - sum_b * (1.0 / pairs)


def far_kernel(count, scale, own_0, own_1, *rest):
    others, (p_0, p_1, area, before, d_0, d_1, loss) = rest[:-7], rest[-7:]
    variables = own_0.shape[0]
    pairs = count * (count - 1)

    @pl.when(pl.program_id(0) == 0)
    def _():
        loss[...] = before[...]

    for c in range(own_0.shape[1] // PAD):
        at = slice(c * PAD, (c + 1) * PAD)
        a, b = own_0[:, at], own_1[:, at]
        dist, sum_a, sum_b = 0.0, 0.0, 0.0
        for other in others:
            o = other[:, at]
            s, t = apart(a - o)
            dist = dist + s
            sum_a = sum_a + t
            s, t = apart(b - o)
            dist = dist + s
            sum_b = sum_b + t
        where = area[:, at]
        loss[...] -= jnp.sum(dist, axis=0, keepdims=True) * where * (0.5 / pairs / scale)
        fold = where * (1.0 / variables)
        for ref, p, t in ((d_0, p_0, sum_a), (d_1, p_1, sum_b)):
            ref[:variables, at] = ((p[:, at] - t * (1.0 / pairs)) * fold).astype(bf16)
            ref[variables:, at] = jnp.zeros((PAD - variables, PAD), bf16)


def crps_near(own, others, area, count):
    variables, points = own[0].shape
    wide = 512
    field = pl.BlockSpec((variables, wide), lambda i: (0, i))
    row = pl.BlockSpec((1, wide), lambda i: (0, i))
    return pl.pallas_call(
        lambda *refs: near_kernel(count, variables * points, *refs),
        grid=(points // wide,),
        in_specs=[field] * (2 + len(others)) + [row],
        out_specs=[field, field, pl.BlockSpec((1, PAD), lambda i: (0, 0))],
        out_shape=[pltpu.VMEM((variables, points), f32)] * 2 + [jax.ShapeDtypeStruct((1, PAD), f32)],
        compiler_params=params(("arbitrary",), 16),
        name="crps_near",
    )(*map(parked, own), *others, area)


def crps_far(own, others, partial, area, before, count):
    variables, points = own[0].shape
    wide = 512
    field = pl.BlockSpec((variables, wide), lambda i: (0, i))
    padded = pl.BlockSpec((PAD, wide), lambda i: (0, i))
    row = pl.BlockSpec((1, wide), lambda i: (0, i))
    one = pl.BlockSpec((1, PAD), lambda i: (0, 0))
    return pl.pallas_call(
        lambda *refs: far_kernel(count, variables * points, *refs),
        grid=(points // wide,),
        in_specs=[field] * (4 + len(others)) + [row, one],
        out_specs=[padded, padded, one],
        out_shape=[pltpu.VMEM((PAD, points), bf16)] * 2 + [jax.ShapeDtypeStruct((1, PAD), f32)],
        compiler_params=params(("arbitrary",), 16),
        name="crps_far",
    )(*map(parked, own), *others, *map(parked, partial), area, before)


def backward_kernel(who, d_0, d_1, w_out, s_0, s_1, h_0, h_1, at, loss, contrib, heads, dpre):
    nodes = at.shape[0] - DEEP
    variables = w_out.shape[0]
    shape = (PAD, WIDE)
    row = lax.broadcasted_iota(jnp.int32, shape, 0)
    lane = lax.broadcasted_iota(jnp.int32, shape, 1)
    for y in range(contrib.shape[0]):
        first = pl.multiple_of((2 * y + who[0]) * WIDE, WIDE)
        rows = pl.ds(first, WIDE)
        total = jnp.where((row == variables + 1) & (lane + first == who[1]), jnp.sum(loss[...]), 0.0)
        turned = w_out[:, rows].T
        for m, (d, slope, hid) in enumerate(((d_0, s_0, h_0), (d_1, s_1, h_1))):
            for g in range(d.shape[1] // WIDE):
                cut = slice(g * WIDE, (g + 1) * WIDE)
                part = dot(turned, d[:variables, cut]) * slope[rows, cut].astype(f32)
                dpre[y, m, :, cut] = part.astype(bf16)
            total = total + dot(d[...], hid[rows, :], 1, 1)
            part = dot(at[: nodes + EDGE], dpre[y, m], 1, 1)
            contrib[y, m * nodes : (m + 1) * nodes, :] = part[:nodes].astype(bf16)
            total = total + jnp.where(row == variables, part[nodes : nodes + 1], 0.0)
        for i in range(PAD // 8):
            for j in range(WIDE // 128):
                heads[y, i, j] = total[i * 8 : (i + 1) * 8, j * 128 : (j + 1) * 128]


def backward(who, dpred, w_out, slope, hid, at, loss):
    width, points = slope[0].shape
    nodes = at.shape[0] - DEEP
    count = width // WIDE // 2
    vm = pl.BlockSpec(memory_space=pltpu.VMEM)
    return pl.pallas_call(
        backward_kernel,
        in_specs=[pl.BlockSpec(memory_space=pltpu.SMEM)] + [vm] * 9,
        out_specs=[vm, vm],
        out_shape=[
            pltpu.VMEM((count, 2 * nodes, WIDE), bf16),
            pltpu.VMEM((count, PAD // 8, WIDE // 128, 8, 128), f32),
        ],
        scratch_shapes=[pltpu.VMEM((count, 2, WIDE, points), bf16)],
        compiler_params=pltpu.CompilerParams(vmem_limit_bytes=24 << 20),
        name="backward",
    )(who, *map(parked, dpred), parked(w_out), *map(parked, slope), *map(parked, hid), parked(at), parked(loss))


def outer_kernel(lat_own, lat_other, c_own, c_other, h_own, h_other, out):
    regions = out.shape[1]
    share = lat_own.shape[0] // regions
    for y in range(c_own.shape[0]):
        part = (dot(lat_own[...], c_own[y]) + dot(lat_other[...], c_other[y])).astype(bf16)
        for r in range(regions):
            for j in range(part.shape[1] // 128):
                out[y, r, j * share : (j + 1) * share] = part[r * share : (r + 1) * share, j * 128 : (j + 1) * 128]
            out[y, r, 2 * share :] = (h_own[y, r] + h_other[y, r]).astype(bf16)


def outer(lat_own, lat_other, c_own, c_other, h_own, h_other, regions):
    inputs, nodes = lat_own.shape
    halves, _, _ = c_own.shape
    share = inputs // regions
    here = WIDE // share
    lat = pl.BlockSpec((WIDE, nodes), lambda i: (i, 0))
    piece = pl.BlockSpec((halves, here, 8, 128), lambda i: (0, i, 0, 0))
    return pl.pallas_call(
        outer_kernel,
        grid=(inputs // WIDE,),
        in_specs=[lat, lat, whole(c_own), whole(c_own), piece, piece],
        out_specs=pl.BlockSpec((halves, here, 2 * share + 8, 128), lambda i: (0, i, 0, 0)),
        out_shape=pltpu.VMEM((halves, regions, 2 * share + 8, 128), bf16),
        compiler_params=params(("arbitrary",), 16),
        name="outer",
    )(parked(lat_own), lat_other, parked(c_own), c_other, parked(h_own), h_other)


def finish_kernel(where, pieces, grad_out, grad_bias, loss):
    variables, _ = grad_out.shape
    per_row = WIDE // 128
    for at in range(pieces.shape[0]):
        ylo, core, place = at // 64, at // 32 % 2, at % 32
        i, j = place // per_row, place % per_row
        left, top = (2 * ylo + core) * WIDE + j * 128, i * 8
        rows = max(0, min(8, variables - top))
        if rows:
            grad_out[top : top + rows, left : left + 128] = pieces[at, :rows]
        line = variables - top
        if 0 <= line < 7:
            grad_bias[:, left : left + 128] = pieces[at, line : line + 1]
            if left == 0:
                values = pieces[at, line + 1 : line + 2]
                spot = lax.broadcasted_iota(jnp.int32, values.shape, 1)
                loss[...] = jnp.sum(jnp.where(spot == where[0], values, 0.0), axis=1, keepdims=True)


def finish(where, pieces, variables, width):
    return pl.pallas_call(
        finish_kernel,
        in_specs=[pl.BlockSpec(memory_space=pltpu.SMEM), pl.BlockSpec(memory_space=pltpu.VMEM)],
        out_shape=[
            jax.ShapeDtypeStruct((variables, width), f32),
            jax.ShapeDtypeStruct((1, width), f32),
            jax.ShapeDtypeStruct((1, 1), f32),
        ],
        compiler_params=pltpu.CompilerParams(vmem_limit_bytes=8 << 20),
        name="finish",
    )(where, pieces)


def local(latent, w_node, bias, w_out, edge_src, edge_weight, target, area):
    members, nodes, width = latent.shape
    variables = target.shape[0]
    regions = lax.axis_size(REGION)
    count = members * lax.axis_size(MEMBER)
    ahead = [(i, (i + 1) % regions) for i in range(regions)]
    behind = [(t, s) for s, t in ahead]
    swap = [(0, 1), (1, 0)]
    core = lax.axis_index("core")
    where = lax.axis_index(REGION)

    mine = [latent[m] for m in range(members)]

    low, high = [], []
    for m in range(members):
        low.append(lax.ppermute(mine[m], REGION, ahead))
        high.append(lax.ppermute(mine[m], REGION, behind))
    at = prep(edge_src.T, edge_weight.T, 3 * nodes)
    bias_row = bias[None, :]

    hid, slope, err, near, far, beside = [], [], [], [], [], []
    for m in range(members):
        h, s, e = forward(low[m], mine[m], high[m], w_node, at, bias_row, w_out, target)
        hid.append(h)
        slope.append(slopes(s))
        err.append(e)
        over = lax.ppermute((e * 0.125).astype(f16), "ylo", swap)
        near.append(lax.ppermute(e, "core", swap))
        far.append(over.astype(f32) * 8.0)
        beside.append(lax.ppermute(over, "core", swap).astype(f32) * 8.0)

    first, err[1] = lax.optimization_barrier((mine[0], err[1]))
    lat_t = turn((low[0], first, high[0], low[1], mine[1], high[1]))
    lat_t_other = lax.ppermute(lat_t, "core", swap)

    area_row = area[None, :]
    p_0, p_1, loss = crps_near(err, near + [far[0], beside[0]], area_row, count)
    d_0, d_1, loss = crps_far(err, [far[1], beside[1]], (p_0, p_1), area_row, loss, count)

    spot = where[None].astype(jnp.int32)
    every = lax.axis_size(EVERY)

    def back(side):
        who = jnp.stack([side, where]).astype(jnp.int32)
        return backward(who, (d_0, d_1), w_out, slope, hid, at, loss)

    given, heads_given = back(1 - core)
    taken = lax.ppermute(given, "core", swap)
    heads_taken = lax.ppermute(heads_given, "core", swap)
    kept, heads_kept = back(core)
    tiles = (2, regions, 8, 128)
    part = outer(lat_t, lat_t_other, kept, taken, heads_kept.reshape(tiles), heads_taken.reshape(tiles), regions)
    chips = lax.axis_size(CHIPS)
    share = width // regions
    shares = lax.all_to_all(
        part.reshape(chips, 2 * share + 8, 128), CHIPS, split_axis=0, concat_axis=0, tiled=True
    )
    summed = shares.astype(f32).sum(axis=0)
    table = lax.all_to_all(
        jnp.broadcast_to(summed[2 * share :], (every, 8, 128)), EVERY, split_axis=0, concat_axis=0, tiled=True
    )
    own = jnp.concatenate([summed[:share], summed[share : 2 * share]], axis=1)
    grad_node = lax.all_gather(own, MEMBER, axis=1, tiled=True)
    grad_out, grad_bias, loss_here = finish(spot, table, variables, width)
    grad_bias = grad_bias.reshape(width)
    loss_here = loss_here.reshape(1)
    return grad_node, grad_out, grad_bias, loss_here


def solution(mesh):
    finer = Mesh(mesh.devices.reshape(2, 2, 4, 2, 4), EVERY)
    in_specs = (
        P(MEMBER, REGION, None),
        P(),
        P(),
        P(),
        P(REGION, None),
        P(REGION, None),
        P(None, REGION),
        P(REGION),
    )
    out_specs = (P(REGION, None), P(), P(), P(REGION))

    return jax.shard_map(local, mesh=finer, in_specs=in_specs, out_specs=out_specs, check_vma=False)
```

```python
import jax
import jax.numpy as jnp
from jax import lax
from jax.experimental import pallas as pl
from jax.experimental.pallas import tpu as pltpu
from jax.sharding import Mesh
from jax.sharding import PartitionSpec as P


REGION = ("z", "yhi", "x")
MEMBER = ("ylo", "core")
CHIPS = ("ylo", "z", "yhi", "x")
EVERY = ("ylo", "core", "z", "yhi", "x")

SMOOTH_SQ = 0.01
C0 = 0.7978845608028654
C1 = 0.044715
WIDE = 256
PAD = 128
bf16 = jnp.bfloat16
f32 = jnp.float32
f16 = jnp.float16
EDGE = 16
DEEP = 128
SPLIT = 3


def dot(a, b, ca=1, cb=0):
    return lax.dot_general(a, b, (((ca,), (cb,)), ((), ())), preferred_element_type=f32)


def params(semantics, mib):
    return pltpu.CompilerParams(dimension_semantics=semantics, vmem_limit_bytes=mib << 20)


def parked(a):
    return pltpu.with_memory_space_constraint(a, pltpu.VMEM)


def whole(a):
    return pl.BlockSpec(a.shape, lambda *i: (0,) * a.ndim)


def prep_kernel(src, weight, bias, *rest):
    at, lift = rest[-2:]
    nodes, wide = at.shape[0] - DEEP, at.shape[1]
    place = lax.broadcasted_iota(jnp.int32, (nodes, wide), 0)
    total = jnp.zeros((nodes, wide), f32)
    for k in range(src.shape[0]):
        total = total + jnp.where(src[k : k + 1, :] == place, weight[k : k + 1, :], 0.0)
    at[:nodes, :] = total.astype(bf16)
    first = lax.broadcasted_iota(jnp.int32, (DEEP, wide), 0) < SPLIT
    at[nodes:, :] = jnp.where(first, 1.0, 0.0).astype(bf16)
    row = lax.broadcasted_iota(jnp.int32, lift.shape, 0)
    block, rest = jnp.zeros(lift.shape, f32), bias[...]
    for k in range(SPLIT):
        part = rest.astype(bf16).astype(f32)
        block = jnp.where(row == k, part, block)
        rest = rest - part
    lift[...] = block.astype(bf16)


def prep(src, weight, bias, nodes, later):
    fan, points = src.shape
    width = bias.shape[1]
    steps = points // WIDE
    row = pl.BlockSpec((fan, WIDE), lambda i: (0, i))
    return pl.pallas_call(
        prep_kernel,
        grid=(steps,),
        in_specs=[row, row, pl.BlockSpec((1, width // steps), lambda i: (0, i))] + [pl.BlockSpec(memory_space=pltpu.VMEM)] * len(later),
        out_specs=[
            pl.BlockSpec((nodes + DEEP, WIDE), lambda i: (0, i)),
            pl.BlockSpec((DEEP, width // steps), lambda i: (0, i)),
        ],
        out_shape=[pltpu.VMEM((nodes + DEEP, points), bf16), pltpu.VMEM((DEEP, width), bf16)],
        compiler_params=params(("arbitrary",), 8),
        name="prep",
    )(src, weight, bias, *map(parked, later))


def turn_kernel(*refs):
    blocks, out = refs[:-1], refs[-1]
    for b, block in enumerate(blocks):
        nodes = block.shape[0]
        out[:, b * nodes : (b + 1) * nodes] = block[...].T


def turn(blocks):
    nodes, width = blocks[0].shape
    return pl.pallas_call(
        turn_kernel,
        grid=(width // WIDE,),
        in_specs=[pl.BlockSpec((nodes, WIDE), lambda i: (0, i))] * len(blocks),
        out_specs=pl.BlockSpec((WIDE, nodes * len(blocks)), lambda i: (i, 0)),
        out_shape=pltpu.VMEM((width, nodes * len(blocks)), bf16),
        compiler_params=params(("arbitrary",), 8),
        name="turn",
    )(*blocks)


def forward_kernel(low, own, high, w_node, at, bias, w_out, target, hid, pre, err, proj):
    nodes = 3 * low.shape[0]

    stacked = jnp.concatenate([low[...], own[...], high[...]], axis=0)
    proj[:, :nodes] = dot(stacked, w_node[...]).astype(bf16).T
    proj[:, nodes:] = bias[...].T

    for g in range(target.shape[1] // 256):
        cols = slice(g * 256, (g + 1) * 256)
        for r in range(proj.shape[0] // 256):
            rows = slice(r * 256, (r + 1) * 256)
            x = dot(proj[rows, :], at[:, cols])
            pre[rows, cols] = x.astype(bf16)
            u = 0.5 + 0.5 * jnp.tanh(x * (C0 + (C0 * C1) * (x * x)))
            hid[rows, cols] = (x * u).astype(bf16)
    err[...] = dot(w_out[...], hid[...]) - target[...]


def forward(low, own, high, w_node, at, bias, w_out, target):
    width = w_node.shape[1]
    points = at.shape[1]
    variables = target.shape[0]
    vm = pl.BlockSpec(memory_space=pltpu.VMEM)
    return pl.pallas_call(
        forward_kernel,
        in_specs=[vm] * 8,
        out_specs=[vm] * 3,
        out_shape=[
            pltpu.VMEM((width, points), bf16),
            pltpu.VMEM((width, points), bf16),
            pltpu.VMEM((variables, points), f32),
        ],
        scratch_shapes=[pltpu.VMEM((width, at.shape[0]), bf16)],
        compiler_params=pltpu.CompilerParams(vmem_limit_bytes=24 << 20),
        name="forward",
    )(parked(low), parked(own), parked(high), parked(w_node), parked(at), parked(bias), parked(w_out), parked(target))


def slope_kernel(pre, out):
    for g in range(pre.shape[1] // WIDE):
        cols = slice(g * WIDE, (g + 1) * WIDE)
        x = pre[:, cols].astype(f32)
        sq = x * x
        u = 0.5 + 0.5 * jnp.tanh(x * (C0 + (C0 * C1) * sq))
        out[:, cols] = (u + (x * u) * (1.0 - u) * (2.0 * C0 + (6.0 * C0 * C1) * sq)).astype(bf16)


def slopes(pre):
    width, points = pre.shape
    rows = pl.BlockSpec((128, points), lambda i: (i, 0))
    return pl.pallas_call(
        slope_kernel,
        grid=(width // 128,),
        in_specs=[rows],
        out_specs=rows,
        out_shape=pltpu.VMEM((width, points), bf16),
        compiler_params=params(("arbitrary",), 8),
        name="slope",
    )(parked(pre))


def apart(d):
    q = d * d + SMOOTH_SQ
    r = lax.rsqrt(q)
    return q * r, d * r


def near_kernel(count, scale, own_0, own_1, *rest):
    others, (area, p_0, p_1, loss) = rest[:-4], rest[-4:]
    pairs = count * (count - 1)

    @pl.when(pl.program_id(0) == 0)
    def _():
        loss[...] = jnp.zeros_like(loss)

    for c in range(own_0.shape[1] // PAD):
        at = slice(c * PAD, (c + 1) * PAD)
        a, b = own_0[:, at], own_1[:, at]
        own_a, slope_a = apart(a)
        own_b, slope_b = apart(b)
        dist, t = apart(a - b)
        dist = 2.0 * dist
        sum_a, sum_b = t, -t
        for other in others:
            o = other[:, at]
            s, t = apart(a - o)
            dist = dist + s
            sum_a = sum_a + t
            s, t = apart(b - o)
            dist = dist + s
            sum_b = sum_b + t
        value = (own_a + own_b) * (1.0 / count) - dist * (0.5 / pairs)
        loss[...] += jnp.sum(value, axis=0, keepdims=True) * area[:, at] * (1.0 / scale)
        p_0[:, at] = slope_a * (1.0 / count) - sum_a * (1.0 / pairs)
        p_1[:, at] = slope_b * (1.0 / count) - sum_b * (1.0 / pairs)


def far_kernel(count, scale, own_0, own_1, *rest):
    others, (p_0, p_1, area, before, d_0, d_1, loss) = rest[:-7], rest[-7:]
    variables = own_0.shape[0]
    pairs = count * (count - 1)

    @pl.when(pl.program_id(0) == 0)
    def _():
        loss[...] = before[...]

    for c in range(own_0.shape[1] // PAD):
        at = slice(c * PAD, (c + 1) * PAD)
        a, b = own_0[:, at], own_1[:, at]
        dist, sum_a, sum_b = 0.0, 0.0, 0.0
        for other in others:
            o = other[:, at]
            s, t = apart(a - o)
            dist = dist + s
            sum_a = sum_a + t
            s, t = apart(b - o)
            dist = dist + s
            sum_b = sum_b + t
        where = area[:, at]
        loss[...] -= jnp.sum(dist, axis=0, keepdims=True) * where * (0.5 / pairs / scale)
        fold = where * (1.0 / variables)
        for ref, p, t in ((d_0, p_0, sum_a), (d_1, p_1, sum_b)):
            ref[:variables, at] = ((p[:, at] - t * (1.0 / pairs)) * fold).astype(bf16)
            ref[variables:, at] = jnp.zeros((PAD - variables, PAD), bf16)


def crps_near(own, others, area, count):
    variables, points = own[0].shape
    wide = 512
    field = pl.BlockSpec((variables, wide), lambda i: (0, i))
    row = pl.BlockSpec((1, wide), lambda i: (0, i))
    return pl.pallas_call(
        lambda *refs: near_kernel(count, variables * points, *refs),
        grid=(points // wide,),
        in_specs=[field] * (2 + len(others)) + [row],
        out_specs=[field, field, pl.BlockSpec((1, PAD), lambda i: (0, 0))],
        out_shape=[pltpu.VMEM((variables, points), f32)] * 2 + [jax.ShapeDtypeStruct((1, PAD), f32)],
        compiler_params=params(("arbitrary",), 16),
        name="crps_near",
    )(*map(parked, own), *others, area)


def crps_far(own, others, partial, area, before, count):
    variables, points = own[0].shape
    wide = 512
    field = pl.BlockSpec((variables, wide), lambda i: (0, i))
    padded = pl.BlockSpec((PAD, wide), lambda i: (0, i))
    row = pl.BlockSpec((1, wide), lambda i: (0, i))
    one = pl.BlockSpec((1, PAD), lambda i: (0, 0))
    return pl.pallas_call(
        lambda *refs: far_kernel(count, variables * points, *refs),
        grid=(points // wide,),
        in_specs=[field] * (4 + len(others)) + [row, one],
        out_specs=[padded, padded, one],
        out_shape=[pltpu.VMEM((PAD, points), bf16)] * 2 + [jax.ShapeDtypeStruct((1, PAD), f32)],
        compiler_params=params(("arbitrary",), 16),
        name="crps_far",
    )(*map(parked, own), *others, *map(parked, partial), area, before)


def backward_kernel(who, d_0, d_1, w_out, s_0, s_1, h_0, h_1, at, loss, contrib, heads, dpre):
    nodes = at.shape[0] - DEEP
    variables = w_out.shape[0]
    shape = (PAD, WIDE)
    row = lax.broadcasted_iota(jnp.int32, shape, 0)
    lane = lax.broadcasted_iota(jnp.int32, shape, 1)
    for y in range(contrib.shape[0]):
        first = pl.multiple_of((2 * y + who[0]) * WIDE, WIDE)
        rows = pl.ds(first, WIDE)
        total = jnp.where((row == variables + 1) & (lane + first == who[1]), jnp.sum(loss[...]), 0.0)
        turned = w_out[:, rows].T
        for m, (d, slope, hid) in enumerate(((d_0, s_0, h_0), (d_1, s_1, h_1))):
            for g in range(d.shape[1] // WIDE):
                cut = slice(g * WIDE, (g + 1) * WIDE)
                part = dot(turned, d[:variables, cut]) * slope[rows, cut].astype(f32)
                dpre[y, m, :, cut] = part.astype(bf16)
            total = total + dot(d[...], hid[rows, :], 1, 1)
            part = dot(at[: nodes + EDGE], dpre[y, m], 1, 1)
            contrib[y, m * nodes : (m + 1) * nodes, :] = part[:nodes].astype(bf16)
            total = total + jnp.where(row == variables, part[nodes : nodes + 1], 0.0)
        for i in range(PAD // 8):
            for j in range(WIDE // 128):
                heads[y, i, j] = total[i * 8 : (i + 1) * 8, j * 128 : (j + 1) * 128]


def backward(who, dpred, w_out, slope, hid, at, loss):
    width, points = slope[0].shape
    nodes = at.shape[0] - DEEP
    count = width // WIDE // 2
    vm = pl.BlockSpec(memory_space=pltpu.VMEM)
    return pl.pallas_call(
        backward_kernel,
        in_specs=[pl.BlockSpec(memory_space=pltpu.SMEM)] + [vm] * 9,
        out_specs=[vm, vm],
        out_shape=[
            pltpu.VMEM((count, 2 * nodes, WIDE), bf16),
            pltpu.VMEM((count, PAD // 8, WIDE // 128, 8, 128), f32),
        ],
        scratch_shapes=[pltpu.VMEM((count, 2, WIDE, points), bf16)],
        compiler_params=pltpu.CompilerParams(vmem_limit_bytes=24 << 20),
        name="backward",
    )(who, *map(parked, dpred), parked(w_out), *map(parked, slope), *map(parked, hid), parked(at), parked(loss))


def outer_kernel(lat_own, lat_other, c_own, c_other, h_own, h_other, out):
    regions = out.shape[1]
    share = lat_own.shape[0] // regions
    for y in range(c_own.shape[0]):
        part = (dot(lat_own[...], c_own[y]) + dot(lat_other[...], c_other[y])).astype(bf16)
        for r in range(regions):
            for j in range(part.shape[1] // 128):
                out[y, r, j * share : (j + 1) * share] = part[r * share : (r + 1) * share, j * 128 : (j + 1) * 128]
            out[y, r, 2 * share :] = (h_own[y, r] + h_other[y, r]).astype(bf16)


def outer(lat_own, lat_other, c_own, c_other, h_own, h_other, regions):
    inputs, nodes = lat_own.shape
    halves, _, _ = c_own.shape
    share = inputs // regions
    here = WIDE // share
    lat = pl.BlockSpec((WIDE, nodes), lambda i: (i, 0))
    piece = pl.BlockSpec((halves, here, 8, 128), lambda i: (0, i, 0, 0))
    return pl.pallas_call(
        outer_kernel,
        grid=(inputs // WIDE,),
        in_specs=[lat, lat, whole(c_own), whole(c_own), piece, piece],
        out_specs=pl.BlockSpec((halves, here, 2 * share + 8, 128), lambda i: (0, i, 0, 0)),
        out_shape=pltpu.VMEM((halves, regions, 2 * share + 8, 128), bf16),
        compiler_params=params(("arbitrary",), 16),
        name="outer",
    )(parked(lat_own), lat_other, parked(c_own), c_other, parked(h_own), h_other)


def finish_kernel(where, pieces, grad_out, grad_bias, loss):
    variables, _ = grad_out.shape
    per_row = WIDE // 128
    for at in range(pieces.shape[0]):
        ylo, core, place = at // 64, at // 32 % 2, at % 32
        i, j = place // per_row, place % per_row
        left, top = (2 * ylo + core) * WIDE + j * 128, i * 8
        rows = max(0, min(8, variables - top))
        if rows:
            grad_out[top : top + rows, left : left + 128] = pieces[at, :rows]
        line = variables - top
        if 0 <= line < 7:
            grad_bias[:, left : left + 128] = pieces[at, line : line + 1]
            if left == 0:
                values = pieces[at, line + 1 : line + 2]
                spot = lax.broadcasted_iota(jnp.int32, values.shape, 1)
                loss[...] = jnp.sum(jnp.where(spot == where[0], values, 0.0), axis=1, keepdims=True)


def finish(where, pieces, variables, width):
    return pl.pallas_call(
        finish_kernel,
        in_specs=[pl.BlockSpec(memory_space=pltpu.SMEM), pl.BlockSpec(memory_space=pltpu.VMEM)],
        out_shape=[
            jax.ShapeDtypeStruct((variables, width), f32),
            jax.ShapeDtypeStruct((1, width), f32),
            jax.ShapeDtypeStruct((1, 1), f32),
        ],
        compiler_params=pltpu.CompilerParams(vmem_limit_bytes=8 << 20),
        name="finish",
    )(where, pieces)


def local(latent, w_node, bias, w_out, edge_src, edge_weight, target, area):
    members, nodes, width = latent.shape
    variables = target.shape[0]
    regions = lax.axis_size(REGION)
    count = members * lax.axis_size(MEMBER)
    ahead = [(i, (i + 1) % regions) for i in range(regions)]
    behind = [(t, s) for s, t in ahead]
    swap = [(0, 1), (1, 0)]
    core = lax.axis_index("core")
    where = lax.axis_index(REGION)

    mine = [latent[0]] + [lax.optimization_barrier(latent)[m] for m in range(1, members)]

    low, high = [], []
    for m in range(members):
        low.append(lax.ppermute(mine[m], REGION, ahead))
        high.append(lax.ppermute(mine[m], REGION, behind))
    at, lift = prep(edge_src.T, edge_weight.T, bias[None, :], 3 * nodes, (w_node, w_out, target))

    hid, slope, err, near, far, beside = [], [], [], [], [], []
    for m in range(members):
        h, s, e = forward(low[m], mine[m], high[m], w_node, at, lift, w_out, target)
        hid.append(h)
        slope.append(slopes(s))
        err.append(e)
        over = lax.ppermute((e * 0.125).astype(f16), "ylo", swap)
        near.append(lax.ppermute(e, "core", swap))
        far.append(over.astype(f32) * 8.0)
        beside.append(lax.ppermute(over, "core", swap).astype(f32) * 8.0)

    first, err[1] = lax.optimization_barrier((mine[0], err[1]))
    lat_t = turn((low[0], first, high[0], low[1], mine[1], high[1]))
    lat_t_other = lax.ppermute(lat_t, "core", swap)

    area_row = area[None, :]
    p_0, p_1, loss = crps_near(err, near + [far[0], beside[0]], area_row, count)
    d_0, d_1, loss = crps_far(err, [far[1], beside[1]], (p_0, p_1), area_row, loss, count)

    spot = where[None].astype(jnp.int32)
    every = lax.axis_size(EVERY)

    def back(side):
        who = jnp.stack([side, where]).astype(jnp.int32)
        return backward(who, (d_0, d_1), w_out, slope, hid, at, loss)

    given, heads_given = back(1 - core)
    taken = lax.ppermute(given, "core", swap)
    heads_taken = lax.ppermute(heads_given, "core", swap)
    kept, heads_kept = back(core)
    tiles = (2, regions, 8, 128)
    part = outer(lat_t, lat_t_other, kept, taken, heads_kept.reshape(tiles), heads_taken.reshape(tiles), regions)
    chips = lax.axis_size(CHIPS)
    share = width // regions
    shares = lax.all_to_all(
        part.reshape(chips, 2 * share + 8, 128), CHIPS, split_axis=0, concat_axis=0, tiled=True
    )
    summed = shares.astype(f32).sum(axis=0)
    table = lax.all_to_all(
        jnp.broadcast_to(summed[2 * share :], (every, 8, 128)), EVERY, split_axis=0, concat_axis=0, tiled=True
    )
    own = jnp.concatenate([summed[:share], summed[share : 2 * share]], axis=1)
    grad_node = lax.all_gather(own, MEMBER, axis=1, tiled=True)
    grad_out, grad_bias, loss_here = finish(spot, table, variables, width)
    grad_bias = grad_bias.reshape(width)
    loss_here = loss_here.reshape(1)
    return grad_node, grad_out, grad_bias, loss_here


def solution(mesh):
    finer = Mesh(mesh.devices.reshape(2, 2, 4, 2, 4), EVERY)
    in_specs = (
        P(MEMBER, REGION, None),
        P(),
        P(),
        P(),
        P(REGION, None),
        P(REGION, None),
        P(None, REGION),
        P(REGION),
    )
    out_specs = (P(REGION, None), P(), P(), P(REGION))

    return jax.shard_map(local, mesh=finer, in_specs=in_specs, out_specs=out_specs, check_vma=False)
```

```python
import jax
import jax.numpy as jnp
from jax import lax
from jax.experimental import pallas as pl
from jax.experimental.pallas import tpu as pltpu
from jax.sharding import Mesh
from jax.sharding import PartitionSpec as P


REGION = ("z", "yhi", "x")
MEMBER = ("ylo", "core")
CHIPS = ("ylo", "z", "yhi", "x")
EVERY = ("ylo", "core", "z", "yhi", "x")

SMOOTH_SQ = 0.01
C0 = 0.7978845608028654
C1 = 0.044715
WIDE = 256
PAD = 128
bf16 = jnp.bfloat16
f32 = jnp.float32
f16 = jnp.float16
EDGE = 16
DEEP = 128
SPLIT = 3


def dot(a, b, ca=1, cb=0):
    return lax.dot_general(a, b, (((ca,), (cb,)), ((), ())), preferred_element_type=f32)


def params(semantics, mib):
    return pltpu.CompilerParams(dimension_semantics=semantics, vmem_limit_bytes=mib << 20)


def parked(a):
    return pltpu.with_memory_space_constraint(a, pltpu.VMEM)


def settled(a):
    return pltpu.with_memory_space_constraint(a, pltpu.HBM)


def whole(a):
    return pl.BlockSpec(a.shape, lambda *i: (0,) * a.ndim)


def prep_kernel(src, weight, bias, *rest):
    at, lift = rest[-2:]
    nodes, wide = at.shape[0] - DEEP, at.shape[1]
    place = lax.broadcasted_iota(jnp.int32, (nodes, wide), 0)
    total = jnp.zeros((nodes, wide), f32)
    for k in range(src.shape[0]):
        total = total + jnp.where(src[k : k + 1, :] == place, weight[k : k + 1, :], 0.0)
    at[:nodes, :] = total.astype(bf16)
    first = lax.broadcasted_iota(jnp.int32, (DEEP, wide), 0) < SPLIT
    at[nodes:, :] = jnp.where(first, 1.0, 0.0).astype(bf16)
    row = lax.broadcasted_iota(jnp.int32, lift.shape, 0)
    block, rest = jnp.zeros(lift.shape, f32), bias[...]
    for k in range(SPLIT):
        part = rest.astype(bf16).astype(f32)
        block = jnp.where(row == k, part, block)
        rest = rest - part
    lift[...] = block.astype(bf16)


def prep(src, weight, bias, nodes, later):
    fan, points = src.shape
    width = bias.shape[1]
    steps = points // WIDE
    row = pl.BlockSpec((fan, WIDE), lambda i: (0, i))
    return pl.pallas_call(
        prep_kernel,
        grid=(steps,),
        in_specs=[row, row, pl.BlockSpec((1, width // steps), lambda i: (0, i))] + [pl.BlockSpec(memory_space=pltpu.VMEM)] * len(later),
        out_specs=[
            pl.BlockSpec((nodes + DEEP, WIDE), lambda i: (0, i)),
            pl.BlockSpec((DEEP, width // steps), lambda i: (0, i)),
        ],
        out_shape=[pltpu.VMEM((nodes + DEEP, points), bf16), pltpu.VMEM((DEEP, width), bf16)],
        compiler_params=params(("arbitrary",), 8),
        name="prep",
    )(*map(settled, (src, weight, bias)), *map(parked, later))


def turn_kernel(*refs):
    blocks, out = refs[:-1], refs[-1]
    for b, block in enumerate(blocks):
        nodes = block.shape[0]
        out[:, b * nodes : (b + 1) * nodes] = block[...].T


def turn(blocks):
    nodes, width = blocks[0].shape
    return pl.pallas_call(
        turn_kernel,
        grid=(width // WIDE,),
        in_specs=[pl.BlockSpec((nodes, WIDE), lambda i: (0, i))] * len(blocks),
        out_specs=pl.BlockSpec((WIDE, nodes * len(blocks)), lambda i: (i, 0)),
        out_shape=pltpu.VMEM((width, nodes * len(blocks)), bf16),
        compiler_params=params(("arbitrary",), 8),
        name="turn",
    )(*blocks)


def forward_kernel(low, own, high, w_node, at, bias, w_out, target, hid, pre, err, proj):
    nodes = 3 * low.shape[0]

    stacked = jnp.concatenate([low[...], own[...], high[...]], axis=0)
    proj[:, :nodes] = dot(stacked, w_node[...]).astype(bf16).T
    proj[:, nodes:] = bias[...].T

    for g in range(target.shape[1] // 256):
        cols = slice(g * 256, (g + 1) * 256)
        for r in range(proj.shape[0] // 256):
            rows = slice(r * 256, (r + 1) * 256)
            x = dot(proj[rows, :], at[:, cols])
            pre[rows, cols] = x.astype(bf16)
            u = 0.5 + 0.5 * jnp.tanh(x * (C0 + (C0 * C1) * (x * x)))
            hid[rows, cols] = (x * u).astype(bf16)
    err[...] = dot(w_out[...], hid[...]) - target[...]


def forward(low, own, high, w_node, at, bias, w_out, target):
    width = w_node.shape[1]
    points = at.shape[1]
    variables = target.shape[0]
    vm = pl.BlockSpec(memory_space=pltpu.VMEM)
    return pl.pallas_call(
        forward_kernel,
        in_specs=[vm] * 8,
        out_specs=[vm] * 3,
        out_shape=[
            pltpu.VMEM((width, points), bf16),
            pltpu.VMEM((width, points), bf16),
            pltpu.VMEM((variables, points), f32),
        ],
        scratch_shapes=[pltpu.VMEM((width, at.shape[0]), bf16)],
        compiler_params=pltpu.CompilerParams(vmem_limit_bytes=24 << 20),
        name="forward",
    )(parked(low), parked(own), parked(high), parked(w_node), parked(at), parked(bias), parked(w_out), parked(target))


def slope_kernel(pre, out):
    for g in range(pre.shape[1] // WIDE):
        cols = slice(g * WIDE, (g + 1) * WIDE)
        x = pre[:, cols].astype(f32)
        sq = x * x
        u = 0.5 + 0.5 * jnp.tanh(x * (C0 + (C0 * C1) * sq))
        out[:, cols] = (u + (x * u) * (1.0 - u) * (2.0 * C0 + (6.0 * C0 * C1) * sq)).astype(bf16)


def slopes(pre):
    width, points = pre.shape
    rows = pl.BlockSpec((128, points), lambda i: (i, 0))
    return pl.pallas_call(
        slope_kernel,
        grid=(width // 128,),
        in_specs=[rows],
        out_specs=rows,
        out_shape=pltpu.VMEM((width, points), bf16),
        compiler_params=params(("arbitrary",), 8),
        name="slope",
    )(parked(pre))


def apart(d):
    q = d * d + SMOOTH_SQ
    r = lax.rsqrt(q)
    return q * r, d * r


def near_kernel(count, scale, own_0, own_1, *rest):
    others, (area, p_0, p_1, loss) = rest[:-4], rest[-4:]
    pairs = count * (count - 1)

    @pl.when(pl.program_id(0) == 0)
    def _():
        loss[...] = jnp.zeros_like(loss)

    for c in range(own_0.shape[1] // PAD):
        at = slice(c * PAD, (c + 1) * PAD)
        a, b = own_0[:, at], own_1[:, at]
        own_a, slope_a = apart(a)
        own_b, slope_b = apart(b)
        dist, t = apart(a - b)
        dist = 2.0 * dist
        sum_a, sum_b = t, -t
        for other in others:
            o = other[:, at]
            s, t = apart(a - o)
            dist = dist + s
            sum_a = sum_a + t
            s, t = apart(b - o)
            dist = dist + s
            sum_b = sum_b + t
        value = (own_a + own_b) * (1.0 / count) - dist * (0.5 / pairs)
        loss[...] += jnp.sum(value, axis=0, keepdims=True) * area[:, at] * (1.0 / scale)
        p_0[:, at] = slope_a * (1.0 / count) - sum_a * (1.0 / pairs)
        p_1[:, at] = slope_b * (1.0 / count) - sum_b * (1.0 / pairs)


def far_kernel(count, scale, own_0, own_1, *rest):
    others, (p_0, p_1, area, before, d_0, d_1, loss) = rest[:-7], rest[-7:]
    variables = own_0.shape[0]
    pairs = count * (count - 1)

    @pl.when(pl.program_id(0) == 0)
    def _():
        loss[...] = before[...]

    for c in range(own_0.shape[1] // PAD):
        at = slice(c * PAD, (c + 1) * PAD)
        a, b = own_0[:, at], own_1[:, at]
        dist, sum_a, sum_b = 0.0, 0.0, 0.0
        for other in others:
            o = other[:, at]
            s, t = apart(a - o)
            dist = dist + s
            sum_a = sum_a + t
            s, t = apart(b - o)
            dist = dist + s
            sum_b = sum_b + t
        where = area[:, at]
        loss[...] -= jnp.sum(dist, axis=0, keepdims=True) * where * (0.5 / pairs / scale)
        fold = where * (1.0 / variables)
        for ref, p, t in ((d_0, p_0, sum_a), (d_1, p_1, sum_b)):
            ref[:variables, at] = ((p[:, at] - t * (1.0 / pairs)) * fold).astype(bf16)
            ref[variables:, at] = jnp.zeros((PAD - variables, PAD), bf16)


def crps_near(own, others, area, count):
    variables, points = own[0].shape
    wide = 512
    field = pl.BlockSpec((variables, wide), lambda i: (0, i))
    row = pl.BlockSpec((1, wide), lambda i: (0, i))
    return pl.pallas_call(
        lambda *refs: near_kernel(count, variables * points, *refs),
        grid=(points // wide,),
        in_specs=[field] * (2 + len(others)) + [row],
        out_specs=[field, field, pl.BlockSpec((1, PAD), lambda i: (0, 0))],
        out_shape=[pltpu.VMEM((variables, points), f32)] * 2 + [jax.ShapeDtypeStruct((1, PAD), f32)],
        compiler_params=params(("arbitrary",), 16),
        name="crps_near",
    )(*map(parked, own), *others, area)


def crps_far(own, others, partial, area, before, count):
    variables, points = own[0].shape
    wide = 512
    field = pl.BlockSpec((variables, wide), lambda i: (0, i))
    padded = pl.BlockSpec((PAD, wide), lambda i: (0, i))
    row = pl.BlockSpec((1, wide), lambda i: (0, i))
    one = pl.BlockSpec((1, PAD), lambda i: (0, 0))
    return pl.pallas_call(
        lambda *refs: far_kernel(count, variables * points, *refs),
        grid=(points // wide,),
        in_specs=[field] * (4 + len(others)) + [row, one],
        out_specs=[padded, padded, one],
        out_shape=[pltpu.VMEM((PAD, points), bf16)] * 2 + [jax.ShapeDtypeStruct((1, PAD), f32)],
        compiler_params=params(("arbitrary",), 16),
        name="crps_far",
    )(*map(parked, own), *others, *map(parked, partial), area, before)


def backward_kernel(who, d_0, d_1, w_out, s_0, s_1, h_0, h_1, at, loss, contrib, heads, dpre):
    nodes = at.shape[0] - DEEP
    variables = w_out.shape[0]
    shape = (PAD, WIDE)
    row = lax.broadcasted_iota(jnp.int32, shape, 0)
    lane = lax.broadcasted_iota(jnp.int32, shape, 1)
    for y in range(contrib.shape[0]):
        first = pl.multiple_of((2 * y + who[0]) * WIDE, WIDE)
        rows = pl.ds(first, WIDE)
        total = jnp.where((row == variables + 1) & (lane + first == who[1]), jnp.sum(loss[...]), 0.0)
        turned = w_out[:, rows].T
        for m, (d, slope, hid) in enumerate(((d_0, s_0, h_0), (d_1, s_1, h_1))):
            for g in range(d.shape[1] // WIDE):
                cut = slice(g * WIDE, (g + 1) * WIDE)
                part = dot(turned, d[:variables, cut]) * slope[rows, cut].astype(f32)
                dpre[y, m, :, cut] = part.astype(bf16)
            total = total + dot(d[...], hid[rows, :], 1, 1)
            part = dot(at[: nodes + EDGE], dpre[y, m], 1, 1)
            contrib[y, m * nodes : (m + 1) * nodes, :] = part[:nodes].astype(bf16)
            total = total + jnp.where(row == variables, part[nodes : nodes + 1], 0.0)
        for i in range(PAD // 8):
            for j in range(WIDE // 128):
                heads[y, i, j] = total[i * 8 : (i + 1) * 8, j * 128 : (j + 1) * 128]


def backward(who, dpred, w_out, slope, hid, at, loss):
    width, points = slope[0].shape
    nodes = at.shape[0] - DEEP
    count = width // WIDE // 2
    vm = pl.BlockSpec(memory_space=pltpu.VMEM)
    return pl.pallas_call(
        backward_kernel,
        in_specs=[pl.BlockSpec(memory_space=pltpu.SMEM)] + [vm] * 9,
        out_specs=[vm, vm],
        out_shape=[
            pltpu.VMEM((count, 2 * nodes, WIDE), bf16),
            pltpu.VMEM((count, PAD // 8, WIDE // 128, 8, 128), f32),
        ],
        scratch_shapes=[pltpu.VMEM((count, 2, WIDE, points), bf16)],
        compiler_params=pltpu.CompilerParams(vmem_limit_bytes=24 << 20),
        name="backward",
    )(who, *map(parked, dpred), parked(w_out), *map(parked, slope), *map(parked, hid), parked(at), parked(loss))


def outer_kernel(lat_own, lat_other, c_own, c_other, h_own, h_other, out):
    regions = out.shape[1]
    share = lat_own.shape[0] // regions
    for y in range(c_own.shape[0]):
        part = (dot(lat_own[...], c_own[y]) + dot(lat_other[...], c_other[y])).astype(bf16)
        for r in range(regions):
            for j in range(part.shape[1] // 128):
                out[y, r, j * share : (j + 1) * share] = part[r * share : (r + 1) * share, j * 128 : (j + 1) * 128]
            out[y, r, 2 * share :] = (h_own[y, r] + h_other[y, r]).astype(bf16)


def outer(lat_own, lat_other, c_own, c_other, h_own, h_other, regions):
    inputs, nodes = lat_own.shape
    halves, _, _ = c_own.shape
    share = inputs // regions
    here = WIDE // share
    lat = pl.BlockSpec((WIDE, nodes), lambda i: (i, 0))
    piece = pl.BlockSpec((halves, here, 8, 128), lambda i: (0, i, 0, 0))
    return pl.pallas_call(
        outer_kernel,
        grid=(inputs // WIDE,),
        in_specs=[lat, lat, whole(c_own), whole(c_own), piece, piece],
        out_specs=pl.BlockSpec((halves, here, 2 * share + 8, 128), lambda i: (0, i, 0, 0)),
        out_shape=pltpu.VMEM((halves, regions, 2 * share + 8, 128), bf16),
        compiler_params=params(("arbitrary",), 16),
        name="outer",
    )(parked(lat_own), lat_other, parked(c_own), c_other, parked(h_own), h_other)


def finish_kernel(where, mine, others, rows_mine, rows_others, grad_node, grad_out, grad_bias, loss):
    variables, _ = grad_out.shape
    per_row = WIDE // 128
    lower = where[1] == 0
    for core in range(2):
        first = lower if core == 0 else jnp.logical_not(lower)
        for ylo in range(rows_mine.shape[0]):
            left = (2 * ylo + core) * WIDE
            grad_node[:, left : left + WIDE] = jnp.where(first, rows_mine[ylo], rows_others[ylo])
        for at in range(mine.shape[0]):
            ylo, place = at // 32, at % 32
            i, j = place // per_row, place % per_row
            left, top = (2 * ylo + core) * WIDE + j * 128, i * 8
            if top >= variables + 2:
                continue
            piece = jnp.where(first, mine[at], others[at])
            rows = min(8, variables - top)
            if rows > 0:
                grad_out[top : top + rows, left : left + 128] = piece[:rows]
            line = variables - top
            if 0 <= line < 7:
                grad_bias[:, left : left + 128] = piece[line : line + 1]
                if left == 0:
                    values = piece[line + 1 : line + 2]
                    spot = lax.broadcasted_iota(jnp.int32, values.shape, 1)
                    loss[...] = jnp.sum(jnp.where(spot == where[0], values, 0.0), axis=1, keepdims=True)


def finish(where, mine, others, rows_mine, rows_others, variables, width):
    vm = pl.BlockSpec(memory_space=pltpu.VMEM)
    return pl.pallas_call(
        finish_kernel,
        in_specs=[pl.BlockSpec(memory_space=pltpu.SMEM)] + [vm] * 4,
        out_shape=[
            jax.ShapeDtypeStruct((rows_mine.shape[1], width), f32),
            jax.ShapeDtypeStruct((variables, width), f32),
            jax.ShapeDtypeStruct((1, width), f32),
            jax.ShapeDtypeStruct((1, 1), f32),
        ],
        compiler_params=pltpu.CompilerParams(vmem_limit_bytes=8 << 20),
        name="finish",
    )(where, mine, others, rows_mine, rows_others)


def local(latent, w_node, bias, w_out, edge_src, edge_weight, target, area):
    members, nodes, width = latent.shape
    variables = target.shape[0]
    regions = lax.axis_size(REGION)
    count = members * lax.axis_size(MEMBER)
    ahead = [(i, (i + 1) % regions) for i in range(regions)]
    behind = [(t, s) for s, t in ahead]
    swap = [(0, 1), (1, 0)]
    core = lax.axis_index("core")
    where = lax.axis_index(REGION)

    mine = [latent[0]] + [lax.optimization_barrier(latent)[m] for m in range(1, members)]

    low, high = [], []
    for m in range(members):
        low.append(lax.ppermute(mine[m], REGION, ahead))
        high.append(lax.ppermute(mine[m], REGION, behind))
    at, lift = prep(edge_src.T, edge_weight.T, bias[None, :], 3 * nodes, (w_node,))

    hid, slope, err, near, far, beside = [], [], [], [], [], []
    for m in range(members):
        h, s, e = forward(low[m], mine[m], high[m], w_node, at, lift, w_out, target)
        hid.append(h)
        slope.append(slopes(s))
        err.append(e)
        over = lax.ppermute((e * 0.125).astype(f16), "ylo", swap)
        near.append(lax.ppermute(e, "core", swap))
        far.append(over.astype(f32) * 8.0)
        beside.append(lax.ppermute(over, "core", swap).astype(f32) * 8.0)

    first, err[1] = lax.optimization_barrier((mine[0], err[1]))
    lat_t = turn((low[0], first, high[0], low[1], mine[1], high[1]))
    lat_t_other = lax.ppermute(lat_t, "core", swap)

    area_row = area[None, :]
    p_0, p_1, loss = crps_near(err, near + [far[0], beside[0]], area_row, count)
    d_0, d_1, loss = crps_far(err, [far[1], beside[1]], (p_0, p_1), area_row, loss, count)


    def back(side):
        who = jnp.stack([side, where]).astype(jnp.int32)
        return backward(who, (d_0, d_1), w_out, slope, hid, at, loss)

    given, heads_given = back(1 - core)
    taken = lax.ppermute(given, "core", swap)
    heads_taken = lax.ppermute(heads_given, "core", swap)
    kept, heads_kept = back(core)
    tiles = (2, regions, 8, 128)
    part = outer(lat_t, lat_t_other, kept, taken, heads_kept.reshape(tiles), heads_taken.reshape(tiles), regions)
    chips = lax.axis_size(CHIPS)
    share = width // regions
    shares = lax.all_to_all(
        part.reshape(chips, 2 * share + 8, 128), CHIPS, split_axis=0, concat_axis=0, tiled=True
    )
    summed = shares.astype(f32).sum(axis=0)
    own = jnp.concatenate([summed[:share], summed[share : 2 * share]], axis=1)
    table = lax.all_to_all(
        jnp.broadcast_to(summed[2 * share :], (chips, 8, 128)), CHIPS, split_axis=0, concat_axis=0, tiled=True
    )
    across = lax.ppermute(own, "ylo", swap)
    upper = lax.axis_index("ylo") == 1
    rows = jnp.stack([jnp.where(upper, across, own), jnp.where(upper, own, across)])
    rows_others = lax.ppermute(rows, "core", swap)
    table_others = lax.ppermute(table, "core", swap)
    who = jnp.stack([where, core]).astype(jnp.int32)
    grad_node, grad_out, grad_bias, loss_here = finish(who, table, table_others, rows, rows_others, variables, width)
    grad_bias = grad_bias.reshape(width)
    loss_here = loss_here.reshape(1)
    return grad_node, grad_out, grad_bias, loss_here


def solution(mesh):
    finer = Mesh(mesh.devices.reshape(2, 2, 4, 2, 4), EVERY)
    in_specs = (
        P(MEMBER, REGION, None),
        P(),
        P(),
        P(),
        P(REGION, None),
        P(REGION, None),
        P(None, REGION),
        P(REGION),
    )
    out_specs = (P(REGION, None), P(), P(), P(REGION))

    return jax.shard_map(local, mesh=finer, in_specs=in_specs, out_specs=out_specs, check_vma=False)
```

```python
import jax
import jax.numpy as jnp
from jax import lax
from jax.experimental import pallas as pl
from jax.experimental.pallas import tpu as pltpu
from jax.sharding import Mesh
from jax.sharding import PartitionSpec as P


REGION = ("z", "yhi", "x")
MEMBER = ("ylo", "core")
CHIPS = ("ylo", "z", "yhi", "x")
EVERY = ("ylo", "core", "z", "yhi", "x")

SMOOTH_SQ = 0.01
C0 = 0.7978845608028654
C1 = 0.044715
WIDE = 256
PAD = 128
bf16 = jnp.bfloat16
f32 = jnp.float32
f16 = jnp.float16
EDGE = 16
DEEP = 128
SPLIT = 3


def dot(a, b, ca=1, cb=0):
    return lax.dot_general(a, b, (((ca,), (cb,)), ((), ())), preferred_element_type=f32)


def params(semantics, mib):
    return pltpu.CompilerParams(dimension_semantics=semantics, vmem_limit_bytes=mib << 20)


def parked(a):
    return pltpu.with_memory_space_constraint(a, pltpu.VMEM)


def settled(a):
    return pltpu.with_memory_space_constraint(a, pltpu.HBM)


def prep_kernel(src, weight, bias, *rest):
    at, lift = rest[-2:]
    nodes, wide = at.shape[0] - DEEP, at.shape[1]
    place = lax.broadcasted_iota(jnp.int32, (nodes, wide), 0)
    total = jnp.zeros((nodes, wide), f32)
    for k in range(src.shape[0]):
        total = total + jnp.where(src[k : k + 1, :] == place, weight[k : k + 1, :], 0.0)
    at[:nodes, :] = total.astype(bf16)
    first = lax.broadcasted_iota(jnp.int32, (DEEP, wide), 0) < SPLIT
    at[nodes:, :] = jnp.where(first, 1.0, 0.0).astype(bf16)
    row = lax.broadcasted_iota(jnp.int32, lift.shape, 0)
    block, rest = jnp.zeros(lift.shape, f32), bias[...]
    for k in range(SPLIT):
        part = rest.astype(bf16).astype(f32)
        block = jnp.where(row == k, part, block)
        rest = rest - part
    lift[...] = block.astype(bf16)


def prep(src, weight, bias, nodes, later):
    fan, points = src.shape
    width = bias.shape[1]
    steps = points // WIDE
    row = pl.BlockSpec((fan, WIDE), lambda i: (0, i))
    return pl.pallas_call(
        prep_kernel,
        grid=(steps,),
        in_specs=[row, row, pl.BlockSpec((1, width // steps), lambda i: (0, i))] + [pl.BlockSpec(memory_space=pltpu.VMEM)] * len(later),
        out_specs=[
            pl.BlockSpec((nodes + DEEP, WIDE), lambda i: (0, i)),
            pl.BlockSpec((DEEP, width // steps), lambda i: (0, i)),
        ],
        out_shape=[pltpu.VMEM((nodes + DEEP, points), bf16), pltpu.VMEM((DEEP, width), bf16)],
        compiler_params=params(("arbitrary",), 8),
        name="prep",
    )(*map(settled, (src, weight, bias)), *map(parked, later))


def turn_kernel(*refs):
    blocks, out = refs[:-1], refs[-1]
    for b, block in enumerate(blocks):
        nodes = block.shape[0]
        out[:, b * nodes : (b + 1) * nodes] = block[...].T


def turn(blocks):
    nodes, width = blocks[0].shape
    return pl.pallas_call(
        turn_kernel,
        grid=(width // WIDE,),
        in_specs=[pl.BlockSpec((nodes, WIDE), lambda i: (0, i))] * len(blocks),
        out_specs=pl.BlockSpec((WIDE, nodes * len(blocks)), lambda i: (i, 0)),
        out_shape=pltpu.VMEM((width, nodes * len(blocks)), bf16),
        compiler_params=params(("arbitrary",), 8),
        name="turn",
    )(*blocks)


def forward_kernel(low, own, high, w_node, at, bias, w_out, target, hid, slope, err, proj):
    nodes = 3 * low.shape[0]

    stacked = jnp.concatenate([low[...], own[...], high[...]], axis=0)
    proj[:, :nodes] = dot(stacked, w_node[...]).astype(bf16).T
    proj[:, nodes:] = bias[...].T

    for g in range(target.shape[1] // 256):
        cols = slice(g * 256, (g + 1) * 256)
        for r in range(proj.shape[0] // 256):
            rows = slice(r * 256, (r + 1) * 256)
            x = dot(proj[rows, :], at[:, cols])
            sq = x * x
            u = 0.5 + 0.5 * jnp.tanh(x * (C0 + (C0 * C1) * sq))
            h = x * u
            hid[rows, cols] = h.astype(bf16)
            slope[rows, cols] = (u + h * (1.0 - u) * (2.0 * C0 + (6.0 * C0 * C1) * sq)).astype(bf16)
    err[...] = dot(w_out[...], hid[...]) - target[...]


def forward(low, own, high, w_node, at, bias, w_out, target):
    width = w_node.shape[1]
    points = at.shape[1]
    variables = target.shape[0]
    vm = pl.BlockSpec(memory_space=pltpu.VMEM)
    return pl.pallas_call(
        forward_kernel,
        in_specs=[vm] * 8,
        out_specs=[vm] * 3,
        out_shape=[
            pltpu.VMEM((width, points), bf16),
            pltpu.VMEM((width, points), bf16),
            pltpu.VMEM((variables, points), f32),
        ],
        scratch_shapes=[pltpu.VMEM((width, at.shape[0]), bf16)],
        compiler_params=pltpu.CompilerParams(vmem_limit_bytes=24 << 20),
        name="forward",
    )(parked(low), parked(own), parked(high), parked(w_node), parked(at), parked(bias), parked(w_out), parked(target))


def apart(d):
    q = d * d + SMOOTH_SQ
    r = lax.rsqrt(q)
    return q * r, d * r


def near_kernel(count, scale, own_0, own_1, *rest):
    others, (area, p_0, p_1, loss) = rest[:-4], rest[-4:]
    pairs = count * (count - 1)

    @pl.when(pl.program_id(0) == 0)
    def _():
        loss[...] = jnp.zeros_like(loss)

    for c in range(own_0.shape[1] // PAD):
        at = slice(c * PAD, (c + 1) * PAD)
        a, b = own_0[:, at], own_1[:, at]
        own_a, slope_a = apart(a)
        own_b, slope_b = apart(b)
        dist, t = apart(a - b)
        dist = 2.0 * dist
        sum_a, sum_b = t, -t
        for other in others:
            o = other[:, at]
            s, t = apart(a - o)
            dist = dist + s
            sum_a = sum_a + t
            s, t = apart(b - o)
            dist = dist + s
            sum_b = sum_b + t
        value = (own_a + own_b) * (1.0 / count) - dist * (0.5 / pairs)
        loss[...] += jnp.sum(value, axis=0, keepdims=True) * area[:, at] * (1.0 / scale)
        p_0[:, at] = slope_a * (1.0 / count) - sum_a * (1.0 / pairs)
        p_1[:, at] = slope_b * (1.0 / count) - sum_b * (1.0 / pairs)


def far_kernel(count, scale, own_0, own_1, *rest):
    others, (p_0, p_1, area, before, d_0, d_1, loss) = rest[:-7], rest[-7:]
    variables = own_0.shape[0]
    pairs = count * (count - 1)

    @pl.when(pl.program_id(0) == 0)
    def _():
        loss[...] = before[...]

    for c in range(own_0.shape[1] // PAD):
        at = slice(c * PAD, (c + 1) * PAD)
        a, b = own_0[:, at], own_1[:, at]
        dist, sum_a, sum_b = 0.0, 0.0, 0.0
        for other in others:
            o = other[:, at]
            s, t = apart(a - o)
            dist = dist + s
            sum_a = sum_a + t
            s, t = apart(b - o)
            dist = dist + s
            sum_b = sum_b + t
        where = area[:, at]
        loss[...] -= jnp.sum(dist, axis=0, keepdims=True) * where * (0.5 / pairs / scale)
        fold = where * (1.0 / variables)
        for ref, p, t in ((d_0, p_0, sum_a), (d_1, p_1, sum_b)):
            ref[:variables, at] = ((p[:, at] - t * (1.0 / pairs)) * fold).astype(bf16)
            ref[variables:, at] = jnp.zeros((PAD - variables, PAD), bf16)


def crps_near(own, others, area, count):
    variables, points = own[0].shape
    wide = 512
    field = pl.BlockSpec((variables, wide), lambda i: (0, i))
    row = pl.BlockSpec((1, wide), lambda i: (0, i))
    return pl.pallas_call(
        lambda *refs: near_kernel(count, variables * points, *refs),
        grid=(points // wide,),
        in_specs=[field] * (2 + len(others)) + [row],
        out_specs=[field, field, pl.BlockSpec((1, PAD), lambda i: (0, 0))],
        out_shape=[pltpu.VMEM((variables, points), f32)] * 2 + [jax.ShapeDtypeStruct((1, PAD), f32)],
        compiler_params=params(("arbitrary",), 16),
        name="crps_near",
    )(*map(parked, own), *others, area)


def crps_far(own, others, partial, area, before, count):
    variables, points = own[0].shape
    wide = 512
    field = pl.BlockSpec((variables, wide), lambda i: (0, i))
    padded = pl.BlockSpec((PAD, wide), lambda i: (0, i))
    row = pl.BlockSpec((1, wide), lambda i: (0, i))
    one = pl.BlockSpec((1, PAD), lambda i: (0, 0))
    return pl.pallas_call(
        lambda *refs: far_kernel(count, variables * points, *refs),
        grid=(points // wide,),
        in_specs=[field] * (4 + len(others)) + [row, one],
        out_specs=[padded, padded, one],
        out_shape=[pltpu.VMEM((PAD, points), bf16)] * 2 + [jax.ShapeDtypeStruct((1, PAD), f32)],
        compiler_params=params(("arbitrary",), 16),
        name="crps_far",
    )(*map(parked, own), *others, *map(parked, partial), area, before)


def backward_kernel(who, d_0, d_1, w_out, s_0, s_1, h_0, h_1, at, loss, contrib, heads, dpre):
    nodes = at.shape[0] - DEEP
    variables = w_out.shape[0]
    shape = (PAD, WIDE)
    row = lax.broadcasted_iota(jnp.int32, shape, 0)
    lane = lax.broadcasted_iota(jnp.int32, shape, 1)
    for y in range(contrib.shape[0]):
        first = pl.multiple_of((2 * y + who[0]) * WIDE, WIDE)
        rows = pl.ds(first, WIDE)
        total = jnp.where((row == variables + 1) & (lane + first == who[1]), jnp.sum(loss[...]), 0.0)
        turned = w_out[:, rows].T
        for m, (d, slope, hid) in enumerate(((d_0, s_0, h_0), (d_1, s_1, h_1))):
            for g in range(d.shape[1] // WIDE):
                cut = slice(g * WIDE, (g + 1) * WIDE)
                part = dot(turned, d[:variables, cut]) * slope[rows, cut].astype(f32)
                dpre[y, m, :, cut] = part.astype(bf16)
            total = total + dot(d[...], hid[rows, :], 1, 1)
            part = dot(at[: nodes + EDGE], dpre[y, m], 1, 1)
            contrib[y, m * nodes : (m + 1) * nodes, :] = part[:nodes].astype(bf16)
            total = total + jnp.where(row == variables, part[nodes : nodes + 1], 0.0)
        for i in range(PAD // 8):
            for j in range(WIDE // 128):
                heads[y, i, j] = total[i * 8 : (i + 1) * 8, j * 128 : (j + 1) * 128]


def backward(who, dpred, w_out, slope, hid, at, loss):
    width, points = slope[0].shape
    nodes = at.shape[0] - DEEP
    count = width // WIDE // 2
    vm = pl.BlockSpec(memory_space=pltpu.VMEM)
    return pl.pallas_call(
        backward_kernel,
        in_specs=[pl.BlockSpec(memory_space=pltpu.SMEM)] + [vm] * 9,
        out_specs=[vm, vm],
        out_shape=[
            pltpu.VMEM((count, 2 * nodes, WIDE), bf16),
            pltpu.VMEM((count, PAD // 8, WIDE // 128, 8, 128), f32),
        ],
        scratch_shapes=[pltpu.VMEM((count, 2, WIDE, points), bf16)],
        compiler_params=pltpu.CompilerParams(vmem_limit_bytes=24 << 20),
        name="backward",
    )(who, *map(parked, dpred), parked(w_out), *map(parked, slope), *map(parked, hid), parked(at), parked(loss))


def outer_kernel(lat_own, lat_other, c_own, c_other, h_own, h_other, out):
    regions = out.shape[1]
    share = lat_own.shape[0] // regions
    for i in range(lat_own.shape[0] // WIDE):
        rows = slice(i * WIDE, (i + 1) * WIDE)
        for y in range(c_own.shape[0]):
            part = (dot(lat_own[rows], c_own[y]) + dot(lat_other[rows], c_other[y])).astype(bf16)
            for k in range(WIDE // share):
                r = i * (WIDE // share) + k
                for j in range(part.shape[1] // 128):
                    out[y, r, j * share : (j + 1) * share] = part[k * share : (k + 1) * share, j * 128 : (j + 1) * 128]
                out[y, r, 2 * share :] = (h_own[y, r] + h_other[y, r]).astype(bf16)


def outer(lat_own, lat_other, c_own, c_other, h_own, h_other, regions):
    inputs = lat_own.shape[0]
    halves = c_own.shape[0]
    share = inputs // regions
    vm = pl.BlockSpec(memory_space=pltpu.VMEM)
    return pl.pallas_call(
        outer_kernel,
        in_specs=[vm] * 6,
        out_specs=vm,
        out_shape=pltpu.VMEM((halves, regions, 2 * share + 8, 128), bf16),
        compiler_params=pltpu.CompilerParams(vmem_limit_bytes=12 << 20),
        name="outer",
    )(*map(parked, (lat_own, lat_other, c_own, c_other, h_own, h_other)))


def finish_kernel(where, table, rows_mine, rows_others, grad_node, grad_out, grad_bias, loss):
    variables, _ = grad_out.shape
    per_row = WIDE // 128
    lower = where[1] == 0
    for core in range(2):
        first = lower if core == 0 else jnp.logical_not(lower)
        for ylo in range(rows_mine.shape[0]):
            left = (2 * ylo + core) * WIDE
            grad_node[:, left : left + WIDE] = jnp.where(first, rows_mine[ylo], rows_others[ylo])
        for at in range(table.shape[0]):
            ylo, place = at // 64, at % 32
            i, j = place // per_row, place % per_row
            left, top = (2 * ylo + core) * WIDE + j * 128, i * 8
            if top >= variables + 2 or at // 32 % 2 != core:
                continue
            piece = table[at]
            rows = min(8, variables - top)
            if rows > 0:
                grad_out[top : top + rows, left : left + 128] = piece[:rows]
            line = variables - top
            if 0 <= line < 7:
                grad_bias[:, left : left + 128] = piece[line : line + 1]
                if left == 0:
                    values = piece[line + 1 : line + 2]
                    spot = lax.broadcasted_iota(jnp.int32, values.shape, 1)
                    loss[...] = jnp.sum(jnp.where(spot == where[0], values, 0.0), axis=1, keepdims=True)


def finish(where, table, rows_mine, rows_others, variables, width):
    vm = pl.BlockSpec(memory_space=pltpu.VMEM)
    return pl.pallas_call(
        finish_kernel,
        in_specs=[pl.BlockSpec(memory_space=pltpu.SMEM)] + [vm] * 3,
        out_shape=[
            jax.ShapeDtypeStruct((rows_mine.shape[1], width), f32),
            jax.ShapeDtypeStruct((variables, width), f32),
            jax.ShapeDtypeStruct((1, width), f32),
            jax.ShapeDtypeStruct((1, 1), f32),
        ],
        compiler_params=pltpu.CompilerParams(vmem_limit_bytes=8 << 20),
        name="finish",
    )(where, table, rows_mine, rows_others)


def local(latent, w_node, bias, w_out, edge_src, edge_weight, target, area):
    members, nodes, width = latent.shape
    variables = target.shape[0]
    regions = lax.axis_size(REGION)
    count = members * lax.axis_size(MEMBER)
    ahead = [(i, (i + 1) % regions) for i in range(regions)]
    behind = [(t, s) for s, t in ahead]
    swap = [(0, 1), (1, 0)]
    core = lax.axis_index("core")
    where = lax.axis_index(REGION)

    mine = [latent[0]] + [lax.optimization_barrier(latent)[m] for m in range(1, members)]

    low, high = [], []
    for m in range(members):
        low.append(lax.ppermute(mine[m], REGION, ahead))
        high.append(lax.ppermute(mine[m], REGION, behind))
    at, lift = prep(edge_src.T, edge_weight.T, bias[None, :], 3 * nodes, (w_node,))

    hid, slope, err, near, far, beside = [], [], [], [], [], []
    for m in range(members):
        h, s, e = forward(low[m], mine[m], high[m], w_node, at, lift, w_out, target)
        hid.append(h)
        slope.append(s)
        err.append(e)
        over = lax.ppermute((e * 0.125).astype(f16), "ylo", swap)
        near.append(lax.ppermute(e, "core", swap))
        far.append(over.astype(f32) * 8.0)
        beside.append(lax.ppermute(over, "core", swap).astype(f32) * 8.0)

    first, err[1] = lax.optimization_barrier((mine[0], err[1]))
    lat_t = turn((low[0], first, high[0], low[1], mine[1], high[1]))
    lat_t_other = lax.ppermute(lat_t, "core", swap)

    area_row = area[None, :]
    p_0, p_1, loss = crps_near(err, near + [far[0], beside[0]], area_row, count)
    d_0, d_1, loss = crps_far(err, [far[1], beside[1]], (p_0, p_1), area_row, loss, count)


    def back(side):
        who = jnp.stack([side, where]).astype(jnp.int32)
        return backward(who, (d_0, d_1), w_out, slope, hid, at, loss)

    given, heads_given = back(1 - core)
    taken = lax.ppermute(given, "core", swap)
    heads_taken = lax.ppermute(heads_given, "core", swap)
    kept, heads_kept = back(core)
    tiles = (2, regions, 8, 128)
    part = outer(lat_t, lat_t_other, kept, taken, heads_kept.reshape(tiles), heads_taken.reshape(tiles), regions)
    chips, every = lax.axis_size(CHIPS), lax.axis_size(EVERY)
    share = width // regions
    shares = lax.all_to_all(
        part.reshape(chips, 2 * share + 8, 128), CHIPS, split_axis=0, concat_axis=0, tiled=True
    )
    summed = shares.astype(f32).sum(axis=0)
    own = jnp.concatenate([summed[:share], summed[share : 2 * share]], axis=1)
    table = lax.all_to_all(
        jnp.broadcast_to(summed[2 * share :], (every, 8, 128)), EVERY, split_axis=0, concat_axis=0, tiled=True
    )
    across = lax.ppermute(own, "ylo", swap)
    upper = lax.axis_index("ylo") == 1
    rows = jnp.stack([jnp.where(upper, across, own), jnp.where(upper, own, across)])
    rows_others = lax.ppermute(rows, "core", swap)
    who = jnp.stack([where, core]).astype(jnp.int32)
    grad_node, grad_out, grad_bias, loss_here = finish(who, table, rows, rows_others, variables, width)
    grad_bias = grad_bias.reshape(width)
    loss_here = loss_here.reshape(1)
    return grad_node, grad_out, grad_bias, loss_here


def solution(mesh):
    finer = Mesh(mesh.devices.reshape(2, 2, 4, 2, 4), EVERY)
    in_specs = (
        P(MEMBER, REGION, None),
        P(),
        P(),
        P(),
        P(REGION, None),
        P(REGION, None),
        P(None, REGION),
        P(REGION),
    )
    out_specs = (P(REGION, None), P(), P(), P(REGION))

    return jax.shard_map(local, mesh=finer, in_specs=in_specs, out_specs=out_specs, check_vma=False)
```

```python
import jax
import jax.numpy as jnp
from jax import lax
from jax.experimental import pallas as pl
from jax.experimental.pallas import tpu as pltpu
from jax.sharding import Mesh
from jax.sharding import PartitionSpec as P


REGION = ("z", "yhi", "x")
MEMBER = ("ylo", "core")
CHIPS = ("ylo", "z", "yhi", "x")
EVERY = ("ylo", "core", "z", "yhi", "x")

SMOOTH_SQ = 0.01
C0 = 0.7978845608028654
C1 = 0.044715
WIDE = 256
PAD = 128
bf16 = jnp.bfloat16
f32 = jnp.float32
f16 = jnp.float16
EDGE = 16
DEEP = 128
SPLIT = 3


def dot(a, b, ca=1, cb=0):
    return lax.dot_general(a, b, (((ca,), (cb,)), ((), ())), preferred_element_type=f32)


def params(semantics, mib):
    return pltpu.CompilerParams(dimension_semantics=semantics, vmem_limit_bytes=mib << 20)


def parked(a):
    return pltpu.with_memory_space_constraint(a, pltpu.VMEM)


def settled(a):
    return pltpu.with_memory_space_constraint(a, pltpu.HBM)


def prep_kernel(src, weight, bias, *rest):
    at, lift = rest[-2:]
    nodes, wide = at.shape[0] - DEEP, at.shape[1]
    place = lax.broadcasted_iota(jnp.int32, (nodes, wide), 0)
    total = jnp.zeros((nodes, wide), f32)
    for k in range(src.shape[0]):
        total = total + jnp.where(src[k : k + 1, :] == place, weight[k : k + 1, :], 0.0)
    at[:nodes, :] = total.astype(bf16)
    first = lax.broadcasted_iota(jnp.int32, (DEEP, wide), 0) < SPLIT
    at[nodes:, :] = jnp.where(first, 1.0, 0.0).astype(bf16)
    row = lax.broadcasted_iota(jnp.int32, lift.shape, 0)
    block, rest = jnp.zeros(lift.shape, f32), bias[...]
    for k in range(SPLIT):
        part = rest.astype(bf16).astype(f32)
        block = jnp.where(row == k, part, block)
        rest = rest - part
    lift[...] = block.astype(bf16)


def prep(src, weight, bias, nodes, later):
    fan, points = src.shape
    width = bias.shape[1]
    steps = points // WIDE
    row = pl.BlockSpec((fan, WIDE), lambda i: (0, i))
    return pl.pallas_call(
        prep_kernel,
        grid=(steps,),
        in_specs=[row, row, pl.BlockSpec((1, width // steps), lambda i: (0, i))] + [pl.BlockSpec(memory_space=pltpu.VMEM)] * len(later),
        out_specs=[
            pl.BlockSpec((nodes + DEEP, WIDE), lambda i: (0, i)),
            pl.BlockSpec((DEEP, width // steps), lambda i: (0, i)),
        ],
        out_shape=[pltpu.VMEM((nodes + DEEP, points), bf16), pltpu.VMEM((DEEP, width), bf16)],
        compiler_params=params(("arbitrary",), 8),
        name="prep",
    )(*map(settled, (src, weight, bias)), *map(parked, later))


def turn_kernel(*refs):
    blocks, out = refs[:-1], refs[-1]
    for b, block in enumerate(blocks):
        nodes = block.shape[0]
        out[:, b * nodes : (b + 1) * nodes] = block[...].T


def turn(blocks):
    nodes, width = blocks[0].shape
    return pl.pallas_call(
        turn_kernel,
        grid=(width // WIDE,),
        in_specs=[pl.BlockSpec((nodes, WIDE), lambda i: (0, i))] * len(blocks),
        out_specs=pl.BlockSpec((WIDE, nodes * len(blocks)), lambda i: (i, 0)),
        out_shape=pltpu.VMEM((width, nodes * len(blocks)), bf16),
        compiler_params=params(("arbitrary",), 8),
        name="turn",
    )(*blocks)


def forward_kernel(low, own, high, w_node, at, bias, w_out, target, hid, slope, err, proj):
    nodes = 3 * low.shape[0]

    stacked = jnp.concatenate([low[...], own[...], high[...]], axis=0)
    proj[:, :nodes] = dot(stacked, w_node[...]).astype(bf16).T
    proj[:, nodes:] = bias[...].T

    for g in range(target.shape[1] // 256):
        cols = slice(g * 256, (g + 1) * 256)
        for r in range(proj.shape[0] // 256):
            rows = slice(r * 256, (r + 1) * 256)
            x = dot(proj[rows, :], at[:, cols])
            sq = x * x
            u = 0.5 + 0.5 * jnp.tanh(x * (C0 + (C0 * C1) * sq))
            h = x * u
            hid[rows, cols] = h.astype(bf16)
            if slope.dtype == f32:
                slope[rows, cols] = x
            else:
                slope[rows, cols] = (u + h * (1.0 - u) * (2.0 * C0 + (6.0 * C0 * C1) * sq)).astype(bf16)
    err[...] = dot(w_out[...], hid[...]) - target[...]


def forward(low, own, high, w_node, at, bias, w_out, target, kept):
    width = w_node.shape[1]
    points = at.shape[1]
    variables = target.shape[0]
    vm = pl.BlockSpec(memory_space=pltpu.VMEM)
    return pl.pallas_call(
        forward_kernel,
        in_specs=[vm] * 8,
        out_specs=[vm] * 3,
        out_shape=[
            pltpu.VMEM((width, points), bf16),
            pltpu.VMEM((width, points), kept),
            pltpu.VMEM((variables, points), f32),
        ],
        scratch_shapes=[pltpu.VMEM((width, at.shape[0]), bf16)],
        compiler_params=pltpu.CompilerParams(vmem_limit_bytes=12 << 20),
        name="forward",
    )(parked(low), parked(own), parked(high), parked(w_node), parked(at), parked(bias), parked(w_out), parked(target))


def slope_kernel(pre, out):
    for g in range(pre.shape[1] // WIDE):
        cols = slice(g * WIDE, (g + 1) * WIDE)
        x = pre[:, cols]
        sq = x * x
        u = 0.5 + 0.5 * jnp.tanh(x * (C0 + (C0 * C1) * sq))
        out[:, cols] = (u + (x * u) * (1.0 - u) * (2.0 * C0 + (6.0 * C0 * C1) * sq)).astype(bf16)


def slopes(pre):
    width, points = pre.shape
    rows = pl.BlockSpec((128, points), lambda i: (i, 0))
    return pl.pallas_call(
        slope_kernel,
        grid=(width // 128,),
        in_specs=[rows],
        out_specs=rows,
        out_shape=pltpu.VMEM((width, points), bf16),
        compiler_params=params(("arbitrary",), 8),
        name="slope",
    )(parked(pre))


def apart(d):
    q = d * d + SMOOTH_SQ
    r = lax.rsqrt(q)
    return q * r, d * r


def near_kernel(count, scale, own_0, own_1, *rest):
    others, (area, p_0, p_1, loss) = rest[:-4], rest[-4:]
    pairs = count * (count - 1)

    @pl.when(pl.program_id(0) == 0)
    def _():
        loss[...] = jnp.zeros_like(loss)

    for c in range(own_0.shape[1] // PAD):
        at = slice(c * PAD, (c + 1) * PAD)
        a, b = own_0[:, at], own_1[:, at]
        own_a, slope_a = apart(a)
        own_b, slope_b = apart(b)
        dist, t = apart(a - b)
        dist = 2.0 * dist
        sum_a, sum_b = t, -t
        for other in others:
            o = other[:, at]
            s, t = apart(a - o)
            dist = dist + s
            sum_a = sum_a + t
            s, t = apart(b - o)
            dist = dist + s
            sum_b = sum_b + t
        value = (own_a + own_b) * (1.0 / count) - dist * (0.5 / pairs)
        loss[...] += jnp.sum(value, axis=0, keepdims=True) * area[:, at] * (1.0 / scale)
        p_0[:, at] = slope_a * (1.0 / count) - sum_a * (1.0 / pairs)
        p_1[:, at] = slope_b * (1.0 / count) - sum_b * (1.0 / pairs)


def far_kernel(count, scale, own_0, own_1, *rest):
    others, (p_0, p_1, area, before, d_0, d_1, loss) = rest[:-7], rest[-7:]
    variables = own_0.shape[0]
    pairs = count * (count - 1)

    @pl.when(pl.program_id(0) == 0)
    def _():
        loss[...] = before[...]

    for c in range(own_0.shape[1] // PAD):
        at = slice(c * PAD, (c + 1) * PAD)
        a, b = own_0[:, at], own_1[:, at]
        dist, sum_a, sum_b = 0.0, 0.0, 0.0
        for other in others:
            o = other[:, at]
            s, t = apart(a - o)
            dist = dist + s
            sum_a = sum_a + t
            s, t = apart(b - o)
            dist = dist + s
            sum_b = sum_b + t
        where = area[:, at]
        loss[...] -= jnp.sum(dist, axis=0, keepdims=True) * where * (0.5 / pairs / scale)
        fold = where * (1.0 / variables)
        for ref, p, t in ((d_0, p_0, sum_a), (d_1, p_1, sum_b)):
            ref[:variables, at] = ((p[:, at] - t * (1.0 / pairs)) * fold).astype(bf16)
            ref[variables:, at] = jnp.zeros((PAD - variables, PAD), bf16)


def crps_near(own, others, area, count):
    variables, points = own[0].shape
    wide = 512
    field = pl.BlockSpec((variables, wide), lambda i: (0, i))
    row = pl.BlockSpec((1, wide), lambda i: (0, i))
    return pl.pallas_call(
        lambda *refs: near_kernel(count, variables * points, *refs),
        grid=(points // wide,),
        in_specs=[field] * (2 + len(others)) + [row],
        out_specs=[field, field, pl.BlockSpec((1, PAD), lambda i: (0, 0))],
        out_shape=[pltpu.VMEM((variables, points), f32)] * 2 + [jax.ShapeDtypeStruct((1, PAD), f32)],
        compiler_params=params(("arbitrary",), 16),
        name="crps_near",
    )(*map(parked, own), *others, area)


def crps_far(own, others, partial, area, before, count):
    variables, points = own[0].shape
    wide = 512
    field = pl.BlockSpec((variables, wide), lambda i: (0, i))
    padded = pl.BlockSpec((PAD, wide), lambda i: (0, i))
    row = pl.BlockSpec((1, wide), lambda i: (0, i))
    one = pl.BlockSpec((1, PAD), lambda i: (0, 0))
    return pl.pallas_call(
        lambda *refs: far_kernel(count, variables * points, *refs),
        grid=(points // wide,),
        in_specs=[field] * (4 + len(others)) + [row, one],
        out_specs=[padded, padded, one],
        out_shape=[pltpu.VMEM((PAD, points), bf16)] * 2 + [jax.ShapeDtypeStruct((1, PAD), f32)],
        compiler_params=params(("arbitrary",), 16),
        name="crps_far",
    )(*map(parked, own), *others, *map(parked, partial), area, before)


def backward_kernel(who, d_0, d_1, w_out, s_0, s_1, h_0, h_1, at, contrib, heads, dpre):
    nodes = at.shape[0] - DEEP
    variables = w_out.shape[0]
    shape = (PAD, WIDE)
    row = lax.broadcasted_iota(jnp.int32, shape, 0)
    for y in range(contrib.shape[0]):
        first = pl.multiple_of((2 * y + who[0]) * WIDE, WIDE)
        rows = pl.ds(first, WIDE)
        total = jnp.zeros(shape, f32)
        turned = w_out[:, rows].T
        for m, (d, slope, hid) in enumerate(((d_0, s_0, h_0), (d_1, s_1, h_1))):
            for g in range(d.shape[1] // WIDE):
                cut = slice(g * WIDE, (g + 1) * WIDE)
                part = dot(turned, d[:variables, cut]) * slope[rows, cut].astype(f32)
                dpre[y, m, :, cut] = part.astype(bf16)
            total = total + dot(d[...], hid[rows, :], 1, 1)
            part = dot(at[: nodes + EDGE], dpre[y, m], 1, 1)
            contrib[y, m * nodes : (m + 1) * nodes, :] = part[:nodes].astype(bf16)
            total = total + jnp.where(row == variables, part[nodes : nodes + 1], 0.0)
        for i in range(PAD // 8):
            for j in range(WIDE // 128):
                heads[y, i, j] = total[i * 8 : (i + 1) * 8, j * 128 : (j + 1) * 128]


def backward(who, dpred, w_out, slope, hid, at):
    width, points = slope[0].shape
    nodes = at.shape[0] - DEEP
    count = width // WIDE // 2
    vm = pl.BlockSpec(memory_space=pltpu.VMEM)
    return pl.pallas_call(
        backward_kernel,
        in_specs=[pl.BlockSpec(memory_space=pltpu.SMEM)] + [vm] * 8,
        out_specs=[vm, vm],
        out_shape=[
            pltpu.VMEM((count, 2 * nodes, WIDE), bf16),
            pltpu.VMEM((count, PAD // 8, WIDE // 128, 8, 128), f32),
        ],
        scratch_shapes=[pltpu.VMEM((count, 2, WIDE, points), bf16)],
        compiler_params=pltpu.CompilerParams(vmem_limit_bytes=24 << 20),
        name="backward",
    )(who, *map(parked, dpred), parked(w_out), *map(parked, slope), *map(parked, hid), parked(at))


def outer_kernel(lat_own, lat_other, c_own, c_other, h_own, h_other, out):
    regions = out.shape[1]
    share = lat_own.shape[0] // regions
    for i in range(lat_own.shape[0] // WIDE):
        rows = slice(i * WIDE, (i + 1) * WIDE)
        for y in range(c_own.shape[0]):
            part = (dot(lat_own[rows], c_own[y]) + dot(lat_other[rows], c_other[y])).astype(bf16)
            for k in range(WIDE // share):
                r = i * (WIDE // share) + k
                for j in range(part.shape[1] // 128):
                    out[y, r, j * share : (j + 1) * share] = part[k * share : (k + 1) * share, j * 128 : (j + 1) * 128]
                out[y, r, 2 * share :] = (h_own[y, r] + h_other[y, r]).astype(bf16)


def outer(lat_own, lat_other, c_own, c_other, h_own, h_other, regions):
    inputs = lat_own.shape[0]
    halves = c_own.shape[0]
    share = inputs // regions
    vm = pl.BlockSpec(memory_space=pltpu.VMEM)
    return pl.pallas_call(
        outer_kernel,
        in_specs=[vm] * 6,
        out_specs=vm,
        out_shape=pltpu.VMEM((halves, regions, 2 * share + 8, 128), bf16),
        compiler_params=pltpu.CompilerParams(vmem_limit_bytes=12 << 20),
        name="outer",
    )(*map(parked, (lat_own, lat_other, c_own, c_other, h_own, h_other)))


def finish_kernel(where, table, rows_mine, rows_others, grad_node, grad_out, grad_bias, loss):
    variables, _ = grad_out.shape
    per_row = WIDE // 128
    lower = where[0] == 0
    share = grad_node.shape[0]
    total = jnp.zeros((1, 1), f32)
    for core in range(2):
        first = lower if core == 0 else jnp.logical_not(lower)
        for ylo in range(rows_mine.shape[0]):
            left = (2 * ylo + core) * WIDE
            both = jnp.where(first, rows_mine[ylo], rows_others[ylo])
            grad_node[:, left : left + WIDE] = both[:share]
            total = total + both[share : share + 1, :1]
        for at in range(table.shape[0]):
            ylo, place = at // 64, at % 32
            i, j = place // per_row, place % per_row
            left, top = (2 * ylo + core) * WIDE + j * 128, i * 8
            if top >= variables + 2 or at // 32 % 2 != core:
                continue
            piece = table[at].astype(f32)
            rows = min(8, variables - top)
            if rows > 0:
                grad_out[top : top + rows, left : left + 128] = piece[:rows]
            line = variables - top
            if 0 <= line < 7:
                grad_bias[:, left : left + 128] = piece[line : line + 1]
    loss[...] = total


def finish(where, table, rows_mine, rows_others, variables, width):
    vm = pl.BlockSpec(memory_space=pltpu.VMEM)
    return pl.pallas_call(
        finish_kernel,
        in_specs=[pl.BlockSpec(memory_space=pltpu.SMEM)] + [vm] * 3,
        out_shape=[
            jax.ShapeDtypeStruct((rows_mine.shape[1] - 8, width), f32),
            jax.ShapeDtypeStruct((variables, width), f32),
            jax.ShapeDtypeStruct((1, width), f32),
            jax.ShapeDtypeStruct((1, 1), f32),
        ],
        compiler_params=pltpu.CompilerParams(vmem_limit_bytes=8 << 20),
        name="finish",
    )(where, table, rows_mine, rows_others)


def local(latent, w_node, bias, w_out, edge_src, edge_weight, target, area):
    members, nodes, width = latent.shape
    variables = target.shape[0]
    regions = lax.axis_size(REGION)
    count = members * lax.axis_size(MEMBER)
    ahead = [(i, (i + 1) % regions) for i in range(regions)]
    behind = [(t, s) for s, t in ahead]
    swap = [(0, 1), (1, 0)]
    core = lax.axis_index("core")

    mine = [latent[0]] + [lax.optimization_barrier(latent)[m] for m in range(1, members)]

    low, high = [], []
    for m in range(members):
        low.append(lax.ppermute(mine[m], REGION, ahead))
        high.append(lax.ppermute(mine[m], REGION, behind))
    at, lift = prep(edge_src.T, edge_weight.T, bias[None, :], 3 * nodes, (w_node, target))

    hid, slope, err, near, far, beside = [], [], [], [], [], []
    for m in range(members):
        h, s, e = forward(low[m], mine[m], high[m], w_node, at, lift, w_out, target, f32 if m else bf16)
        hid.append(h)
        slope.append(slopes(s) if m else s)
        err.append(e)
        over = lax.ppermute((e * 0.125).astype(f16), "ylo", swap)
        near.append(lax.ppermute(e, "core", swap))
        far.append(over.astype(f32) * 8.0)
        beside.append(lax.ppermute(over, "core", swap).astype(f32) * 8.0)

    first, err[1] = lax.optimization_barrier((mine[0], err[1]))
    lat_t = turn((low[0], first, high[0], low[1], mine[1], high[1]))
    lat_t_other = lax.ppermute(lat_t, "core", swap)

    area_row = area[None, :]
    p_0, p_1, loss = crps_near(err, near + [far[0], beside[0]], area_row, count)
    d_0, d_1, loss = crps_far(err, [far[1], beside[1]], (p_0, p_1), area_row, loss, count)


    def back(side):
        return backward(side[None].astype(jnp.int32), (d_0, d_1), w_out, slope, hid, at)

    given, heads_given = back(1 - core)
    taken = lax.ppermute(given, "core", swap)
    heads_taken = lax.ppermute(heads_given, "core", swap)
    kept, heads_kept = back(core)
    tiles = (2, regions, 8, 128)
    part = outer(lat_t, lat_t_other, kept, taken, heads_kept.reshape(tiles), heads_taken.reshape(tiles), regions)
    chips, every = lax.axis_size(CHIPS), lax.axis_size(EVERY)
    share = width // regions
    shares = lax.all_to_all(
        part.reshape(chips, 2 * share + 8, 128), CHIPS, split_axis=0, concat_axis=0, tiled=True
    )
    summed = shares.astype(f32).sum(axis=0)
    own = jnp.concatenate([summed[:share], summed[share : 2 * share]], axis=1)
    own = jnp.concatenate([own, jnp.full((8, own.shape[1]), jnp.sum(loss), f32)])
    table = lax.all_to_all(
        jnp.broadcast_to(summed[2 * share :].astype(bf16), (every, 8, 128)), EVERY, split_axis=0, concat_axis=0, tiled=True
    )
    across = lax.ppermute(own, "ylo", swap)
    upper = lax.axis_index("ylo") == 1
    rows = jnp.stack([jnp.where(upper, across, own), jnp.where(upper, own, across)])
    rows_others = lax.ppermute(rows, "core", swap)
    who = core[None].astype(jnp.int32)
    grad_node, grad_out, grad_bias, loss_here = finish(who, table, rows, rows_others, variables, width)
    grad_bias = grad_bias.reshape(width)
    loss_here = loss_here.reshape(1)
    return grad_node, grad_out, grad_bias, loss_here


def solution(mesh):
    finer = Mesh(mesh.devices.reshape(2, 2, 4, 2, 4), EVERY)
    in_specs = (
        P(MEMBER, REGION, None),
        P(),
        P(),
        P(),
        P(REGION, None),
        P(REGION, None),
        P(None, REGION),
        P(REGION),
    )
    out_specs = (P(REGION, None), P(), P(), P(REGION))

    return jax.shard_map(local, mesh=finer, in_specs=in_specs, out_specs=out_specs, check_vma=False)
```
